512 devices in a mesh: grp: 4 (over x), node: 128 (over z, y, core).
Axes of the slice: x: 4, y: 8, z: 8, core: 2. Of those that a mesh axis runs over, the one named last changes fastest.
Arguments:
- start_block: float32 [64, 65536], P(None, ('grp', 'node')), may hold values from -24 to 24
- weight_tiles: bfloat16 [512, 12, 128, 128], P(('grp', 'node')), may hold values from -0.15625 to 0.15625
- tile_scales: float32 [512, 12], P(('grp', 'node')), may hold values from 0.5 to 2
- neighbour_ids: int32 [512, 12], P(('grp', 'node')), may hold values from 0 to 511, as said below
- live_counts: int32 [512], P(('grp', 'node')), may hold values from 1 to 12
- row_order: int32 [512, 128], P(('grp', 'node')), may hold values from 0 to 127, each once within a row
Outputs:
- embedding: float32 [64, 65536], P(None, ('grp', 'node'))
- ritz: float32 [64, 64], replicated
- start_theta: float32 [64, 64], replicated
The draws below stay inside these ranges and needn't reach their ends.
Inputs may be any that keep to these rules, and one draw needn't show every extreme that they name: `neighbour_ids`: row tile t belongs to device t in group-major order. Every id names a row tile of a device of any group whose node index differs from that of row tile t by at most 2, around the cycle of 128. Ids may repeat within a row tile; unused slots also hold such ids.
All inputs are finite; a program needn't handle non-finite values.
Results may differ from the reference program's by a relative error of at most 0.002.
The reference program's roundings to bfloat16 on the way count: a program that leaves them out, or rounds other values in their place, can miss the bound.
Values may be sent and summed in bfloat16 or wider, within the bound.
No kernel may reach another device: no remote copies, remote signals or barrier semaphores. Data moves between devices by JAX's collectives and lax.ppermute only.
A program may use at most 64 MiB of HBM per device.

```python
import math
import jax
import jax.numpy as jnp
from jax import lax

COLS = 64
TILE = 128
SLOTS = 12
REACH = 2
NSUB = 4
STEPS = 2
TILES_DEV = 1
ROWS_DEV = 128
SEG = 1
TILES_ALL = 512
ROWS = 65536
N_GRP = 4
N_NODE = 128


def draw_start_block(key, part):
    key_one = jax.random.fold_in(jax.random.fold_in(key, 11), 0)
    position = jnp.arange(ROWS, dtype=jnp.float32)[None, :] / ROWS
    rising = 1.0 + 2.0 * position
    baseline = jnp.clip(jax.random.normal(key_one, (COLS, ROWS), jnp.float32), -6.0, 6.0)
    return baseline * rising


def draw_neighbour_ids(key, part):
    key_one, key_two, key_three = jax.random.split(jax.random.fold_in(key, 23), 3)
    tiles = jnp.arange(TILES_ALL, dtype=jnp.int32)[:, None]
    device = tiles // TILES_DEV
    node_here = device % N_NODE
    group_pick = jax.random.randint(key_one, (TILES_ALL, SLOTS), 0, N_GRP, dtype=jnp.int32)
    offset_pick = jax.random.randint(key_two, (TILES_ALL, SLOTS), -REACH, REACH + 1, dtype=jnp.int32)
    tile_pick = jax.random.randint(key_three, (TILES_ALL, SLOTS), 0, TILES_DEV, dtype=jnp.int32)
    node_there = (node_here + offset_pick + N_NODE) % N_NODE
    return ((group_pick * N_NODE + node_there) * TILES_DEV + tile_pick).astype(jnp.int32)


def draw_live_counts(key, part):
    key_one, key_two = jax.random.split(jax.random.fold_in(key, 37))
    levels = jax.random.randint(key_one, (N_GRP * N_NODE,), 2, SLOTS + 1, dtype=jnp.int32)
    counts = jnp.repeat(levels, TILES_DEV) + jax.random.randint(key_two, (TILES_ALL,), -1, 2, dtype=jnp.int32)
    counts = jnp.clip(counts, 1, SLOTS)
    counts = counts.at[0].set(SLOTS).at[1].set(1)
    return counts.astype(jnp.int32)


def shard_levels(own_key, dims, pieces, least, high):
    factor_of = 1.0
    for dim, parts in pieces:
        heights = jax.random.uniform(jax.random.fold_in(jax.random.fold_in(own_key, 6), dim), (parts,), jnp.float32, least / len(pieces), high / len(pieces))
        factor_of = factor_of * jnp.repeat(jnp.exp(heights), dims[dim] // parts).reshape((-1,) + (1,) * (len(dims) - 1 - dim))
    return factor_of


def normal_values(stream_key, shape, scale, reach, pieces=(), held_as=jnp.bfloat16):
    entries = scale * jax.random.normal(stream_key, shape, jnp.float32)
    if pieces:
        entries = entries * shard_levels(stream_key, shape, pieces, -0.22, 0.18)
    return jnp.clip(entries, -reach, reach).astype(held_as)


def setup_inputs(seed: int = 0) -> dict:
    streams_of = jax.random.split(jax.random.key(seed), 7)
    start_block = draw_start_block(jax.random.fold_in(streams_of[6], 71), 0)
    weight_tiles = normal_values(streams_of[1], (TILES_ALL, SLOTS, TILE, TILE), (TILE * SLOTS) ** -0.5, 0.15625, ((0, 512),))
    tile_scales = jnp.clip(jnp.exp(math.log(2.0) - 1.3862944 * jax.random.uniform(streams_of[2], (TILES_ALL, SLOTS), jnp.float32) ** shard_levels(streams_of[2], (TILES_ALL, SLOTS), ((0, 512),), -0.2, 0.2)), 0.5, 2.0)
    neighbour_ids = draw_neighbour_ids(jax.random.fold_in(streams_of[6], 71), 0)
    live_counts = draw_live_counts(jax.random.fold_in(streams_of[6], 71), 0)
    row_order = jax.vmap(lambda own: jax.random.permutation(own, ROWS_DEV))(jax.random.split(streams_of[5], (N_GRP * N_NODE))).reshape((N_GRP * N_NODE, ROWS_DEV)).astype(jnp.int32)
    return {"start_block": start_block, "weight_tiles": weight_tiles, "tile_scales": tile_scales, "neighbour_ids": neighbour_ids, "live_counts": live_counts, "row_order": row_order}


def symmetric(matrix):
    return 0.5 * (matrix + matrix.T)

def exact_dot(left, right):
    return jnp.dot(left.astype(jnp.float32), right.astype(jnp.float32), precision=lax.Precision.HIGHEST, preferred_element_type=jnp.float32)

def lower_solve(factor, rhs, transposed):
    return lax.linalg.triangular_solve(factor, rhs, left_side=True, lower=True, transpose_a=transposed)

def rayleigh(gram_basis, gram_operator, columns):
    order = gram_basis.shape[0]
    chol_basis = jnp.linalg.cholesky(gram_basis)
    half = lower_solve(chol_basis, symmetric(gram_operator), False)
    projected = symmetric(lower_solve(chol_basis, half.T, False))
    scale = jnp.sqrt(jnp.sum(projected * projected) + 1e-06)
    filtered = projected / scale + 1.25 * jnp.eye(order, dtype=jnp.float32)
    square = exact_dot(filtered, filtered)
    fourth = exact_dot(square, square)
    basis = jnp.eye(order, dtype=jnp.float32)[:, :columns]
    for sweep in range(NSUB):
        image = exact_dot(fourth, basis)
        chol_image = jnp.linalg.cholesky(exact_dot(image.T, image))
        basis = lower_solve(chol_image, image.T, False).T
    coeffs = lower_solve(chol_basis, basis, True)
    ritz_now = symmetric(exact_dot(basis.T, exact_dot(projected, basis)))
    return (coeffs, ritz_now)

def apply_tiles(values, weight_tiles, tile_scales, neighbour_ids, live_counts):
    columns = values.shape[0]
    devices = N_GRP * N_NODE
    rounded = values.astype(jnp.bfloat16).reshape(columns, TILES_ALL, TILE)
    slot_iota = jnp.arange(SLOTS, dtype=jnp.int32)[None, :]
    weights = jnp.where(slot_iota < live_counts[:, None], tile_scales, jnp.float32(0.0))

    def one_device(items):
        ids, tiles, slot_weights = items
        picked = rounded[:, ids, :].astype(jnp.float32)
        product = jnp.einsum('ctsj,tsij->ctsi', picked, tiles.astype(jnp.float32))
        return lax.optimization_barrier(jnp.sum(product * slot_weights[None, :, :, None], axis=2))
    result = lax.map(one_device, (neighbour_ids.reshape(devices, TILES_DEV, SLOTS), weight_tiles.reshape(devices, TILES_DEV, SLOTS, TILE, TILE), weights.reshape(devices, TILES_DEV, SLOTS)))
    return result.transpose(1, 0, 2, 3).reshape(columns, ROWS)

def reference(start_block, weight_tiles, tile_scales, neighbour_ids, live_counts, row_order):

    def operate(values):
        return apply_tiles(values, weight_tiles, tile_scales, neighbour_ids, live_counts)
    start_gram = exact_dot(start_block, start_block.T)
    start_chol = jnp.linalg.cholesky(start_gram)
    block = lower_solve(start_chol, start_block, False)
    applied = operate(block)
    theta = symmetric(exact_dot(block, applied.T))
    start_theta = jnp.sqrt(jnp.float32(ROWS)) * theta
    momentum = None
    applied_momentum = None
    ritz = theta
    for step in range(STEPS):
        residual = applied - exact_dot(theta, block)
        applied_residual = operate(residual)
        if momentum is None:
            trial = jnp.concatenate([block, residual], axis=0)
            applied_trial = jnp.concatenate([applied, applied_residual], axis=0)
        else:
            trial = jnp.concatenate([block, residual, momentum], axis=0)
            applied_trial = jnp.concatenate([applied, applied_residual, applied_momentum], axis=0)
        gram_basis = exact_dot(trial, trial.T)
        gram_operator = exact_dot(trial, applied_trial.T)
        coeffs, ritz = rayleigh(gram_basis, gram_operator, COLS)
        lower_coeffs = coeffs[COLS:]
        block = exact_dot(coeffs.T, trial)
        applied = exact_dot(coeffs.T, applied_trial)
        momentum = exact_dot(lower_coeffs.T, trial[COLS:])
        applied_momentum = exact_dot(lower_coeffs.T, applied_trial[COLS:])
        theta = ritz
    scaled = jnp.sqrt(jnp.float32(ROWS)) * block
    per_device = scaled.reshape(COLS, N_GRP * N_NODE, ROWS_DEV)
    permuted = jnp.take_along_axis(per_device, row_order[None, :, :], axis=2)
    arranged = permuted.reshape(COLS, N_GRP, N_NODE, N_NODE, SEG).transpose(0, 1, 3, 2, 4)
    embedding = arranged.reshape(COLS, ROWS)
    return (embedding, ritz, start_theta)
```

```python
import jax
import jax.numpy as jnp
from jax import lax
from jax.experimental import pallas as pl
from jax.experimental.pallas import tpu as pltpu
from jax.sharding import PartitionSpec as P

REACH = 2
NSUB = 4
STEPS = 2
BOTH = ("grp", "node")
CORE_Y = (1, 2, 4, 8)
Z_X = (16, 32, 64, 128, 256)
CORE_X = (1, 128, 256)


def groups_over(bits):
    mask = sum(bits)
    groups = []
    for base in range(512):
        if base & mask:
            continue
        members = [base]
        for bit in bits:
            members = members + [member | bit for member in members]
        groups.append(members)
    return groups


def swap(values, bits):
    return lax.all_to_all(
        values, BOTH, split_axis=0, concat_axis=0, tiled=True, axis_index_groups=groups_over(bits)
    )


def copies(value, count):
    return jnp.broadcast_to(value[None], (count,) + value.shape)


def total(part):
    rows = part.shape[0]
    scattered = jnp.sum(swap(part.reshape(16, rows // 16, 128), CORE_Y), axis=0)
    summed = jnp.sum(swap(copies(scattered, 32), Z_X), axis=0)
    return swap(copies(summed, 16), CORE_Y).reshape(rows, 128)


def total_square(matrix):
    half = matrix.shape[0] // 2
    packed = total(jnp.concatenate([matrix[:half], matrix[half:]], axis=1))
    width = matrix.shape[1]
    return jnp.concatenate([packed[:, :width], packed[:, width:]], axis=0)


def symmetric(matrix):
    return 0.5 * (matrix + matrix.T)


def exact_dot(left, right):
    return jnp.dot(left, right, precision=lax.Precision.HIGHEST, preferred_element_type=jnp.float32)


def lower_solve(factor, rhs, transposed):
    return lax.linalg.triangular_solve(
        factor, rhs, left_side=True, lower=True, transpose_a=transposed
    )


def rayleigh(gram_basis, gram_operator, columns):
    order = gram_basis.shape[0]
    chol_basis = jnp.linalg.cholesky(gram_basis)
    half = lower_solve(chol_basis, symmetric(gram_operator), False)
    projected = symmetric(lower_solve(chol_basis, half.T, False))
    scale = jnp.sqrt(jnp.sum(projected * projected) + 1e-06)
    filtered = projected / scale + 1.25 * jnp.eye(order, dtype=jnp.float32)
    square = exact_dot(filtered, filtered)
    fourth = exact_dot(square, square)
    basis = jnp.eye(order, dtype=jnp.float32)[:, :columns]
    for sweep in range(NSUB):
        image = exact_dot(fourth, basis)
        chol_image = jnp.linalg.cholesky(exact_dot(image.T, image))
        basis = lower_solve(chol_image, image.T, False).T
    coeffs = lower_solve(chol_basis, basis, True)
    ritz_now = symmetric(exact_dot(basis.T, exact_dot(projected, basis)))
    return (coeffs, ritz_now)


def tiles_kernel(index_ref, weight_ref, own_ref, up_ref, down_ref, tiles_ref, out_ref, window_ref):
    window_ref[0:8] = down_ref[...]
    window_ref[8:16] = own_ref[...]
    window_ref[16:24] = up_ref[...]
    acc = jnp.zeros(out_ref.shape, jnp.float32)
    for slot in range(tiles_ref.shape[0]):
        product = lax.dot_general(
            window_ref[index_ref[slot]],
            tiles_ref[slot],
            (((1,), (1,)), ((), ())),
            preferred_element_type=jnp.float32,
        )
        acc = acc + weight_ref[slot] * product
    out_ref[...] = acc


def apply_tiles(index, weights, own, up, down, tiles):
    smem = pl.BlockSpec(memory_space=pltpu.SMEM)
    vmem = pl.BlockSpec(memory_space=pltpu.VMEM)
    return pl.pallas_call(
        tiles_kernel,
        out_shape=jax.ShapeDtypeStruct(own.shape[1:], jnp.float32),
        in_specs=[smem, smem, vmem, vmem, vmem, vmem],
        out_specs=vmem,
        scratch_shapes=[pltpu.VMEM((24,) + own.shape[1:], jnp.bfloat16)],
        compiler_params=pltpu.CompilerParams(vmem_limit_bytes=16 << 20),
        name="apply_tiles",
    )(index, weights, own, up, down, tiles)


def local(start_block, weight_tiles, tile_scales, neighbour_ids, live_counts, row_order):
    columns = start_block.shape[0]
    rows_dev = start_block.shape[1]
    groups = lax.axis_size("grp")
    nodes = lax.axis_size("node")
    here = lax.axis_index("node")
    ids = neighbour_ids[0]
    slots = ids.shape[0]
    group_index = ids // nodes
    node_index = ids % nodes
    chips = nodes // 2
    chip_offset = (node_index // 2 - here // 2 + 1 + chips) % chips
    index = jnp.clip(chip_offset * 8 + node_index % 2 + 2 * group_index, 0, 23).astype(jnp.int32)
    slot_iota = jnp.arange(slots, dtype=jnp.int32)
    weights = jnp.where(slot_iota < live_counts[0], tile_scales[0], jnp.float32(0.0))
    tiles = weight_tiles[0]
    to_next = [(source, (source + 2) % nodes) for source in range(nodes)]
    to_last = [(source, (source - 2) % nodes) for source in range(nodes)]

    def operate(values):
        rounded = values.astype(jnp.bfloat16)
        own = swap(copies(rounded, 8), CORE_X)
        down = lax.ppermute(own, "node", to_next)
        up = lax.ppermute(own, "node", to_last)
        return apply_tiles(index, weights, own, up, down, tiles)

    total_rows = rows_dev * groups * nodes
    start_gram = total_square(exact_dot(start_block, start_block.T))
    start_chol = jnp.linalg.cholesky(start_gram)
    block = lower_solve(start_chol, start_block, False)
    applied = operate(block)
    theta = symmetric(total_square(exact_dot(block, applied.T)))
    start_theta = jnp.sqrt(jnp.float32(total_rows)) * theta
    momentum = None
    applied_momentum = None
    ritz = theta
    for step in range(STEPS):
        residual = applied - exact_dot(theta, block)
        applied_residual = operate(residual)
        if momentum is None:
            trial = jnp.concatenate([block, residual], axis=0)
            applied_trial = jnp.concatenate([applied, applied_residual], axis=0)
        else:
            trial = jnp.concatenate([block, residual, momentum], axis=0)
            applied_trial = jnp.concatenate([applied, applied_residual, applied_momentum], axis=0)
        order = trial.shape[0]
        grams = jnp.concatenate([exact_dot(trial, trial.T), exact_dot(trial, applied_trial.T)], axis=0)
        grams = total(grams.reshape(-1, 128)).reshape(2 * order, order)
        coeffs, ritz = rayleigh(grams[:order], grams[order:], columns)
        lower_coeffs = coeffs[columns:]
        block = exact_dot(coeffs.T, trial)
        applied = exact_dot(coeffs.T, applied_trial)
        momentum = exact_dot(lower_coeffs.T, trial[columns:])
        applied_momentum = exact_dot(lower_coeffs.T, applied_trial[columns:])
        theta = ritz
    scaled = jnp.sqrt(jnp.float32(total_rows)) * block
    pick = (row_order[0][None, :] == jnp.arange(rows_dev, dtype=jnp.int32)[:, None]).astype(jnp.float32)
    permuted = exact_dot(scaled, pick)
    pieces = permuted.reshape(columns, nodes, rows_dev // nodes)
    arrived = lax.all_to_all(pieces, "node", split_axis=1, concat_axis=1, tiled=True)
    embedding = arrived.reshape(columns, rows_dev)
    return (embedding, ritz, start_theta)


def solution(mesh):
    return jax.shard_map(
        local,
        mesh=mesh,
        in_specs=(
            P(None, BOTH),
            P(BOTH, None, None, None),
            P(BOTH, None),
            P(BOTH, None),
            P(BOTH),
            P(BOTH, None),
        ),
        out_specs=(P(None, BOTH), P(), P()),
        check_vma=False,
    )
```

```python
import jax
import jax.numpy as jnp
from jax import lax
from jax.experimental import pallas as pl
from jax.experimental.pallas import tpu as pltpu
from jax.sharding import PartitionSpec as P

REACH = 2
NSUB = 4
BLOCK = 4
RADIUS = 0.18
BOTH = ("grp", "node")
CORE_Y = (1, 2, 4, 8)
Z_X = (16, 32, 64, 128, 256)
CORE_X = (1, 128, 256)


def groups_over(bits):
    mask = sum(bits)
    groups = []
    for base in range(512):
        if base & mask:
            continue
        members = [base]
        for bit in bits:
            members = members + [member | bit for member in members]
        groups.append(members)
    return groups


def swap(values, bits):
    return lax.all_to_all(
        values, BOTH, split_axis=0, concat_axis=0, tiled=True, axis_index_groups=groups_over(bits)
    )


def run(kernel, name, results, *operands, scalars=0, scratch=()):
    smem = pl.BlockSpec(memory_space=pltpu.SMEM)
    vmem = pl.BlockSpec(memory_space=pltpu.VMEM)
    return pl.pallas_call(
        kernel,
        out_shape=[jax.ShapeDtypeStruct(shape, dtype) for shape, dtype in results],
        in_specs=[smem] * scalars + [vmem] * (len(operands) - scalars),
        out_specs=[vmem] * len(results),
        scratch_shapes=list(scratch),
        compiler_params=pltpu.CompilerParams(vmem_limit_bytes=32 << 20),
        name=name,
    )(*operands)


F32 = jnp.float32
BF16 = jnp.bfloat16


def sum_kernel(parts_ref, out_ref):
    parts = [parts_ref[i] for i in range(parts_ref.shape[0])]
    while len(parts) > 1:
        parts = [parts[i] + parts[i + 1] for i in range(0, len(parts), 2)]
    for i in range(out_ref.shape[0]):
        out_ref[i] = parts[0]


def sum_copies(parts, count):
    return run(sum_kernel, "sum_copies", [((count,) + parts.shape[1:], F32)], parts)[0]


def total(part):
    rows = part.shape[0]
    scattered = swap(part.reshape(16, rows // 16, 128), CORE_Y)
    shared = swap(sum_copies(scattered, 32), Z_X)
    return swap(sum_copies(shared, 16), CORE_Y).reshape(rows, 128)


def mm(left, right, contract):
    return lax.dot_general(
        left,
        right,
        ((contract[:1], contract[1:]), ((), ())),
        precision=lax.Precision.HIGHEST,
        preferred_element_type=jnp.float32,
    )


def nn(left, right):
    return mm(left, right, (1, 0))


def nt(left, right):
    return mm(left, right, (1, 1))


def tn(left, right):
    return mm(left, right, (0, 0))


def eye(order):
    row = lax.broadcasted_iota(jnp.int32, (order, order), 0)
    column = lax.broadcasted_iota(jnp.int32, (order, order), 1)
    return jnp.where(row == column, jnp.float32(1.0), jnp.float32(0.0))


def inverse_root(value):
    guess = lax.rsqrt(value)
    return guess * (1.5 - 0.5 * value * guess * guess)


def inverse_factor(matrix):
    order = matrix.shape[0]
    lanes = 2 * order
    both = jnp.concatenate([matrix, eye(order)], axis=1)
    bands = [both[8 * i : 8 * i + 8] for i in range(order // 8)]
    sublane = lax.broadcasted_iota(jnp.int32, (8, lanes), 0)
    done = [None] * len(bands)
    for first in range(0, order, BLOCK):
        band = first // 8
        base = first % 8
        last_of_band = base + BLOCK == 8
        live = range(band, len(bands))
        column = [
            [jnp.broadcast_to(bands[i][:, first + k : first + k + 1], (8, lanes)) for i in live]
            for k in range(BLOCK)
        ]
        row = [
            jnp.broadcast_to(bands[band][base + k : base + k + 1], (8, lanes)) for k in range(BLOCK)
        ]
        entry = [
            [
                jnp.broadcast_to(column[l][0][base + k : base + k + 1], (8, lanes))
                for l in range(k + 1)
            ]
            for k in range(BLOCK)
        ]
        inverse = []
        factor = [[None] * BLOCK for _ in range(BLOCK)]
        for l in range(BLOCK):
            inverse.append(1.0 / entry[l][l])
            for k in range(l + 1, BLOCK):
                factor[k][l] = entry[k][l] * inverse[l]
                for m in range(l + 1, k + 1):
                    entry[k][m] = entry[k][m] - factor[k][l] * entry[m][l]
        start = 1 if last_of_band else 0
        for k in range(BLOCK):
            for l in range(k):
                row[k] = row[k] - factor[k][l] * row[l]
                for i in range(start, len(live)):
                    column[k][i] = column[k][i] - factor[k][l] * column[l][i]
        for k in range(BLOCK):
            scaled = row[k] * inverse_root(entry[k][k])
            if done[band] is None:
                done[band] = scaled
            else:
                done[band] = jnp.where(sublane == base + k, scaled, done[band])
            left = row[k] * inverse[k]
            for i in range(start, len(live)):
                bands[band + i] = bands[band + i] - column[k][i] * left
    return jnp.concatenate(done, axis=0)[:, order:]


def half_sum(matrix):
    return 0.5 * (matrix + matrix.T)


def orthonormal(image):
    return nt(image, inverse_factor(tn(image, image)))


def project(linv, gram, basis_ref):
    order = linv.shape[0]
    columns = basis_ref.shape[1]
    projected = half_sum(nt(nn(linv, gram), linv))
    scale = jnp.sqrt(jnp.sum(projected * projected, keepdims=True) + 1e-06)
    unit = projected / scale
    identity = eye(order)
    filtered = unit + 1.25 * identity
    square = nn(filtered, filtered)
    fourth = nn(square, square)
    eighth = nn(fourth, fourth)
    unit2 = square - 2.5 * unit - 1.5625 * identity
    unit4 = nn(unit2, unit2)
    bound = jnp.sum(unit4 * unit4)
    basis_ref[...] = orthonormal(nn(eighth, eighth[:, :columns]))

    @pl.when(jnp.logical_not(bound < RADIUS**8))
    def _():
        basis_ref[...] = identity[:, :columns]

        def sweep(_, carry):
            basis_ref[...] = orthonormal(nn(fourth, basis_ref[...]))
            return carry

        lax.fori_loop(0, NSUB, sweep, 0)

    basis = basis_ref[...]
    coeffs = tn(linv, basis)
    theta = half_sum(tn(basis, nn(projected, basis)))
    return coeffs, theta


def store_packed(ref, matrix):
    half = matrix.shape[0] // 2
    ref[...] = jnp.concatenate([matrix[:half], matrix[half:]], axis=1)


def load_packed(ref):
    width = ref.shape[1] // 2
    return jnp.concatenate([ref[:, :width], ref[:, width:]], axis=0)


def store_copies(ref, value):
    rounded = value.astype(BF16)
    for i in range(ref.shape[0]):
        ref[i] = rounded


def gram_kernel(start_ref, gram_ref):
    start = start_ref[...]
    store_packed(gram_ref, nt(start, start))


def start_kernel(gram_ref, start_ref, block_ref, rounded_ref):
    block = nn(inverse_factor(load_packed(gram_ref)), start_ref[...])
    block_ref[...] = block
    store_copies(rounded_ref, block)


def multiply_tiles(index_ref, weight_ref, own_ref, up_ref, down_ref, tiles_ref, window_ref):
    window_ref[0:8] = down_ref[...]
    window_ref[8:16] = own_ref[...]
    window_ref[16:24] = up_ref[...]
    acc = jnp.zeros(own_ref.shape[1:], F32)
    for slot in range(tiles_ref.shape[0]):
        product = lax.dot_general(
            window_ref[index_ref[slot]],
            tiles_ref[slot],
            (((1,), (1,)), ((), ())),
            preferred_element_type=F32,
        )
        acc = acc + weight_ref[slot] * product
    return acc


def first_kernel(index_ref, weight_ref, own_ref, up_ref, down_ref, tiles_ref, block_ref, applied_ref, theta_ref, window_ref):
    block = block_ref[...]
    applied = multiply_tiles(index_ref, weight_ref, own_ref, up_ref, down_ref, tiles_ref, window_ref)
    applied_ref[...] = applied
    store_packed(theta_ref, 0.5 * (nt(block, applied) + nt(applied, block)))


def residual_kernel(root, theta_in_ref, block_ref, applied_ref, theta_ref, start_theta_ref, residual_ref, rounded_ref):
    theta = half_sum(load_packed(theta_in_ref))
    theta_ref[...] = theta
    start_theta_ref[...] = root * theta
    residual = applied_ref[...] - nn(theta, block_ref[...])
    residual_ref[...] = residual
    store_copies(rounded_ref, residual)


def trial_kernel(index_ref, weight_ref, own_ref, up_ref, down_ref, tiles_ref, trial_ref, applied_ref, image_ref, grams_ref, window_ref):
    columns = image_ref.shape[0]
    image = multiply_tiles(index_ref, weight_ref, own_ref, up_ref, down_ref, tiles_ref, window_ref)
    image_ref[...] = image
    trial = trial_ref[...]
    residual = trial[columns : 2 * columns]
    applied = applied_ref[...]
    bands = [applied[i : i + columns] for i in range(0, applied.shape[0], columns)]
    applied_trial = jnp.concatenate(bands[:1] + [image] + bands[1:], axis=0)
    cross = 0.5 * (nt(trial, image) + nt(applied_trial, residual))
    grams_ref[...] = jnp.concatenate([nt(trial, residual), cross], axis=1)


def assemble_first(grams, theta):
    columns = theta.shape[0]
    cross = grams[:columns, columns:]
    overlap = grams[:columns, :columns]
    own = half_sum(grams[columns:, columns:])
    basis = (overlap, grams[columns:, :columns])
    gram = jnp.concatenate(
        [jnp.concatenate([theta, cross], axis=1), jnp.concatenate([cross.T, own], axis=1)], axis=0
    )
    return basis, gram


def first_step_kernel(grams_ref, theta_ref, trial_ref, applied_ref, image_ref, coeffs_ref, theta_out_ref, trial_out_ref, applied_out_ref, rounded_ref, basis_ref):
    columns = theta_ref.shape[0]
    (overlap, own), gram = assemble_first(grams_ref[...], theta_ref[...])
    factor = inverse_factor(own - tn(overlap, overlap))
    linv = jnp.concatenate(
        [
            jnp.concatenate([eye(columns), jnp.zeros((columns, columns), F32)], axis=1),
            jnp.concatenate([-nt(factor, overlap), factor], axis=1),
        ],
        axis=0,
    )
    coeffs, theta = project(linv, gram, basis_ref)
    theta_out_ref[...] = theta
    lower = jnp.concatenate([jnp.zeros((columns, columns), F32), coeffs[columns:]], axis=0)
    both = jnp.concatenate([coeffs, lower], axis=1)
    coeffs_ref[...] = both
    applied_trial = jnp.concatenate([applied_ref[...], image_ref[...]], axis=0)
    fresh = tn(both, jnp.concatenate([trial_ref[...], applied_trial], axis=1))
    width = trial_ref.shape[1]
    block = fresh[:columns, :width]
    applied = fresh[:columns, width:]
    residual = applied - nn(theta, block)
    store_copies(rounded_ref, residual)
    trial_out_ref[...] = jnp.concatenate([block, residual, fresh[columns:, :width]], axis=0)
    applied_out_ref[...] = jnp.concatenate([applied, fresh[columns:, width:]], axis=0)


def carry_kernel(coeffs_ref, grams_ref, theta_ref, trial_ref, order_ref, carried_ref, pieces_ref):
    columns = theta_ref.shape[0]
    coeffs = coeffs_ref[...]
    (overlap, own), gram = assemble_first(grams_ref[...], theta_ref[...])
    basis = jnp.concatenate(
        [
            jnp.concatenate([eye(columns), overlap], axis=1),
            jnp.concatenate([overlap.T, own], axis=1),
        ],
        axis=0,
    )
    carried_ref[...] = jnp.concatenate(
        [tn(coeffs, nn(basis, coeffs)), tn(coeffs, nn(gram, coeffs))], axis=0
    )
    width = trial_ref.shape[1]
    place = lax.broadcasted_iota(jnp.int32, (width, width), 0)
    pick = jnp.where(place == order_ref[...], F32(1.0), F32(0.0))
    pieces_ref[...] = mm(pick, trial_ref[...], (0, 1))


def last_step_kernel(root, grams_ref, carried_ref, theta_ref, arrived_ref, theta_out_ref, embedding_ref, basis_ref):
    columns = theta_ref.shape[0]
    grams = grams_ref[...]
    carried = carried_ref[...]
    wide = 2 * columns
    overlap = jnp.concatenate([grams[:columns, :columns], carried[:columns, columns:wide]], axis=1)
    mixed = grams[wide:, :columns]
    spread = tn(overlap, overlap)
    first = grams[columns:wide, :columns] - spread[:columns, :columns]
    corner = mixed.T - spread[:columns, columns:]
    second = carried[columns:wide, columns:wide] - spread[columns:, columns:]
    factor = inverse_factor(first)
    middle = nn(factor, corner)
    other = inverse_factor(second - tn(middle, middle))
    zero = jnp.zeros((columns, columns), F32)
    lower = jnp.concatenate(
        [
            jnp.concatenate([factor, zero], axis=1),
            jnp.concatenate([-nn(other, tn(middle, factor)), other], axis=1),
        ],
        axis=0,
    )
    linv = jnp.concatenate(
        [
            jnp.concatenate([eye(columns), zero, zero], axis=1),
            jnp.concatenate([-nt(lower, overlap), lower], axis=1),
        ],
        axis=0,
    )
    cross = grams[:columns, columns:]
    own = half_sum(grams[columns:wide, columns:])
    momentum_cross = grams[wide:, columns:]
    block_momentum = carried[wide : wide + columns, columns:wide]
    momentum = half_sum(carried[wide + columns :, columns:wide])
    gram = jnp.concatenate(
        [
            jnp.concatenate([theta_ref[...], cross, block_momentum], axis=1),
            jnp.concatenate([cross.T, own, momentum_cross.T], axis=1),
            jnp.concatenate([block_momentum.T, momentum_cross, momentum], axis=1),
        ],
        axis=0,
    )
    coeffs, theta = project(linv, gram, basis_ref)
    theta_out_ref[...] = theta
    embedding_ref[...] = root * mm(coeffs, arrived_ref[...], (0, 1))


def local(start_block, weight_tiles, tile_scales, neighbour_ids, live_counts, row_order):
    columns = start_block.shape[0]
    rows_dev = start_block.shape[1]
    groups = lax.axis_size("grp")
    nodes = lax.axis_size("node")
    here = lax.axis_index("node")
    ids = neighbour_ids[0]
    slots = ids.shape[0]
    group_index = ids // nodes
    node_index = ids % nodes
    chips = nodes // 2
    chip_offset = (node_index // 2 - here // 2 + 1 + chips) % chips
    index = jnp.clip(chip_offset * 8 + node_index % 2 + 2 * group_index, 0, 23).astype(jnp.int32)
    slot_iota = jnp.arange(slots, dtype=jnp.int32)
    weights = jnp.where(slot_iota < live_counts[0], tile_scales[0], F32(0.0))
    tiles = weight_tiles[0]
    to_next = [(source, (source + 2) % nodes) for source in range(nodes)]
    to_last = [(source, (source - 2) % nodes) for source in range(nodes)]
    root = float(rows_dev * groups * nodes) ** 0.5
    slab = (columns, rows_dev)
    square = (columns, columns)
    packed = (columns // 2, 2 * columns)
    rounded_copies = ((2 * groups,) + slab, BF16)
    window = [pltpu.VMEM((6 * groups,) + slab, BF16)]

    def halo(rounded):
        own = swap(rounded, CORE_X)
        down = lax.ppermute(own, "node", to_next)
        up = lax.ppermute(own, "node", to_last)
        return index, weights, own, up, down, tiles

    gram = total(run(gram_kernel, "start_gram", [(packed, F32)], start_block)[0])
    block, rounded = run(
        start_kernel, "start_basis", [(slab, F32), rounded_copies], gram, start_block
    )
    applied, theta_part = run(
        first_kernel,
        "apply_start",
        [(slab, F32), (packed, F32)],
        *halo(rounded),
        block,
        scalars=2,
        scratch=window,
    )
    theta, start_theta, residual, rounded = run(
        lambda *refs: residual_kernel(root, *refs),
        "residual",
        [(square, F32), (square, F32), (slab, F32), rounded_copies],
        total(theta_part),
        block,
        applied,
    )
    trial = jnp.concatenate([block, residual], axis=0)
    image, grams = run(
        trial_kernel,
        "apply_first",
        [(slab, F32), ((2 * columns, 2 * columns), F32)],
        *halo(rounded),
        trial,
        applied,
        scalars=2,
        scratch=window,
    )
    grams = total(grams)
    coeffs, next_theta, next_trial, next_applied, rounded = run(
        first_step_kernel,
        "first_step",
        [
            ((2 * columns, 2 * columns), F32),
            (square, F32),
            ((3 * columns, rows_dev), F32),
            ((2 * columns, rows_dev), F32),
            rounded_copies,
        ],
        grams,
        theta,
        trial,
        applied,
        image,
        scratch=[pltpu.VMEM((2 * columns, columns), F32)],
    )
    carried, pieces = run(
        carry_kernel,
        "carry",
        [((4 * columns, 2 * columns), F32), ((rows_dev, 3 * columns), F32)],
        coeffs,
        grams,
        theta,
        next_trial,
        row_order,
    )
    arrived = lax.all_to_all(pieces, "node", split_axis=0, concat_axis=0, tiled=True)
    _, last_grams = run(
        trial_kernel,
        "apply_last",
        [(slab, F32), ((3 * columns, 2 * columns), F32)],
        *halo(rounded),
        next_trial,
        next_applied,
        scalars=2,
        scratch=window,
    )
    ritz, embedding = run(
        lambda *refs: last_step_kernel(root, *refs),
        "last_step",
        [(square, F32), (slab, F32)],
        total(last_grams),
        carried,
        next_theta,
        arrived,
        scratch=[pltpu.VMEM((3 * columns, columns), F32)],
    )
    return (embedding, ritz, start_theta)


def solution(mesh):
    return jax.shard_map(
        local,
        mesh=mesh,
        in_specs=(
            P(None, BOTH),
            P(BOTH, None, None, None),
            P(BOTH, None),
            P(BOTH, None),
            P(BOTH),
            P(BOTH, None),
        ),
        out_specs=(P(None, BOTH), P(), P()),
        check_vma=False,
    )
```

```python
import jax
import jax.numpy as jnp
from jax import lax
from jax.experimental import pallas as pl
from jax.experimental.pallas import tpu as pltpu
from jax.sharding import PartitionSpec as P

REACH = 2
NSUB = 4
BLOCK = 4
RADIUS = 0.18
BOTH = ("grp", "node")
CORE_Y = (1, 2, 4, 8)
Z_X = (16, 32, 64, 128, 256)
CORE_X = (1, 128, 256)
Y_Z = (2, 4, 8, 16, 32, 64)


def groups_over(bits):
    mask = sum(bits)
    groups = []
    for base in range(512):
        if base & mask:
            continue
        members = [base]
        for bit in bits:
            members = members + [member | bit for member in members]
        groups.append(members)
    return groups


def swap(values, bits):
    return lax.all_to_all(
        values, BOTH, split_axis=0, concat_axis=0, tiled=True, axis_index_groups=groups_over(bits)
    )


def run(kernel, name, results, *operands, scalars=0, scratch=()):
    smem = pl.BlockSpec(memory_space=pltpu.SMEM)
    vmem = pl.BlockSpec(memory_space=pltpu.VMEM)
    return pl.pallas_call(
        kernel,
        out_shape=[jax.ShapeDtypeStruct(shape, dtype) for shape, dtype in results],
        in_specs=[smem] * scalars + [vmem] * (len(operands) - scalars),
        out_specs=[vmem] * len(results),
        scratch_shapes=list(scratch),
        compiler_params=pltpu.CompilerParams(vmem_limit_bytes=32 << 20),
        name=name,
    )(*operands)


F32 = jnp.float32
BF16 = jnp.bfloat16


def sum_kernel(parts_ref, out_ref):
    parts = [parts_ref[i] for i in range(parts_ref.shape[0])]
    while len(parts) > 1:
        parts = [parts[i] + parts[i + 1] for i in range(0, len(parts), 2)]
    for i in range(out_ref.shape[0]):
        out_ref[i] = parts[0]


def sum_copies(parts, count):
    return run(sum_kernel, "sum_copies", [((count,) + parts.shape[1:], F32)], parts)[0]


def total(part, inner, outer):
    rows = part.shape[0]
    count = 2 ** len(inner)
    scattered = swap(part.reshape(count, rows // count, 128), inner)
    shared = swap(sum_copies(scattered, 2 ** len(outer)), outer)
    return swap(sum_copies(shared, count), inner).reshape(rows, 128)


def mm(left, right, contract):
    return lax.dot_general(
        left,
        right,
        ((contract[:1], contract[1:]), ((), ())),
        precision=lax.Precision.HIGHEST,
        preferred_element_type=jnp.float32,
    )


def nn(left, right):
    return mm(left, right, (1, 0))


def nt(left, right):
    return mm(left, right, (1, 1))


def tn(left, right):
    return mm(left, right, (0, 0))


def eye(order):
    row = lax.broadcasted_iota(jnp.int32, (order, order), 0)
    column = lax.broadcasted_iota(jnp.int32, (order, order), 1)
    return jnp.where(row == column, jnp.float32(1.0), jnp.float32(0.0))


def inverse_root(value):
    guess = lax.rsqrt(value)
    return guess * (1.5 - 0.5 * value * guess * guess)


def inverse_factor(matrix):
    order = matrix.shape[0]
    lanes = 2 * order
    both = jnp.concatenate([matrix, eye(order)], axis=1)
    bands = [both[8 * i : 8 * i + 8] for i in range(order // 8)]
    sublane = lax.broadcasted_iota(jnp.int32, (8, lanes), 0)
    done = [None] * len(bands)
    for first in range(0, order, BLOCK):
        band = first // 8
        base = first % 8
        last_of_band = base + BLOCK == 8
        live = range(band, len(bands))
        column = [
            [jnp.broadcast_to(bands[i][:, first + k : first + k + 1], (8, lanes)) for i in live]
            for k in range(BLOCK)
        ]
        row = [
            jnp.broadcast_to(bands[band][base + k : base + k + 1], (8, lanes)) for k in range(BLOCK)
        ]
        entry = [
            [
                jnp.broadcast_to(column[l][0][base + k : base + k + 1], (8, lanes))
                for l in range(k + 1)
            ]
            for k in range(BLOCK)
        ]
        inverse = []
        factor = [[None] * BLOCK for _ in range(BLOCK)]
        for l in range(BLOCK):
            inverse.append(1.0 / entry[l][l])
            for k in range(l + 1, BLOCK):
                factor[k][l] = entry[k][l] * inverse[l]
                for m in range(l + 1, k + 1):
                    entry[k][m] = entry[k][m] - factor[k][l] * entry[m][l]
        start = 1 if last_of_band else 0
        for k in range(BLOCK):
            for l in range(k):
                row[k] = row[k] - factor[k][l] * row[l]
                for i in range(start, len(live)):
                    column[k][i] = column[k][i] - factor[k][l] * column[l][i]
        for k in range(BLOCK):
            scaled = row[k] * inverse_root(entry[k][k])
            if done[band] is None:
                done[band] = scaled
            else:
                done[band] = jnp.where(sublane == base + k, scaled, done[band])
            left = row[k] * inverse[k]
            for i in range(start, len(live)):
                bands[band + i] = bands[band + i] - column[k][i] * left
    return jnp.concatenate(done, axis=0)[:, order:]


def half_sum(matrix):
    return 0.5 * (matrix + matrix.T)


def orthonormal(image):
    return nt(image, inverse_factor(tn(image, image)))


def project(linv, gram, basis_ref):
    order = linv.shape[0]
    columns = basis_ref.shape[1]
    projected = half_sum(nt(nn(linv, gram), linv))
    scale = jnp.sqrt(jnp.sum(projected * projected, keepdims=True) + 1e-06)
    unit = projected / scale
    identity = eye(order)
    filtered = unit + 1.25 * identity
    square = nn(filtered, filtered)
    fourth = nn(square, square)
    eighth = nn(fourth, fourth)
    unit2 = square - 2.5 * unit - 1.5625 * identity
    unit4 = nn(unit2, unit2)
    bound = jnp.sum(unit4 * unit4)
    basis_ref[...] = orthonormal(nn(eighth, eighth[:, :columns]))

    @pl.when(jnp.logical_not(bound < RADIUS**8))
    def _():
        basis_ref[...] = identity[:, :columns]

        def sweep(_, carry):
            basis_ref[...] = orthonormal(nn(fourth, basis_ref[...]))
            return carry

        lax.fori_loop(0, NSUB, sweep, 0)

    basis = basis_ref[...]
    coeffs = tn(linv, basis)
    theta = half_sum(tn(basis, nn(projected, basis)))
    return coeffs, theta


def store_packed(ref, matrix):
    half = matrix.shape[0] // 2
    ref[...] = jnp.concatenate([matrix[:half], matrix[half:]], axis=1)


def load_packed(ref):
    width = ref.shape[1] // 2
    return jnp.concatenate([ref[:, :width], ref[:, width:]], axis=0)


def store_copies(ref, value):
    for i in range(ref.shape[0]):
        ref[i] = value


def gram_kernel(start_ref, gram_ref, copies_ref):
    start = start_ref[...]
    store_packed(gram_ref, nt(start, start))
    store_copies(copies_ref, start)


def pick_kernel(index_ref, own_ref, up_ref, down_ref, slots_ref):
    count = own_ref.shape[0]
    for slot in range(slots_ref.shape[0]):
        chosen = index_ref[slot]
        for side, ref in enumerate((down_ref, own_ref, up_ref)):

            @pl.when(chosen // count == side)
            def _(ref=ref, slot=slot, chosen=chosen):
                slots_ref[slot] = ref[chosen % count]


def multiply_tiles(weight_ref, tiles_ref, slot_values):
    acc = None
    for slot in range(tiles_ref.shape[0]):
        product = lax.dot_general(
            slot_values(slot).astype(BF16),
            tiles_ref[slot],
            (((1,), (1,)), ((), ())),
            preferred_element_type=F32,
        )
        product = weight_ref[slot] * product
        acc = product if acc is None else acc + product
    return acc


def start_kernel(weight_ref, gram_ref, start_ref, slots_ref, tiles_ref, block_ref, block_slots_ref, applied_ref, copies_ref, theta_ref):
    inverse = inverse_factor(load_packed(gram_ref))
    block = nn(inverse, start_ref[...])
    block_ref[...] = block

    def values(slot):
        there = nn(inverse, slots_ref[slot])
        block_slots_ref[slot] = there
        return there

    applied = multiply_tiles(weight_ref, tiles_ref, values)
    applied_ref[...] = applied
    store_copies(copies_ref, applied)
    store_packed(theta_ref, 0.5 * (nt(block, applied) + nt(applied, block)))


def first_kernel(root, weight_ref, sum_ref, block_ref, applied_ref, block_slots_ref, applied_slots_ref, tiles_ref, theta_ref, start_theta_ref, residual_ref, residual_slots_ref, image_ref, copies_ref, grams_ref):
    theta = half_sum(load_packed(sum_ref))
    theta_ref[...] = theta
    start_theta_ref[...] = root * theta
    block = block_ref[...]
    applied = applied_ref[...]
    residual = applied - nn(theta, block)
    residual_ref[...] = residual

    def values(slot):
        there = applied_slots_ref[slot] - nn(theta, block_slots_ref[slot])
        residual_slots_ref[slot] = there
        return there

    image = multiply_tiles(weight_ref, tiles_ref, values)
    image_ref[...] = image
    store_copies(copies_ref, image)
    trial = jnp.concatenate([block, residual], axis=0)
    applied_trial = jnp.concatenate([applied, image], axis=0)
    cross = 0.5 * (nt(trial, image) + nt(applied_trial, residual))
    grams_ref[...] = jnp.concatenate([nt(trial, residual), cross], axis=1)


def assemble_first(grams, theta):
    columns = theta.shape[0]
    cross = grams[:columns, columns:]
    overlap = grams[:columns, :columns]
    own = half_sum(grams[columns:, columns:])
    basis = (overlap, grams[columns:, :columns])
    gram = jnp.concatenate(
        [jnp.concatenate([theta, cross], axis=1), jnp.concatenate([cross.T, own], axis=1)], axis=0
    )
    return basis, gram


def second_kernel(weight_ref, grams_ref, theta_ref, block_ref, residual_ref, applied_ref, image_ref, block_slots_ref, residual_slots_ref, applied_slots_ref, image_slots_ref, tiles_ref, coeffs_ref, theta_out_ref, trial_ref, grams_out_ref, basis_ref):
    columns = theta_ref.shape[0]
    width = block_ref.shape[1]
    (overlap, own), gram = assemble_first(grams_ref[...], theta_ref[...])
    factor = inverse_factor(own - tn(overlap, overlap))
    linv = jnp.concatenate(
        [
            jnp.concatenate([eye(columns), jnp.zeros((columns, columns), F32)], axis=1),
            jnp.concatenate([-nt(factor, overlap), factor], axis=1),
        ],
        axis=0,
    )
    coeffs, theta = project(linv, gram, basis_ref)
    theta_out_ref[...] = theta
    lower = jnp.concatenate([jnp.zeros((columns, columns), F32), coeffs[columns:]], axis=0)
    both = jnp.concatenate([coeffs, lower], axis=1)
    coeffs_ref[...] = both
    mix = jnp.concatenate([coeffs, -nn(coeffs, theta)], axis=0).T

    def values(slot):
        parts = (applied_slots_ref, image_slots_ref, block_slots_ref, residual_slots_ref)
        return nn(mix, jnp.concatenate([ref[slot] for ref in parts], axis=0))

    image = multiply_tiles(weight_ref, tiles_ref, values)
    block, applied = block_ref[...], applied_ref[...]
    previous, previous_image = residual_ref[...], image_ref[...]
    residual = nn(mix, jnp.concatenate([applied, previous_image, block, previous], axis=0))
    old_trial = jnp.concatenate([block, previous], axis=0)
    old_applied = jnp.concatenate([applied, previous_image], axis=0)
    fresh = tn(both, jnp.concatenate([old_trial, old_applied], axis=1))
    trial = jnp.concatenate([fresh[:columns, :width], residual, fresh[columns:, :width]], axis=0)
    trial_ref[...] = trial
    applied_trial = jnp.concatenate([fresh[:columns, width:], image, fresh[columns:, width:]], axis=0)
    cross = 0.5 * (nt(trial, image) + nt(applied_trial, residual))
    grams_out_ref[...] = jnp.concatenate([nt(trial, residual), cross], axis=1)


def carry_kernel(coeffs_ref, grams_ref, theta_ref, trial_ref, order_ref, carried_ref, pieces_ref):
    columns = theta_ref.shape[0]
    coeffs = coeffs_ref[...]
    (overlap, own), gram = assemble_first(grams_ref[...], theta_ref[...])
    basis = jnp.concatenate(
        [
            jnp.concatenate([eye(columns), overlap], axis=1),
            jnp.concatenate([overlap.T, own], axis=1),
        ],
        axis=0,
    )
    carried_ref[...] = jnp.concatenate(
        [tn(coeffs, nn(basis, coeffs)), tn(coeffs, nn(gram, coeffs))], axis=0
    )
    width = trial_ref.shape[1]
    place = lax.broadcasted_iota(jnp.int32, (width, width), 0)
    pick = jnp.where(place == order_ref[...], F32(1.0), F32(0.0))
    pieces_ref[...] = mm(pick, trial_ref[...], (0, 1))


def last_step_kernel(root, grams_ref, carried_ref, theta_ref, arrived_ref, theta_out_ref, embedding_ref, basis_ref):
    columns = theta_ref.shape[0]
    grams = grams_ref[...]
    carried = carried_ref[...]
    wide = 2 * columns
    overlap = jnp.concatenate([grams[:columns, :columns], carried[:columns, columns:wide]], axis=1)
    mixed = grams[wide:, :columns]
    spread = tn(overlap, overlap)
    first = grams[columns:wide, :columns] - spread[:columns, :columns]
    corner = mixed.T - spread[:columns, columns:]
    second = carried[columns:wide, columns:wide] - spread[columns:, columns:]
    factor = inverse_factor(first)
    middle = nn(factor, corner)
    other = inverse_factor(second - tn(middle, middle))
    zero = jnp.zeros((columns, columns), F32)
    lower = jnp.concatenate(
        [
            jnp.concatenate([factor, zero], axis=1),
            jnp.concatenate([-nn(other, tn(middle, factor)), other], axis=1),
        ],
        axis=0,
    )
    linv = jnp.concatenate(
        [
            jnp.concatenate([eye(columns), zero, zero], axis=1),
            jnp.concatenate([-nt(lower, overlap), lower], axis=1),
        ],
        axis=0,
    )
    cross = grams[:columns, columns:]
    own = half_sum(grams[columns:wide, columns:])
    momentum_cross = grams[wide:, columns:]
    block_momentum = carried[wide : wide + columns, columns:wide]
    momentum = half_sum(carried[wide + columns :, columns:wide])
    gram = jnp.concatenate(
        [
            jnp.concatenate([theta_ref[...], cross, block_momentum], axis=1),
            jnp.concatenate([cross.T, own, momentum_cross.T], axis=1),
            jnp.concatenate([block_momentum.T, momentum_cross, momentum], axis=1),
        ],
        axis=0,
    )
    coeffs, theta = project(linv, gram, basis_ref)
    theta_out_ref[...] = theta
    embedding_ref[...] = root * mm(coeffs, arrived_ref[...], (0, 1))


def local(start_block, weight_tiles, tile_scales, neighbour_ids, live_counts, row_order):
    columns = start_block.shape[0]
    rows_dev = start_block.shape[1]
    groups = lax.axis_size("grp")
    nodes = lax.axis_size("node")
    here = lax.axis_index("node")
    ids = neighbour_ids[0]
    slots = ids.shape[0]
    group_index = ids // nodes
    node_index = ids % nodes
    chips = nodes // 2
    chip_offset = (node_index // 2 - here // 2 + 1 + chips) % chips
    index = jnp.clip(chip_offset * 8 + node_index % 2 + 2 * group_index, 0, 23).astype(jnp.int32)
    slot_iota = jnp.arange(slots, dtype=jnp.int32)
    weights = jnp.where(slot_iota < live_counts[0], tile_scales[0], F32(0.0))
    tiles = weight_tiles[0]
    to_next = [(source, (source + 2) % nodes) for source in range(nodes)]
    to_last = [(source, (source - 2) % nodes) for source in range(nodes)]
    root = float(rows_dev * groups * nodes) ** 0.5
    slab = (columns, rows_dev)
    square = (columns, columns)
    packed = (columns // 2, 2 * columns)
    slab_copies = ((2 * groups,) + slab, F32)
    slab_slots = ((slots,) + slab, F32)

    def slot_rows(copied):
        own = swap(copied, CORE_X)
        down = lax.ppermute(own, "node", to_next)
        up = lax.ppermute(own, "node", to_last)
        return run(pick_kernel, "pick_slots", [slab_slots], index, own, up, down, scalars=1)[0]

    gram, copied = run(gram_kernel, "start_gram", [(packed, F32), slab_copies], start_block)
    start_slots = slot_rows(copied)
    block, block_slots, applied, copied, theta_part = run(
        start_kernel,
        "start_step",
        [(slab, F32), slab_slots, (slab, F32), slab_copies, (packed, F32)],
        weights,
        total(gram, CORE_X, Y_Z),
        start_block,
        start_slots,
        tiles,
        scalars=1,
    )
    applied_slots = slot_rows(copied)
    theta, start_theta, residual, residual_slots, image, copied, grams = run(
        lambda *refs: first_kernel(root, *refs),
        "first_residual",
        [
            (square, F32),
            (square, F32),
            (slab, F32),
            slab_slots,
            (slab, F32),
            slab_copies,
            ((2 * columns, 2 * columns), F32),
        ],
        weights,
        total(theta_part, CORE_X, Y_Z),
        block,
        applied,
        block_slots,
        applied_slots,
        tiles,
        scalars=1,
    )
    image_slots = slot_rows(copied)
    grams = total(grams, CORE_Y, Z_X)
    coeffs, next_theta, trial, last_grams = run(
        second_kernel,
        "second_step",
        [
            ((2 * columns, 2 * columns), F32),
            (square, F32),
            ((3 * columns, rows_dev), F32),
            ((3 * columns, 2 * columns), F32),
        ],
        weights,
        grams,
        theta,
        block,
        residual,
        applied,
        image,
        block_slots,
        residual_slots,
        applied_slots,
        image_slots,
        tiles,
        scalars=1,
        scratch=[pltpu.VMEM((2 * columns, columns), F32)],
    )
    carried, pieces = run(
        carry_kernel,
        "carry",
        [((4 * columns, 2 * columns), F32), ((rows_dev, 3 * columns), F32)],
        coeffs,
        grams,
        theta,
        trial,
        row_order,
    )
    arrived = lax.all_to_all(pieces, "node", split_axis=0, concat_axis=0, tiled=True)
    ritz, embedding = run(
        lambda *refs: last_step_kernel(root, *refs),
        "last_step",
        [(square, F32), (slab, F32)],
        total(last_grams, CORE_Y, Z_X),
        carried,
        next_theta,
        arrived,
        scratch=[pltpu.VMEM((3 * columns, columns), F32)],
    )
    return (embedding, ritz, start_theta)


def solution(mesh):
    return jax.shard_map(
        local,
        mesh=mesh,
        in_specs=(
            P(None, BOTH),
            P(BOTH, None, None, None),
            P(BOTH, None),
            P(BOTH, None),
            P(BOTH),
            P(BOTH, None),
        ),
        out_specs=(P(None, BOTH), P(), P()),
        check_vma=False,
    )
```

```python
import jax
import jax.numpy as jnp
from jax import lax
from jax.experimental import pallas as pl
from jax.experimental.pallas import tpu as pltpu
from jax.sharding import PartitionSpec as P

REACH = 2
NSUB = 4
BLOCK = 4
RADIUS = 0.18
BOTH = ("grp", "node")
CORE_X = (1, 128, 256)
Y_Z = (2, 4, 8, 16, 32, 64)


def groups_over(bits):
    mask = sum(bits)
    groups = []
    for base in range(512):
        if base & mask:
            continue
        members = [base]
        for bit in bits:
            members = members + [member | bit for member in members]
        groups.append(members)
    return groups


def swap(values, bits):
    return lax.all_to_all(
        values, BOTH, split_axis=0, concat_axis=0, tiled=True, axis_index_groups=groups_over(bits)
    )


def run(kernel, name, results, *operands, scalars=0, scratch=()):
    smem = pl.BlockSpec(memory_space=pltpu.SMEM)
    vmem = pl.BlockSpec(memory_space=pltpu.VMEM)
    return pl.pallas_call(
        kernel,
        out_shape=[jax.ShapeDtypeStruct(shape, dtype) for shape, dtype in results],
        in_specs=[smem] * scalars + [vmem] * (len(operands) - scalars),
        out_specs=[vmem] * len(results),
        scratch_shapes=list(scratch),
        compiler_params=pltpu.CompilerParams(vmem_limit_bytes=32 << 20),
        name=name,
    )(*operands)


F32 = jnp.float32
BF16 = jnp.bfloat16


def tree_sum(parts):
    while len(parts) > 1:
        parts = [parts[i] + parts[i + 1] for i in range(0, len(parts), 2)]
    return parts[0]


def sum_kernel(first, parts_ref, out_ref):
    summed = tree_sum([parts_ref[i, first:] for i in range(parts_ref.shape[0])])
    for i in range(out_ref.shape[0]):
        out_ref[i] = summed


def sum_copies(parts, count, first=0):
    return run(
        lambda *refs: sum_kernel(first, *refs),
        "sum_copies",
        [((count, parts.shape[1] - first, parts.shape[2]), F32)],
        parts,
    )[0]


def row_sum_kernel(parts_ref, out_ref):
    summed = jnp.sum(parts_ref[...], axis=0, keepdims=True)
    out_ref[...] = jnp.broadcast_to(summed, out_ref.shape)


def gather_kernel(parts_ref, pieces_ref, out_ref):
    summed = tree_sum([parts_ref[i : i + 1] for i in range(parts_ref.shape[0])])
    rows, width = pieces_ref.shape
    out_ref[:, :width] = jnp.broadcast_to(summed, (rows, width))
    out_ref[:, width:] = pieces_ref[...]


def mm(left, right, contract):
    return lax.dot_general(
        left,
        right,
        ((contract[:1], contract[1:]), ((), ())),
        precision=lax.Precision.HIGHEST,
        preferred_element_type=jnp.float32,
    )


def nn(left, right):
    return mm(left, right, (1, 0))


def nt(left, right):
    return mm(left, right, (1, 1))


def tn(left, right):
    return mm(left, right, (0, 0))


def eye(order):
    row = lax.broadcasted_iota(jnp.int32, (order, order), 0)
    column = lax.broadcasted_iota(jnp.int32, (order, order), 1)
    return jnp.where(row == column, jnp.float32(1.0), jnp.float32(0.0))


def inverse_root(value):
    guess = lax.rsqrt(value)
    return guess * (1.5 - 0.5 * value * guess * guess)


def inverse_factor(matrix):
    order = matrix.shape[0]
    lanes = 2 * order
    both = jnp.concatenate([matrix, eye(order)], axis=1)
    bands = [both[8 * i : 8 * i + 8] for i in range(order // 8)]
    sublane = lax.broadcasted_iota(jnp.int32, (8, lanes), 0)
    done = [None] * len(bands)
    for first in range(0, order, BLOCK):
        band = first // 8
        base = first % 8
        last_of_band = base + BLOCK == 8
        live = range(band, len(bands))
        column = [
            [jnp.broadcast_to(bands[i][:, first + k : first + k + 1], (8, lanes)) for i in live]
            for k in range(BLOCK)
        ]
        row = [
            jnp.broadcast_to(bands[band][base + k : base + k + 1], (8, lanes)) for k in range(BLOCK)
        ]
        entry = [
            [
                jnp.broadcast_to(column[l][0][base + k : base + k + 1], (8, lanes))
                for l in range(k + 1)
            ]
            for k in range(BLOCK)
        ]
        inverse = []
        factor = [[None] * BLOCK for _ in range(BLOCK)]
        for l in range(BLOCK):
            inverse.append(1.0 / entry[l][l])
            for k in range(l + 1, BLOCK):
                factor[k][l] = entry[k][l] * inverse[l]
                for m in range(l + 1, k + 1):
                    entry[k][m] = entry[k][m] - factor[k][l] * entry[m][l]
        start = 1 if last_of_band else 0
        for k in range(BLOCK):
            for l in range(k):
                row[k] = row[k] - factor[k][l] * row[l]
                for i in range(start, len(live)):
                    column[k][i] = column[k][i] - factor[k][l] * column[l][i]
        for k in range(BLOCK):
            scaled = row[k] * inverse_root(entry[k][k])
            if done[band] is None:
                done[band] = scaled
            else:
                done[band] = jnp.where(sublane == base + k, scaled, done[band])
            left = row[k] * inverse[k]
            for i in range(start, len(live)):
                bands[band + i] = bands[band + i] - column[k][i] * left
    return jnp.concatenate(done, axis=0)[:, order:]


def half_sum(matrix):
    return 0.5 * (matrix + matrix.T)


def orthonormal(image):
    return nt(image, inverse_factor(tn(image, image)))


def project(linv, gram, basis_ref):
    order = linv.shape[0]
    columns = basis_ref.shape[1]
    projected = half_sum(nt(nn(linv, gram), linv))
    scale = jnp.sqrt(jnp.sum(projected * projected, keepdims=True) + 1e-06)
    unit = projected / scale
    identity = eye(order)
    filtered = unit + 1.25 * identity
    square = nn(filtered, filtered)
    fourth = nn(square, square)
    eighth = nn(fourth, fourth)
    unit2 = square - 2.5 * unit - 1.5625 * identity
    unit4 = nn(unit2, unit2)
    bound = jnp.sum(unit4 * unit4)
    basis_ref[...] = orthonormal(nn(eighth, eighth[:, :columns]))

    @pl.when(jnp.logical_not(bound < RADIUS**8))
    def _():
        basis_ref[...] = identity[:, :columns]

        def sweep(_, carry):
            basis_ref[...] = orthonormal(nn(fourth, basis_ref[...]))
            return carry

        lax.fori_loop(0, NSUB, sweep, 0)

    basis = basis_ref[...]
    coeffs = tn(linv, basis)
    theta = half_sum(tn(basis, nn(projected, basis)))
    return coeffs, theta


def load_packed(ref):
    width = ref.shape[1] // 2
    return jnp.concatenate([ref[:, :width], ref[:, width:]], axis=0)


def store_parcel(ref, value, partial):
    members, rows = ref.shape[0], value.shape[0]
    share = partial.shape[0] // members
    for i in range(members):
        ref[i, :rows] = value
        ref[i, rows:] = partial[share * i : share * (i + 1)]


def pack(matrix):
    half = matrix.shape[0] // 2
    return jnp.concatenate([matrix[:half], matrix[half:]], axis=1)


def gram_kernel(start_ref, parcel_ref):
    start = start_ref[...]
    store_parcel(parcel_ref, start, pack(nt(start, start)))


def pick_kernel(index_ref, own_ref, up_ref, down_ref, slots_ref):
    count = own_ref.shape[0]
    for slot in range(slots_ref.shape[0]):
        chosen = index_ref[slot]
        for side, ref in enumerate((down_ref, own_ref, up_ref)):

            @pl.when(chosen // count == side)
            def _(ref=ref, slot=slot, chosen=chosen):
                slots_ref[slot] = ref[chosen % count, : slots_ref.shape[1]]


def multiply_tiles(weight_ref, tiles_ref, slot_values):
    acc = None
    for slot in range(tiles_ref.shape[0]):
        product = lax.dot_general(
            slot_values(slot).astype(BF16),
            tiles_ref[slot],
            (((1,), (1,)), ((), ())),
            preferred_element_type=F32,
        )
        product = weight_ref[slot] * product
        acc = product if acc is None else acc + product
    return acc


def start_kernel(weight_ref, gram_ref, start_ref, slots_ref, tiles_ref, block_ref, block_slots_ref, applied_ref, parcel_ref):
    inverse = inverse_factor(load_packed(gram_ref))
    block = nn(inverse, start_ref[...])
    block_ref[...] = block

    def values(slot):
        there = nn(inverse, slots_ref[slot])
        block_slots_ref[slot] = there
        return there

    applied = multiply_tiles(weight_ref, tiles_ref, values)
    applied_ref[...] = applied
    store_parcel(parcel_ref, applied, pack(0.5 * (nt(block, applied) + nt(applied, block))))


def first_kernel(root, weight_ref, sum_ref, block_ref, applied_ref, block_slots_ref, applied_slots_ref, tiles_ref, theta_ref, start_theta_ref, residual_ref, residual_slots_ref, image_ref, parcel_ref):
    theta = half_sum(load_packed(sum_ref))
    theta_ref[...] = theta
    start_theta_ref[...] = root * theta
    block = block_ref[...]
    applied = applied_ref[...]
    residual = applied - nn(theta, block)
    residual_ref[...] = residual

    def values(slot):
        there = applied_slots_ref[slot] - nn(theta, block_slots_ref[slot])
        residual_slots_ref[slot] = there
        return there

    image = multiply_tiles(weight_ref, tiles_ref, values)
    image_ref[...] = image
    trial = jnp.concatenate([block, residual], axis=0)
    applied_trial = jnp.concatenate([applied, image], axis=0)
    cross = 0.5 * (nt(trial, image) + nt(applied_trial, residual))
    store_parcel(parcel_ref, image, jnp.concatenate([nt(trial, residual), cross], axis=1))


def assemble_first(grams, theta):
    columns = theta.shape[0]
    cross = grams[:columns, columns:]
    overlap = grams[:columns, :columns]
    own = half_sum(grams[columns:, columns:])
    basis = (overlap, grams[columns:, :columns])
    gram = jnp.concatenate(
        [jnp.concatenate([theta, cross], axis=1), jnp.concatenate([cross.T, own], axis=1)], axis=0
    )
    return basis, gram


def second_kernel(weight_ref, grams_ref, theta_ref, block_ref, residual_ref, applied_ref, image_ref, block_slots_ref, residual_slots_ref, applied_slots_ref, image_slots_ref, tiles_ref, coeffs_ref, theta_out_ref, trial_ref, grams_out_ref, basis_ref):
    columns = theta_ref.shape[0]
    width = block_ref.shape[1]
    (overlap, own), gram = assemble_first(grams_ref[...], theta_ref[...])
    factor = inverse_factor(own - tn(overlap, overlap))
    linv = jnp.concatenate(
        [
            jnp.concatenate([eye(columns), jnp.zeros((columns, columns), F32)], axis=1),
            jnp.concatenate([-nt(factor, overlap), factor], axis=1),
        ],
        axis=0,
    )
    coeffs, theta = project(linv, gram, basis_ref)
    theta_out_ref[...] = theta
    lower = jnp.concatenate([jnp.zeros((columns, columns), F32), coeffs[columns:]], axis=0)
    both = jnp.concatenate([coeffs, lower], axis=1)
    coeffs_ref[...] = both
    mix = jnp.concatenate([coeffs, -nn(coeffs, theta)], axis=0).T

    def values(slot):
        parts = (applied_slots_ref, image_slots_ref, block_slots_ref, residual_slots_ref)
        return nn(mix, jnp.concatenate([ref[slot] for ref in parts], axis=0))

    image = multiply_tiles(weight_ref, tiles_ref, values)
    block, applied = block_ref[...], applied_ref[...]
    previous, previous_image = residual_ref[...], image_ref[...]
    residual = nn(mix, jnp.concatenate([applied, previous_image, block, previous], axis=0))
    old_trial = jnp.concatenate([block, previous], axis=0)
    old_applied = jnp.concatenate([applied, previous_image], axis=0)
    fresh = tn(both, jnp.concatenate([old_trial, old_applied], axis=1))
    trial = jnp.concatenate([fresh[:columns, :width], residual, fresh[columns:, :width]], axis=0)
    trial_ref[...] = trial
    applied_trial = jnp.concatenate([fresh[:columns, width:], image, fresh[columns:, width:]], axis=0)
    cross = 0.5 * (nt(image, trial) + nt(residual, applied_trial))
    grams_out_ref[...] = jnp.concatenate([nt(residual, trial), cross], axis=0)


def carry_kernel(coeffs_ref, grams_ref, theta_ref, trial_ref, order_ref, carried_ref, pieces_ref):
    columns = theta_ref.shape[0]
    coeffs = coeffs_ref[...]
    (overlap, own), gram = assemble_first(grams_ref[...], theta_ref[...])
    basis = jnp.concatenate(
        [
            jnp.concatenate([eye(columns), overlap], axis=1),
            jnp.concatenate([overlap.T, own], axis=1),
        ],
        axis=0,
    )
    carried_ref[...] = jnp.concatenate(
        [tn(coeffs, nn(basis, coeffs)), tn(coeffs, nn(gram, coeffs))], axis=0
    )
    width = trial_ref.shape[1]
    place = lax.broadcasted_iota(jnp.int32, (width, width), 0)
    pick = jnp.where(place == order_ref[...], F32(1.0), F32(0.0))
    pieces_ref[...] = mm(pick, trial_ref[...], (0, 1))


def last_step_kernel(root, gathered_ref, carried_ref, theta_ref, theta_out_ref, embedding_ref, basis_ref):
    columns = theta_ref.shape[0]
    width = gathered_ref.shape[1] // 2
    grams = gathered_ref[:, :width].T
    arrived = gathered_ref[:, width:]
    carried = carried_ref[...]
    wide = 2 * columns
    overlap = jnp.concatenate([grams[:columns, :columns], carried[:columns, columns:wide]], axis=1)
    mixed = grams[wide:, :columns]
    spread = tn(overlap, overlap)
    first = grams[columns:wide, :columns] - spread[:columns, :columns]
    corner = mixed.T - spread[:columns, columns:]
    second = carried[columns:wide, columns:wide] - spread[columns:, columns:]
    factor = inverse_factor(first)
    middle = nn(factor, corner)
    other = inverse_factor(second - tn(middle, middle))
    zero = jnp.zeros((columns, columns), F32)
    lower = jnp.concatenate(
        [
            jnp.concatenate([factor, zero], axis=1),
            jnp.concatenate([-nn(other, tn(middle, factor)), other], axis=1),
        ],
        axis=0,
    )
    linv = jnp.concatenate(
        [
            jnp.concatenate([eye(columns), zero, zero], axis=1),
            jnp.concatenate([-nt(lower, overlap), lower], axis=1),
        ],
        axis=0,
    )
    cross = grams[:columns, columns:]
    own = half_sum(grams[columns:wide, columns:])
    momentum_cross = grams[wide:, columns:]
    block_momentum = carried[wide : wide + columns, columns:wide]
    momentum = half_sum(carried[wide + columns :, columns:wide])
    gram = jnp.concatenate(
        [
            jnp.concatenate([theta_ref[...], cross, block_momentum], axis=1),
            jnp.concatenate([cross.T, own, momentum_cross.T], axis=1),
            jnp.concatenate([block_momentum.T, momentum_cross, momentum], axis=1),
        ],
        axis=0,
    )
    coeffs, theta = project(linv, gram, basis_ref)
    theta_out_ref[...] = theta
    embedding_ref[...] = root * mm(coeffs, arrived, (0, 1))


def local(start_block, weight_tiles, tile_scales, neighbour_ids, live_counts, row_order):
    columns = start_block.shape[0]
    rows_dev = start_block.shape[1]
    groups = lax.axis_size("grp")
    nodes = lax.axis_size("node")
    here = lax.axis_index("node")
    ids = neighbour_ids[0]
    slots = ids.shape[0]
    group_index = ids // nodes
    node_index = ids % nodes
    chips = nodes // 2
    chip_offset = (node_index // 2 - here // 2 + 1 + chips) % chips
    index = jnp.clip(chip_offset * 8 + node_index % 2 + 2 * group_index, 0, 23).astype(jnp.int32)
    slot_iota = jnp.arange(slots, dtype=jnp.int32)
    weights = jnp.where(slot_iota < live_counts[0], tile_scales[0], F32(0.0))
    tiles = weight_tiles[0]
    to_next = [(source, (source + 2) % nodes) for source in range(nodes)]
    to_last = [(source, (source - 2) % nodes) for source in range(nodes)]
    root = float(rows_dev * groups * nodes) ** 0.5
    slab = (columns, rows_dev)
    square = (columns, columns)
    packed = (columns // 2, 2 * columns)
    slab_slots = ((slots,) + slab, F32)

    def exchange(parcel):
        received = swap(parcel, CORE_X)
        down = lax.ppermute(received, "node", to_next)
        up = lax.ppermute(received, "node", to_last)
        rows = run(pick_kernel, "pick_slots", [slab_slots], index, received, up, down, scalars=1)[0]
        shared = swap(sum_copies(received, 2 ** len(Y_Z), columns), Y_Z)
        summed = swap(sum_copies(shared, 2 ** len(CORE_X)), CORE_X)
        return rows, summed.reshape(-1, rows_dev)

    def parcel_of(rows):
        members = 2 * groups
        return ((members, columns + rows // members, rows_dev), F32)

    small = parcel_of(columns // 2)
    start_slots, gram = exchange(run(gram_kernel, "start_gram", [small], start_block)[0])
    block, block_slots, applied, parcel = run(
        start_kernel,
        "start_step",
        [(slab, F32), slab_slots, (slab, F32), small],
        weights,
        gram,
        start_block,
        start_slots,
        tiles,
        scalars=1,
    )
    applied_slots, theta_sum = exchange(parcel)
    theta, start_theta, residual, residual_slots, image, parcel = run(
        lambda *refs: first_kernel(root, *refs),
        "first_residual",
        [
            (square, F32),
            (square, F32),
            (slab, F32),
            slab_slots,
            (slab, F32),
            parcel_of(2 * columns),
        ],
        weights,
        theta_sum,
        block,
        applied,
        block_slots,
        applied_slots,
        tiles,
        scalars=1,
    )
    image_slots, grams = exchange(parcel)
    coeffs, next_theta, trial, last_grams = run(
        second_kernel,
        "second_step",
        [
            ((2 * columns, 2 * columns), F32),
            (square, F32),
            ((3 * columns, rows_dev), F32),
            ((2 * columns, 3 * columns), F32),
        ],
        weights,
        grams,
        theta,
        block,
        residual,
        applied,
        image,
        block_slots,
        residual_slots,
        applied_slots,
        image_slots,
        tiles,
        scalars=1,
        scratch=[pltpu.VMEM((2 * columns, columns), F32)],
    )
    carried, pieces = run(
        carry_kernel,
        "carry",
        [((4 * columns, 2 * columns), F32), ((rows_dev, 3 * columns), F32)],
        coeffs,
        grams,
        theta,
        trial,
        row_order,
    )

    def over(values, axis):
        return lax.all_to_all(values, axis, split_axis=0, concat_axis=0, tiled=True)

    row_parts = run(
        row_sum_kernel, "row_sum", [((groups, 3 * columns), F32)], over(last_grams, "node")
    )[0]
    gathered = over(
        run(
            gather_kernel, "gather", [((nodes, 6 * columns), F32)], over(row_parts, "grp"), pieces
        )[0],
        "node",
    )
    ritz, embedding = run(
        lambda *refs: last_step_kernel(root, *refs),
        "last_step",
        [(square, F32), (slab, F32)],
        gathered,
        carried,
        next_theta,
        scratch=[pltpu.VMEM((3 * columns, columns), F32)],
    )
    return (embedding, ritz, start_theta)


def solution(mesh):
    return jax.shard_map(
        local,
        mesh=mesh,
        in_specs=(
            P(None, BOTH),
            P(BOTH, None, None, None),
            P(BOTH, None),
            P(BOTH, None),
            P(BOTH),
            P(BOTH, None),
        ),
        out_specs=(P(None, BOTH), P(), P()),
        check_vma=False,
    )
```

```python
import jax
import jax.numpy as jnp
from jax import lax
from jax.experimental import pallas as pl
from jax.experimental.pallas import tpu as pltpu
from jax.sharding import PartitionSpec as P

REACH = 2
NSUB = 4
BLOCK = 8
RADIUS = 0.18
BOTH = ("grp", "node")
CORE_X = (1, 128, 256)
Y_Z = (2, 4, 8, 16, 32, 64)


def groups_over(bits):
    mask = sum(bits)
    groups = []
    for base in range(512):
        if base & mask:
            continue
        members = [base]
        for bit in bits:
            members = members + [member | bit for member in members]
        groups.append(members)
    return groups


def swap(values, bits):
    return lax.all_to_all(
        values, BOTH, split_axis=0, concat_axis=0, tiled=True, axis_index_groups=groups_over(bits)
    )


def run(kernel, name, results, *operands, scalars=0, scratch=()):
    smem = pl.BlockSpec(memory_space=pltpu.SMEM)
    vmem = pl.BlockSpec(memory_space=pltpu.VMEM)
    return pl.pallas_call(
        kernel,
        out_shape=[jax.ShapeDtypeStruct(shape, dtype) for shape, dtype in results],
        in_specs=[smem] * scalars + [vmem] * (len(operands) - scalars),
        out_specs=[vmem] * len(results),
        scratch_shapes=list(scratch),
        compiler_params=pltpu.CompilerParams(vmem_limit_bytes=32 << 20),
        name=name,
    )(*operands)


F32 = jnp.float32
BF16 = jnp.bfloat16


def tree_sum(parts):
    while len(parts) > 1:
        parts = [parts[i] + parts[i + 1] for i in range(0, len(parts), 2)]
    return parts[0]


def sum_kernel(first, parts_ref, out_ref):
    summed = tree_sum([parts_ref[i, first:] for i in range(parts_ref.shape[0])])
    for i in range(out_ref.shape[0]):
        out_ref[i] = summed


def sum_copies(parts, count, first=0):
    return run(
        lambda *refs: sum_kernel(first, *refs),
        "sum_copies",
        [((count, parts.shape[1] - first, parts.shape[2]), F32)],
        parts,
    )[0]


def row_sum_kernel(parts_ref, out_ref):
    summed = jnp.sum(parts_ref[...], axis=0, keepdims=True)
    out_ref[...] = jnp.broadcast_to(summed, out_ref.shape)


def gather_kernel(parts_ref, pieces_ref, out_ref):
    summed = tree_sum([parts_ref[i : i + 1] for i in range(parts_ref.shape[0])])
    rows, width = pieces_ref.shape
    out_ref[:, :width] = jnp.broadcast_to(summed, (rows, width))
    out_ref[:, width:] = pieces_ref[...]


def mm(left, right, contract):
    return lax.dot_general(
        left,
        right,
        ((contract[:1], contract[1:]), ((), ())),
        precision=lax.Precision.HIGHEST,
        preferred_element_type=jnp.float32,
    )


def nn(left, right):
    return mm(left, right, (1, 0))


def nt(left, right):
    return mm(left, right, (1, 1))


def tn(left, right):
    return mm(left, right, (0, 0))


def eye(order):
    row = lax.broadcasted_iota(jnp.int32, (order, order), 0)
    column = lax.broadcasted_iota(jnp.int32, (order, order), 1)
    return jnp.where(row == column, jnp.float32(1.0), jnp.float32(0.0))


def inverse_root(value):
    guess = lax.rsqrt(value)
    return guess * (1.5 - 0.5 * value * guess * guess)


def inverse_factor(matrix):
    order = matrix.shape[0]
    lanes = 2 * order
    both = jnp.concatenate([matrix, eye(order)], axis=1)
    bands = [both[8 * i : 8 * i + 8] for i in range(order // 8)]
    sublane = lax.broadcasted_iota(jnp.int32, (8, lanes), 0)
    done = [None] * len(bands)
    for first in range(0, order, BLOCK):
        band = first // 8
        base = first % 8
        last_of_band = base + BLOCK == 8
        live = range(band, len(bands))
        column = [
            [jnp.broadcast_to(bands[i][:, first + k : first + k + 1], (8, lanes)) for i in live]
            for k in range(BLOCK)
        ]
        row = [
            jnp.broadcast_to(bands[band][base + k : base + k + 1], (8, lanes)) for k in range(BLOCK)
        ]
        entry = [
            [
                jnp.broadcast_to(column[l][0][base + k : base + k + 1], (8, lanes))
                for l in range(k + 1)
            ]
            for k in range(BLOCK)
        ]
        inverse = []
        factor = [[None] * BLOCK for _ in range(BLOCK)]
        for l in range(BLOCK):
            inverse.append(1.0 / entry[l][l])
            for k in range(l + 1, BLOCK):
                factor[k][l] = entry[k][l] * inverse[l]
                for m in range(l + 1, k + 1):
                    entry[k][m] = entry[k][m] - factor[k][l] * entry[m][l]
        start = 1 if last_of_band else 0
        for k in range(BLOCK):
            for l in range(k):
                row[k] = row[k] - factor[k][l] * row[l]
                for i in range(start, len(live)):
                    column[k][i] = column[k][i] - factor[k][l] * column[l][i]
        for k in range(BLOCK):
            scaled = row[k] * inverse_root(entry[k][k])
            if done[band] is None:
                done[band] = scaled
            else:
                done[band] = jnp.where(sublane == base + k, scaled, done[band])
            left = row[k] * inverse[k]
            for i in range(start, len(live)):
                bands[band + i] = bands[band + i] - column[k][i] * left
    return jnp.concatenate(done, axis=0)[:, order:]


def half_sum(matrix):
    return 0.5 * (matrix + matrix.T)


def orthonormal(image):
    return nt(image, inverse_factor(tn(image, image)))


def project(linv, gram, basis_ref):
    order = linv.shape[0]
    columns = basis_ref.shape[1]
    projected = half_sum(nt(nn(linv, gram), linv))
    scale = jnp.sqrt(jnp.sum(projected * projected, keepdims=True) + 1e-06)
    unit = projected / scale
    identity = eye(order)
    filtered = unit + 1.25 * identity
    square = nn(filtered, filtered)
    fourth = nn(square, square)
    eighth = nn(fourth, fourth)
    unit2 = square - 2.5 * unit - 1.5625 * identity
    unit4 = nn(unit2, unit2)
    bound = jnp.sum(unit4 * unit4)
    basis_ref[...] = orthonormal(nn(eighth, eighth[:, :columns]))

    @pl.when(jnp.logical_not(bound < RADIUS**8))
    def _():
        basis_ref[...] = identity[:, :columns]

        def sweep(_, carry):
            basis_ref[...] = orthonormal(nn(fourth, basis_ref[...]))
            return carry

        lax.fori_loop(0, NSUB, sweep, 0)

    basis = basis_ref[...]
    coeffs = tn(linv, basis)
    theta = half_sum(tn(basis, nn(projected, basis)))
    return coeffs, theta


def load_packed(ref):
    width = ref.shape[1] // 2
    return jnp.concatenate([ref[:, :width], ref[:, width:]], axis=0)


def store_parcel(ref, value, partial):
    members, rows = ref.shape[0], value.shape[0]
    share = partial.shape[0] // members
    for i in range(members):
        ref[i, :rows] = value
        ref[i, rows:] = partial[share * i : share * (i + 1)]


def pack(matrix):
    half = matrix.shape[0] // 2
    return jnp.concatenate([matrix[:half], matrix[half:]], axis=1)


def gram_kernel(start_ref, parcel_ref):
    start = start_ref[...]
    store_parcel(parcel_ref, start, pack(nt(start, start)))


def half_kernel(core_ref, own_ref, half_ref):
    count, rows = half_ref.shape[:2]
    for i in range(count):
        half_ref[i] = own_ref[core_ref[0] * count + i, :rows]


def pick_kernel(index_ref, own_ref, mine_ref, other_ref, slots_ref):
    count = own_ref.shape[0]
    for slot in range(slots_ref.shape[0]):
        chosen = index_ref[slot]
        for side, ref in enumerate((mine_ref, own_ref, other_ref)):

            @pl.when(chosen // count == side)
            def _(ref=ref, slot=slot, chosen=chosen):
                slots_ref[slot] = ref[chosen % count, : slots_ref.shape[1]]


def multiply_tiles(weight_ref, tiles_ref, slot_values):
    acc = None
    for slot in range(tiles_ref.shape[0]):
        product = lax.dot_general(
            slot_values(slot).astype(BF16),
            tiles_ref[slot],
            (((1,), (1,)), ((), ())),
            preferred_element_type=F32,
        )
        product = weight_ref[slot] * product
        acc = product if acc is None else acc + product
    return acc


def start_kernel(weight_ref, gram_ref, start_ref, slots_ref, tiles_ref, block_ref, block_slots_ref, applied_ref, parcel_ref):
    inverse = inverse_factor(load_packed(gram_ref))
    block = nn(inverse, start_ref[...])
    block_ref[...] = block

    def values(slot):
        there = nn(inverse, slots_ref[slot])
        block_slots_ref[slot] = there
        return there

    applied = multiply_tiles(weight_ref, tiles_ref, values)
    applied_ref[...] = applied
    store_parcel(parcel_ref, applied, pack(nt(block, applied)))


def first_kernel(root, weight_ref, sum_ref, block_ref, applied_ref, block_slots_ref, applied_slots_ref, tiles_ref, theta_ref, start_theta_ref, residual_ref, residual_slots_ref, image_ref, parcel_ref, overlap_ref):
    product = load_packed(sum_ref)
    theta = half_sum(product)
    overlap_ref[...] = product - theta
    theta_ref[...] = theta
    start_theta_ref[...] = root * theta
    block = block_ref[...]
    applied = applied_ref[...]
    residual = applied - nn(theta, block)
    residual_ref[...] = residual

    def values(slot):
        there = applied_slots_ref[slot] - nn(theta, block_slots_ref[slot])
        residual_slots_ref[slot] = there
        return there

    image = multiply_tiles(weight_ref, tiles_ref, values)
    image_ref[...] = image
    cross = 0.5 * (nt(block, image) + nt(applied, residual))
    own = nt(residual, image)
    order = cross.shape[0]
    row = lax.broadcasted_iota(jnp.int32, (order, order), 0)
    column = lax.broadcasted_iota(jnp.int32, (order, order), 1)
    both = jnp.where(row >= column, nt(residual, residual), half_sum(own))
    diagonal = jnp.sum(jnp.where(row == column, own, F32(0.0)), axis=0, keepdims=True)
    partial = jnp.concatenate([cross, both], axis=1)
    tail = jnp.concatenate([diagonal, jnp.zeros_like(diagonal)], axis=1)
    members = parcel_ref.shape[0]
    share = order // members
    for i in range(members):
        parcel_ref[i, :order] = image
        parcel_ref[i, order : order + share] = partial[share * i : share * (i + 1)]
        parcel_ref[i, order + share :] = tail


def assemble_first(gathered_ref, theta):
    members = gathered_ref.shape[0]
    columns = theta.shape[0]
    share = columns // members
    grams = jnp.concatenate([gathered_ref[i, :share] for i in range(members)], axis=0)
    diagonal = gathered_ref[0, share:, :columns]
    cross = grams[:, :columns]
    both = grams[:, columns:]
    turned = both.T
    row = lax.broadcasted_iota(jnp.int32, (columns, columns), 0)
    column = lax.broadcasted_iota(jnp.int32, (columns, columns), 1)
    basis = jnp.where(row >= column, both, turned)
    own = jnp.where(row < column, both, jnp.where(row > column, turned, diagonal))
    gram = jnp.concatenate(
        [jnp.concatenate([theta, cross], axis=1), jnp.concatenate([cross.T, own], axis=1)], axis=0
    )
    return basis, gram


def second_kernel(weight_ref, grams_ref, overlap_ref, theta_ref, block_ref, residual_ref, applied_ref, image_ref, block_slots_ref, residual_slots_ref, applied_slots_ref, image_slots_ref, tiles_ref, coeffs_ref, theta_out_ref, trial_ref, grams_out_ref, basis_ref):
    columns = theta_ref.shape[0]
    width = block_ref.shape[1]
    overlap = overlap_ref[...]
    own, gram = assemble_first(grams_ref, theta_ref[...])
    factor = inverse_factor(own - tn(overlap, overlap))
    linv = jnp.concatenate(
        [
            jnp.concatenate([eye(columns), jnp.zeros((columns, columns), F32)], axis=1),
            jnp.concatenate([-nt(factor, overlap), factor], axis=1),
        ],
        axis=0,
    )
    coeffs, theta = project(linv, gram, basis_ref)
    theta_out_ref[...] = theta
    lower = jnp.concatenate([jnp.zeros((columns, columns), F32), coeffs[columns:]], axis=0)
    both = jnp.concatenate([coeffs, lower], axis=1)
    coeffs_ref[...] = both
    mix = jnp.concatenate([coeffs, -nn(coeffs, theta)], axis=0).T

    def values(slot):
        parts = (applied_slots_ref, image_slots_ref, block_slots_ref, residual_slots_ref)
        return nn(mix, jnp.concatenate([ref[slot] for ref in parts], axis=0))

    image = multiply_tiles(weight_ref, tiles_ref, values)
    block, applied = block_ref[...], applied_ref[...]
    previous, previous_image = residual_ref[...], image_ref[...]
    residual = nn(mix, jnp.concatenate([applied, previous_image, block, previous], axis=0))
    old_trial = jnp.concatenate([block, previous], axis=0)
    old_applied = jnp.concatenate([applied, previous_image], axis=0)
    fresh = tn(both, jnp.concatenate([old_trial, old_applied], axis=1))
    trial = jnp.concatenate([fresh[:columns, :width], residual, fresh[columns:, :width]], axis=0)
    trial_ref[...] = trial
    applied_trial = jnp.concatenate([fresh[:columns, width:], image, fresh[columns:, width:]], axis=0)
    cross = 0.5 * (nt(image, trial) + nt(residual, applied_trial))
    grams_out_ref[...] = jnp.concatenate([nt(residual, trial), cross], axis=0)


def carry_kernel(coeffs_ref, grams_ref, overlap_ref, theta_ref, trial_ref, order_ref, carried_ref, pieces_ref):
    columns = theta_ref.shape[0]
    coeffs = coeffs_ref[...]
    overlap = overlap_ref[...]
    own, gram = assemble_first(grams_ref, theta_ref[...])
    basis = jnp.concatenate(
        [
            jnp.concatenate([eye(columns), overlap], axis=1),
            jnp.concatenate([overlap.T, own], axis=1),
        ],
        axis=0,
    )
    carried_ref[...] = jnp.concatenate(
        [tn(coeffs, nn(basis, coeffs)), tn(coeffs, nn(gram, coeffs))], axis=0
    )
    width = trial_ref.shape[1]
    place = lax.broadcasted_iota(jnp.int32, (width, width), 0)
    pick = jnp.where(place == order_ref[...], F32(1.0), F32(0.0))
    pieces_ref[...] = mm(pick, trial_ref[...], (0, 1))


def last_step_kernel(root, gathered_ref, carried_ref, theta_ref, theta_out_ref, embedding_ref, basis_ref):
    columns = theta_ref.shape[0]
    width = gathered_ref.shape[1] // 2
    grams = gathered_ref[:, :width].T
    arrived = gathered_ref[:, width:]
    carried = carried_ref[...]
    wide = 2 * columns
    overlap = jnp.concatenate([grams[:columns, :columns], carried[:columns, columns:wide]], axis=1)
    mixed = grams[wide:, :columns]
    spread = tn(overlap, overlap)
    first = grams[columns:wide, :columns] - spread[:columns, :columns]
    corner = mixed.T - spread[:columns, columns:]
    second = carried[columns:wide, columns:wide] - spread[columns:, columns:]
    factor = inverse_factor(first)
    middle = nn(factor, corner)
    other = inverse_factor(second - tn(middle, middle))
    zero = jnp.zeros((columns, columns), F32)
    lower = jnp.concatenate(
        [
            jnp.concatenate([factor, zero], axis=1),
            jnp.concatenate([-nn(other, tn(middle, factor)), other], axis=1),
        ],
        axis=0,
    )
    linv = jnp.concatenate(
        [
            jnp.concatenate([eye(columns), zero, zero], axis=1),
            jnp.concatenate([-nt(lower, overlap), lower], axis=1),
        ],
        axis=0,
    )
    cross = grams[:columns, columns:]
    own = half_sum(grams[columns:wide, columns:])
    momentum_cross = grams[wide:, columns:]
    block_momentum = carried[wide : wide + columns, columns:wide]
    momentum = half_sum(carried[wide + columns :, columns:wide])
    gram = jnp.concatenate(
        [
            jnp.concatenate([theta_ref[...], cross, block_momentum], axis=1),
            jnp.concatenate([cross.T, own, momentum_cross.T], axis=1),
            jnp.concatenate([block_momentum.T, momentum_cross, momentum], axis=1),
        ],
        axis=0,
    )
    coeffs, theta = project(linv, gram, basis_ref)
    theta_out_ref[...] = theta
    embedding_ref[...] = root * mm(coeffs, arrived, (0, 1))


def local(start_block, weight_tiles, tile_scales, neighbour_ids, live_counts, row_order):
    columns = start_block.shape[0]
    rows_dev = start_block.shape[1]
    groups = lax.axis_size("grp")
    nodes = lax.axis_size("node")
    here = lax.axis_index("node")
    ids = neighbour_ids[0]
    slots = ids.shape[0]
    group_index = ids // nodes
    node_index = ids % nodes
    chips = nodes // 2
    chip_offset = (node_index // 2 - here // 2 + 1 + chips) % chips
    core = here % 2
    member = node_index % 2 + 2 * group_index
    half = 2 * groups // 2
    fetched = jnp.where(member // half == core, 0, 4 * groups) + chip_offset // 2 * half + member % half
    index = jnp.where(chip_offset == 1, 2 * groups + member, fetched)
    index = jnp.clip(index, 0, 6 * groups - 1).astype(jnp.int32)
    slot_iota = jnp.arange(slots, dtype=jnp.int32)
    weights = jnp.where(slot_iota < live_counts[0], tile_scales[0], F32(0.0))
    tiles = weight_tiles[0]
    to_next = [(source, (source + 2) % nodes) for source in range(nodes)]
    to_last = [(source, (source - 2) % nodes) for source in range(nodes)]
    to_pair = [(source, source ^ 1) for source in range(nodes)]
    root = float(rows_dev * groups * nodes) ** 0.5
    slab = (columns, rows_dev)
    square = (columns, columns)
    packed = (columns // 2, 2 * columns)
    slab_slots = ((slots,) + slab, F32)

    def exchange(parcel):
        received = swap(parcel, CORE_X)
        partial = sum_copies(received, 2 ** len(Y_Z), columns)
        shared = swap(partial, Y_Z)
        later, _ = lax.optimization_barrier((received, partial))
        part = run(half_kernel, "half", [((half,) + slab, F32)], core[None], later, scalars=1)[0]
        mine = jnp.concatenate(
            [lax.ppermute(part, "node", to_next), lax.ppermute(part, "node", to_last)], axis=0
        )
        other = lax.ppermute(mine, "node", to_pair)
        rows = run(pick_kernel, "pick_slots", [slab_slots], index, received, mine, other, scalars=1)[0]
        summed = swap(sum_copies(shared, 2 ** len(CORE_X)), CORE_X)
        return rows, summed

    def parcel_of(share):
        return ((2 * groups, columns + share, rows_dev), F32)

    small = parcel_of(columns // (4 * groups))
    start_slots, gram = exchange(run(gram_kernel, "start_gram", [small], start_block)[0])
    block, block_slots, applied, parcel = run(
        start_kernel,
        "start_step",
        [(slab, F32), slab_slots, (slab, F32), small],
        weights,
        gram.reshape(packed),
        start_block,
        start_slots,
        tiles,
        scalars=1,
    )
    applied_slots, theta_sum = exchange(parcel)
    theta, start_theta, residual, residual_slots, image, parcel, overlap = run(
        lambda *refs: first_kernel(root, *refs),
        "first_residual",
        [
            (square, F32),
            (square, F32),
            (slab, F32),
            slab_slots,
            (slab, F32),
            parcel_of(columns // (2 * groups) + 1),
            (square, F32),
        ],
        weights,
        theta_sum.reshape(packed),
        block,
        applied,
        block_slots,
        applied_slots,
        tiles,
        scalars=1,
    )
    image_slots, grams = exchange(parcel)
    coeffs, next_theta, trial, last_grams = run(
        second_kernel,
        "second_step",
        [
            ((2 * columns, 2 * columns), F32),
            (square, F32),
            ((3 * columns, rows_dev), F32),
            ((2 * columns, 3 * columns), F32),
        ],
        weights,
        grams,
        overlap,
        theta,
        block,
        residual,
        applied,
        image,
        block_slots,
        residual_slots,
        applied_slots,
        image_slots,
        tiles,
        scalars=1,
        scratch=[pltpu.VMEM((2 * columns, columns), F32)],
    )
    carried, pieces = run(
        carry_kernel,
        "carry",
        [((4 * columns, 2 * columns), F32), ((rows_dev, 3 * columns), F32)],
        coeffs,
        grams,
        overlap,
        theta,
        trial,
        row_order,
    )

    def over(values, axis):
        return lax.all_to_all(values, axis, split_axis=0, concat_axis=0, tiled=True)

    row_parts = run(
        row_sum_kernel, "row_sum", [((groups, 3 * columns), F32)], over(last_grams, "node")
    )[0]
    gathered = over(
        run(
            gather_kernel, "gather", [((nodes, 6 * columns), F32)], over(row_parts, "grp"), pieces
        )[0],
        "node",
    )
    ritz, embedding = run(
        lambda *refs: last_step_kernel(root, *refs),
        "last_step",
        [(square, F32), (slab, F32)],
        gathered,
        carried,
        next_theta,
        scratch=[pltpu.VMEM((3 * columns, columns), F32)],
    )
    return (embedding, ritz, start_theta)


def solution(mesh):
    return jax.shard_map(
        local,
        mesh=mesh,
        in_specs=(
            P(None, BOTH),
            P(BOTH, None, None, None),
            P(BOTH, None),
            P(BOTH, None),
            P(BOTH),
            P(BOTH, None),
        ),
        out_specs=(P(None, BOTH), P(), P()),
        check_vma=False,
    )
```

```python
import jax
import jax.numpy as jnp
from jax import lax
from jax.experimental import pallas as pl
from jax.experimental.pallas import tpu as pltpu
from jax.sharding import PartitionSpec as P

REACH = 2
NSUB = 4
BLOCK = 8
RADIUS = 0.18
BOTH = ("grp", "node")
CORE_X = (1, 128, 256)
Y_Z = (2, 4, 8, 16, 32, 64)


def groups_over(bits):
    mask = sum(bits)
    groups = []
    for base in range(512):
        if base & mask:
            continue
        members = [base]
        for bit in bits:
            members = members + [member | bit for member in members]
        groups.append(members)
    return groups


def swap(values, bits):
    return lax.all_to_all(
        values, BOTH, split_axis=0, concat_axis=0, tiled=True, axis_index_groups=groups_over(bits)
    )


def run(kernel, name, results, *operands, scalars=0, scratch=()):
    smem = pl.BlockSpec(memory_space=pltpu.SMEM)
    vmem = pl.BlockSpec(memory_space=pltpu.VMEM)
    return pl.pallas_call(
        kernel,
        out_shape=[jax.ShapeDtypeStruct(shape, dtype) for shape, dtype in results],
        in_specs=[smem] * scalars + [vmem] * (len(operands) - scalars),
        out_specs=[vmem] * len(results),
        scratch_shapes=list(scratch),
        compiler_params=pltpu.CompilerParams(vmem_limit_bytes=32 << 20),
        name=name,
    )(*operands)


F32 = jnp.float32
BF16 = jnp.bfloat16


def tree_sum(parts):
    while len(parts) > 1:
        parts = [parts[i] + parts[i + 1] for i in range(0, len(parts), 2)]
    return parts[0]


def sum_kernel(first, parts_ref, out_ref):
    summed = tree_sum([parts_ref[i, first:] for i in range(parts_ref.shape[0])])
    for i in range(out_ref.shape[0]):
        out_ref[i] = summed


def sum_copies(parts, count, first=0):
    return run(
        lambda *refs: sum_kernel(first, *refs),
        "sum_copies",
        [((count, parts.shape[1] - first, parts.shape[2]), F32)],
        parts,
    )[0]


def row_sum_kernel(parts_ref, out_ref):
    summed = jnp.sum(parts_ref[...], axis=0, keepdims=True)
    out_ref[...] = jnp.broadcast_to(summed, out_ref.shape)


def gather_kernel(parts_ref, pieces_ref, out_ref):
    summed = tree_sum([parts_ref[i : i + 1] for i in range(parts_ref.shape[0])])
    rows, width = pieces_ref.shape
    out_ref[:, :width] = jnp.broadcast_to(summed, (rows, width))
    out_ref[:, width:] = pieces_ref[...]


def mm(left, right, contract):
    return lax.dot_general(
        left,
        right,
        ((contract[:1], contract[1:]), ((), ())),
        precision=lax.Precision.HIGHEST,
        preferred_element_type=jnp.float32,
    )


def nn(left, right):
    return mm(left, right, (1, 0))


def nt(left, right):
    return mm(left, right, (1, 1))


def tn(left, right):
    return mm(left, right, (0, 0))


def eye(order):
    row = lax.broadcasted_iota(jnp.int32, (order, order), 0)
    column = lax.broadcasted_iota(jnp.int32, (order, order), 1)
    return jnp.where(row == column, jnp.float32(1.0), jnp.float32(0.0))


def inverse_root(value):
    guess = lax.rsqrt(value)
    return guess * (1.5 - 0.5 * value * guess * guess)


def inverse_factor(matrix):
    order = matrix.shape[0]
    lanes = 2 * order
    both = jnp.concatenate([matrix, eye(order)], axis=1)
    bands = [both[8 * i : 8 * i + 8] for i in range(order // 8)]
    sublane = lax.broadcasted_iota(jnp.int32, (8, lanes), 0)
    done = [None] * len(bands)
    for first in range(0, order, BLOCK):
        band = first // 8
        base = first % 8
        last_of_band = base + BLOCK == 8
        live = range(band, len(bands))
        column = [
            [jnp.broadcast_to(bands[i][:, first + k : first + k + 1], (8, lanes)) for i in live]
            for k in range(BLOCK)
        ]
        row = [
            jnp.broadcast_to(bands[band][base + k : base + k + 1], (8, lanes)) for k in range(BLOCK)
        ]
        entry = [
            [
                jnp.broadcast_to(column[l][0][base + k : base + k + 1], (8, lanes))
                for l in range(k + 1)
            ]
            for k in range(BLOCK)
        ]
        inverse = []
        factor = [[None] * BLOCK for _ in range(BLOCK)]
        for l in range(BLOCK):
            inverse.append(1.0 / entry[l][l])
            for k in range(l + 1, BLOCK):
                factor[k][l] = entry[k][l] * inverse[l]
                for m in range(l + 1, k + 1):
                    entry[k][m] = entry[k][m] - factor[k][l] * entry[m][l]
        start = 1 if last_of_band else 0
        for k in range(BLOCK):
            for l in range(k):
                row[k] = row[k] - factor[k][l] * row[l]
                for i in range(start, len(live)):
                    column[k][i] = column[k][i] - factor[k][l] * column[l][i]
        for k in range(BLOCK):
            scaled = row[k] * inverse_root(entry[k][k])
            if done[band] is None:
                done[band] = scaled
            else:
                done[band] = jnp.where(sublane == base + k, scaled, done[band])
            left = row[k] * inverse[k]
            for i in range(start, len(live)):
                bands[band + i] = bands[band + i] - column[k][i] * left
    return jnp.concatenate(done, axis=0)[:, order:]


def half_sum(matrix):
    return 0.5 * (matrix + matrix.T)


def orthonormal(image):
    return nt(image, inverse_factor(tn(image, image)))


def project(linv, gram, basis_ref):
    order = linv.shape[0]
    columns = basis_ref.shape[1]
    projected = half_sum(nt(nn(linv, gram), linv))
    scale = jnp.sqrt(jnp.sum(projected * projected, keepdims=True) + 1e-06)
    unit = projected / scale
    identity = eye(order)
    filtered = unit + 1.25 * identity
    square = nn(filtered, filtered)
    fourth = nn(square, square)
    eighth = nn(fourth, fourth)
    unit2 = square - 2.5 * unit - 1.5625 * identity
    unit4 = nn(unit2, unit2)
    bound = jnp.sum(unit4 * unit4)
    basis_ref[...] = orthonormal(nn(eighth, eighth[:, :columns]))

    @pl.when(jnp.logical_not(bound < RADIUS**8))
    def _():
        basis_ref[...] = identity[:, :columns]

        def sweep(_, carry):
            basis_ref[...] = orthonormal(nn(fourth, basis_ref[...]))
            return carry

        lax.fori_loop(0, NSUB, sweep, 0)

    basis = basis_ref[...]
    coeffs = tn(linv, basis)
    theta = half_sum(tn(basis, nn(projected, basis)))
    return coeffs, theta


def load_packed(ref):
    width = ref.shape[1] // 2
    return jnp.concatenate([ref[:, :width], ref[:, width:]], axis=0)


def store_parcel(ref, value, partial):
    members, rows = ref.shape[0], value.shape[0]
    share = partial.shape[0] // members
    for i in range(members):
        ref[i, :rows] = value
        ref[i, rows:] = partial[share * i : share * (i + 1)]


def pack(matrix):
    half = matrix.shape[0] // 2
    return jnp.concatenate([matrix[:half], matrix[half:]], axis=1)


def gram_kernel(start_ref, parcel_ref):
    start = start_ref[...]
    store_parcel(parcel_ref, start, pack(nt(start, start)))


def neighbour_rows(index_ref, own_ref, up_ref, down_ref, rows):
    count = own_ref.shape[0]

    def at(slot):
        side = lax.div(index_ref[slot], count)
        member = lax.rem(index_ref[slot], count)
        outer = jnp.where(side == 0, down_ref[member, :rows], up_ref[member, :rows])
        return jnp.where(side == 1, own_ref[member, :rows], outer)

    return at


def multiply_tiles(weight_ref, tiles_ref, slot_values):
    acc = None
    for slot in range(tiles_ref.shape[0]):
        product = lax.dot_general(
            slot_values(slot).astype(BF16),
            tiles_ref[slot],
            (((1,), (1,)), ((), ())),
            preferred_element_type=F32,
        )
        product = weight_ref[slot] * product
        acc = product if acc is None else acc + product
    return acc


def start_kernel(weight_ref, index_ref, own_ref, up_ref, down_ref, gram_ref, start_ref, tiles_ref, block_ref, block_slots_ref, applied_ref, parcel_ref):
    inverse = inverse_factor(load_packed(gram_ref))
    block = nn(inverse, start_ref[...])
    block_ref[...] = block

    rows_at = neighbour_rows(index_ref, own_ref, up_ref, down_ref, block.shape[0])

    def values(slot):
        there = nn(inverse, rows_at(slot))
        block_slots_ref[slot] = there
        return there

    applied = multiply_tiles(weight_ref, tiles_ref, values)
    applied_ref[...] = applied
    store_parcel(parcel_ref, applied, pack(nt(block, applied)))


def first_kernel(root, weight_ref, index_ref, own_ref, up_ref, down_ref, sum_ref, block_ref, applied_ref, block_slots_ref, tiles_ref, theta_ref, start_theta_ref, residual_ref, residual_slots_ref, image_ref, parcel_ref, overlap_ref, applied_slots_ref):
    product = load_packed(sum_ref)
    theta = half_sum(product)
    overlap_ref[...] = product - theta
    theta_ref[...] = theta
    start_theta_ref[...] = root * theta
    block = block_ref[...]
    applied = applied_ref[...]
    residual = applied - nn(theta, block)
    residual_ref[...] = residual

    rows_at = neighbour_rows(index_ref, own_ref, up_ref, down_ref, block.shape[0])

    def values(slot):
        applied_there = rows_at(slot)
        applied_slots_ref[slot] = applied_there
        there = applied_there - nn(theta, block_slots_ref[slot])
        residual_slots_ref[slot] = there
        return there

    image = multiply_tiles(weight_ref, tiles_ref, values)
    image_ref[...] = image
    cross = 0.5 * (nt(block, image) + nt(applied, residual))
    own = nt(residual, image)
    order = cross.shape[0]
    row = lax.broadcasted_iota(jnp.int32, (order, order), 0)
    column = lax.broadcasted_iota(jnp.int32, (order, order), 1)
    both = jnp.where(row >= column, nt(residual, residual), half_sum(own))
    diagonal = jnp.sum(jnp.where(row == column, own, F32(0.0)), axis=0, keepdims=True)
    partial = jnp.concatenate([cross, both], axis=1)
    tail = jnp.concatenate([diagonal, jnp.zeros_like(diagonal)], axis=1)
    members = parcel_ref.shape[0]
    share = order // members
    for i in range(members):
        parcel_ref[i, :order] = image
        parcel_ref[i, order : order + share] = partial[share * i : share * (i + 1)]
        parcel_ref[i, order + share :] = tail


def assemble_first(gathered_ref, theta):
    members = gathered_ref.shape[0]
    columns = theta.shape[0]
    share = columns // members
    grams = jnp.concatenate([gathered_ref[i, :share] for i in range(members)], axis=0)
    diagonal = gathered_ref[0, share:, :columns]
    cross = grams[:, :columns]
    both = grams[:, columns:]
    turned = both.T
    row = lax.broadcasted_iota(jnp.int32, (columns, columns), 0)
    column = lax.broadcasted_iota(jnp.int32, (columns, columns), 1)
    basis = jnp.where(row >= column, both, turned)
    own = jnp.where(row < column, both, jnp.where(row > column, turned, diagonal))
    gram = jnp.concatenate(
        [jnp.concatenate([theta, cross], axis=1), jnp.concatenate([cross.T, own], axis=1)], axis=0
    )
    return basis, gram


def second_kernel(weight_ref, index_ref, own_ref, up_ref, down_ref, grams_ref, overlap_ref, theta_ref, block_ref, residual_ref, applied_ref, image_ref, block_slots_ref, residual_slots_ref, applied_slots_ref, tiles_ref, coeffs_ref, theta_out_ref, trial_ref, grams_out_ref, basis_ref):
    columns = theta_ref.shape[0]
    width = block_ref.shape[1]
    overlap = overlap_ref[...]
    own, gram = assemble_first(grams_ref, theta_ref[...])
    factor = inverse_factor(own - tn(overlap, overlap))
    linv = jnp.concatenate(
        [
            jnp.concatenate([eye(columns), jnp.zeros((columns, columns), F32)], axis=1),
            jnp.concatenate([-nt(factor, overlap), factor], axis=1),
        ],
        axis=0,
    )
    coeffs, theta = project(linv, gram, basis_ref)
    theta_out_ref[...] = theta
    lower = jnp.concatenate([jnp.zeros((columns, columns), F32), coeffs[columns:]], axis=0)
    both = jnp.concatenate([coeffs, lower], axis=1)
    coeffs_ref[...] = both
    mix = jnp.concatenate([coeffs, -nn(coeffs, theta)], axis=0).T

    image_at = neighbour_rows(index_ref, own_ref, up_ref, down_ref, columns)

    def values(slot):
        parts = [
            applied_slots_ref[slot],
            image_at(slot),
            block_slots_ref[slot],
            residual_slots_ref[slot],
        ]
        return nn(mix, jnp.concatenate(parts, axis=0))

    image = multiply_tiles(weight_ref, tiles_ref, values)
    block, applied = block_ref[...], applied_ref[...]
    previous, previous_image = residual_ref[...], image_ref[...]
    residual = nn(mix, jnp.concatenate([applied, previous_image, block, previous], axis=0))
    old_trial = jnp.concatenate([block, previous], axis=0)
    old_applied = jnp.concatenate([applied, previous_image], axis=0)
    fresh = tn(both, jnp.concatenate([old_trial, old_applied], axis=1))
    trial = jnp.concatenate([fresh[:columns, :width], residual, fresh[columns:, :width]], axis=0)
    trial_ref[...] = trial
    applied_trial = jnp.concatenate([fresh[:columns, width:], image, fresh[columns:, width:]], axis=0)
    cross = 0.5 * (nt(image, trial) + nt(residual, applied_trial))
    grams_out_ref[...] = jnp.concatenate([nt(residual, trial), cross], axis=0)


def carry_kernel(coeffs_ref, grams_ref, overlap_ref, theta_ref, trial_ref, order_ref, carried_ref, pieces_ref):
    columns = theta_ref.shape[0]
    coeffs = coeffs_ref[...]
    overlap = overlap_ref[...]
    own, gram = assemble_first(grams_ref, theta_ref[...])
    basis = jnp.concatenate(
        [
            jnp.concatenate([eye(columns), overlap], axis=1),
            jnp.concatenate([overlap.T, own], axis=1),
        ],
        axis=0,
    )
    carried_ref[...] = jnp.concatenate(
        [tn(coeffs, nn(basis, coeffs)), tn(coeffs, nn(gram, coeffs))], axis=0
    )
    width = trial_ref.shape[1]
    place = lax.broadcasted_iota(jnp.int32, (width, width), 0)
    pick = jnp.where(place == order_ref[...], F32(1.0), F32(0.0))
    pieces_ref[...] = mm(pick, trial_ref[...], (0, 1))


def last_step_kernel(root, gathered_ref, carried_ref, theta_ref, theta_out_ref, embedding_ref, basis_ref):
    columns = theta_ref.shape[0]
    width = gathered_ref.shape[1] // 2
    grams = gathered_ref[:, :width].T
    arrived = gathered_ref[:, width:]
    carried = carried_ref[...]
    wide = 2 * columns
    overlap = jnp.concatenate([grams[:columns, :columns], carried[:columns, columns:wide]], axis=1)
    mixed = grams[wide:, :columns]
    spread = tn(overlap, overlap)
    first = grams[columns:wide, :columns] - spread[:columns, :columns]
    corner = mixed.T - spread[:columns, columns:]
    second = carried[columns:wide, columns:wide] - spread[columns:, columns:]
    factor = inverse_factor(first)
    middle = nn(factor, corner)
    other = inverse_factor(second - tn(middle, middle))
    zero = jnp.zeros((columns, columns), F32)
    lower = jnp.concatenate(
        [
            jnp.concatenate([factor, zero], axis=1),
            jnp.concatenate([-nn(other, tn(middle, factor)), other], axis=1),
        ],
        axis=0,
    )
    linv = jnp.concatenate(
        [
            jnp.concatenate([eye(columns), zero, zero], axis=1),
            jnp.concatenate([-nt(lower, overlap), lower], axis=1),
        ],
        axis=0,
    )
    cross = grams[:columns, columns:]
    own = half_sum(grams[columns:wide, columns:])
    momentum_cross = grams[wide:, columns:]
    block_momentum = carried[wide : wide + columns, columns:wide]
    momentum = half_sum(carried[wide + columns :, columns:wide])
    gram = jnp.concatenate(
        [
            jnp.concatenate([theta_ref[...], cross, block_momentum], axis=1),
            jnp.concatenate([cross.T, own, momentum_cross.T], axis=1),
            jnp.concatenate([block_momentum.T, momentum_cross, momentum], axis=1),
        ],
        axis=0,
    )
    coeffs, theta = project(linv, gram, basis_ref)
    theta_out_ref[...] = theta
    embedding_ref[...] = root * mm(coeffs, arrived, (0, 1))


def local(start_block, weight_tiles, tile_scales, neighbour_ids, live_counts, row_order):
    columns = start_block.shape[0]
    rows_dev = start_block.shape[1]
    groups = lax.axis_size("grp")
    nodes = lax.axis_size("node")
    here = lax.axis_index("node")
    ids = neighbour_ids[0]
    slots = ids.shape[0]
    group_index = ids // nodes
    node_index = ids % nodes
    chips = nodes // 2
    chip_offset = (node_index // 2 - here // 2 + 1 + chips) % chips
    index = jnp.clip(chip_offset * 8 + node_index % 2 + 2 * group_index, 0, 23).astype(jnp.int32)
    slot_iota = jnp.arange(slots, dtype=jnp.int32)
    weights = jnp.where(slot_iota < live_counts[0], tile_scales[0], F32(0.0))
    tiles = weight_tiles[0]
    to_next = [(source, (source + 2) % nodes) for source in range(nodes)]
    to_last = [(source, (source - 2) % nodes) for source in range(nodes)]
    root = float(rows_dev * groups * nodes) ** 0.5
    slab = (columns, rows_dev)
    square = (columns, columns)
    packed = (columns // 2, 2 * columns)
    slab_slots = ((slots,) + slab, F32)

    def exchange(parcel):
        received = swap(parcel, CORE_X)
        partial = sum_copies(received, 2 ** len(Y_Z), columns)
        shared = swap(partial, Y_Z)
        later, _ = lax.optimization_barrier((received, partial))
        down = lax.ppermute(later, "node", to_next)
        up = lax.ppermute(later, "node", to_last)
        summed = swap(sum_copies(shared, 2 ** len(CORE_X)), CORE_X)
        return (received, up, down), summed

    def parcel_of(share):
        return ((2 * groups, columns + share, rows_dev), F32)

    small = parcel_of(columns // (4 * groups))
    start_rows, gram = exchange(run(gram_kernel, "start_gram", [small], start_block)[0])
    block, block_slots, applied, parcel = run(
        start_kernel,
        "start_step",
        [(slab, F32), slab_slots, (slab, F32), small],
        weights,
        index,
        *start_rows,
        gram.reshape(packed),
        start_block,
        tiles,
        scalars=2,
    )
    applied_rows, theta_sum = exchange(parcel)
    theta, start_theta, residual, residual_slots, image, parcel, overlap, applied_slots = run(
        lambda *refs: first_kernel(root, *refs),
        "first_residual",
        [
            (square, F32),
            (square, F32),
            (slab, F32),
            slab_slots,
            (slab, F32),
            parcel_of(columns // (2 * groups) + 1),
            (square, F32),
            slab_slots,
        ],
        weights,
        index,
        *applied_rows,
        theta_sum.reshape(packed),
        block,
        applied,
        block_slots,
        tiles,
        scalars=2,
    )
    image_rows, grams = exchange(parcel)
    coeffs, next_theta, trial, last_grams = run(
        second_kernel,
        "second_step",
        [
            ((2 * columns, 2 * columns), F32),
            (square, F32),
            ((3 * columns, rows_dev), F32),
            ((2 * columns, 3 * columns), F32),
        ],
        weights,
        index,
        *image_rows,
        grams,
        overlap,
        theta,
        block,
        residual,
        applied,
        image,
        block_slots,
        residual_slots,
        applied_slots,
        tiles,
        scalars=2,
        scratch=[pltpu.VMEM((2 * columns, columns), F32)],
    )
    carried, pieces = run(
        carry_kernel,
        "carry",
        [((4 * columns, 2 * columns), F32), ((rows_dev, 3 * columns), F32)],
        coeffs,
        grams,
        overlap,
        theta,
        trial,
        row_order,
    )

    def over(values, axis):
        return lax.all_to_all(values, axis, split_axis=0, concat_axis=0, tiled=True)

    row_parts = run(
        row_sum_kernel, "row_sum", [((groups, 3 * columns), F32)], over(last_grams, "node")
    )[0]
    gathered = over(
        run(
            gather_kernel, "gather", [((nodes, 6 * columns), F32)], over(row_parts, "grp"), pieces
        )[0],
        "node",
    )
    ritz, embedding = run(
        lambda *refs: last_step_kernel(root, *refs),
        "last_step",
        [(square, F32), (slab, F32)],
        gathered,
        carried,
        next_theta,
        scratch=[pltpu.VMEM((3 * columns, columns), F32)],
    )
    return (embedding, ritz, start_theta)


def solution(mesh):
    return jax.shard_map(
        local,
        mesh=mesh,
        in_specs=(
            P(None, BOTH),
            P(BOTH, None, None, None),
            P(BOTH, None),
            P(BOTH, None),
            P(BOTH),
            P(BOTH, None),
        ),
        out_specs=(P(None, BOTH), P(), P()),
        check_vma=False,
    )
```

```python
import jax
import jax.numpy as jnp
from jax import lax
from jax.experimental import pallas as pl
from jax.experimental.pallas import tpu as pltpu
from jax.sharding import PartitionSpec as P

REACH = 2
NSUB = 4
BLOCK = 8
RADIUS = 0.18
BOTH = ("grp", "node")
CORE_X = (1, 128, 256)
Y_Z = (2, 4, 8, 16, 32, 64)


def groups_over(bits):
    mask = sum(bits)
    groups = []
    for base in range(512):
        if base & mask:
            continue
        members = [base]
        for bit in bits:
            members = members + [member | bit for member in members]
        groups.append(members)
    return groups


def swap(values, bits):
    return lax.all_to_all(
        values, BOTH, split_axis=0, concat_axis=0, tiled=True, axis_index_groups=groups_over(bits)
    )


def run(kernel, name, results, *operands, scalars=0, scratch=()):
    smem = pl.BlockSpec(memory_space=pltpu.SMEM)
    vmem = pl.BlockSpec(memory_space=pltpu.VMEM)
    return pl.pallas_call(
        kernel,
        out_shape=[jax.ShapeDtypeStruct(shape, dtype) for shape, dtype in results],
        in_specs=[smem] * scalars + [vmem] * (len(operands) - scalars),
        out_specs=[vmem] * len(results),
        scratch_shapes=list(scratch),
        compiler_params=pltpu.CompilerParams(vmem_limit_bytes=32 << 20),
        name=name,
    )(*operands)


F32 = jnp.float32
BF16 = jnp.bfloat16


def tree_sum(parts):
    while len(parts) > 1:
        parts = [parts[i] + parts[i + 1] for i in range(0, len(parts), 2)]
    return parts[0]


def sum_kernel(first, parts_ref, out_ref):
    summed = tree_sum([parts_ref[i, first:] for i in range(parts_ref.shape[0])])
    for i in range(out_ref.shape[0]):
        out_ref[i] = summed


def sum_copies(parts, count, first=0):
    return run(
        lambda *refs: sum_kernel(first, *refs),
        "sum_copies",
        [((count, parts.shape[1] - first, parts.shape[2]), F32)],
        parts,
    )[0]


def row_sum_kernel(parts_ref, out_ref):
    summed = jnp.sum(parts_ref[...], axis=0, keepdims=True)
    out_ref[...] = jnp.broadcast_to(summed, out_ref.shape)


def gather_kernel(parts_ref, pieces_ref, out_ref):
    summed = tree_sum([parts_ref[i : i + 1] for i in range(parts_ref.shape[0])])
    rows, width = pieces_ref.shape
    out_ref[:, :width] = jnp.broadcast_to(summed, (rows, width))
    out_ref[:, width:] = pieces_ref[...]


def mm(left, right, contract):
    return lax.dot_general(
        left,
        right,
        ((contract[:1], contract[1:]), ((), ())),
        precision=lax.Precision.HIGHEST,
        preferred_element_type=jnp.float32,
    )


def nn(left, right):
    return mm(left, right, (1, 0))


def nt(left, right):
    return mm(left, right, (1, 1))


def tn(left, right):
    return mm(left, right, (0, 0))


def eye(order):
    row = lax.broadcasted_iota(jnp.int32, (order, order), 0)
    column = lax.broadcasted_iota(jnp.int32, (order, order), 1)
    return jnp.where(row == column, jnp.float32(1.0), jnp.float32(0.0))


def inverse_root(value):
    guess = lax.rsqrt(value)
    return guess * (1.5 - 0.5 * value * guess * guess)


def inverse_factor(matrix):
    order = matrix.shape[0]
    lanes = 2 * order
    both = jnp.concatenate([matrix, eye(order)], axis=1)
    bands = [both[8 * i : 8 * i + 8] for i in range(order // 8)]
    sublane = lax.broadcasted_iota(jnp.int32, (8, lanes), 0)
    done = [None] * len(bands)
    for first in range(0, order, BLOCK):
        band = first // 8
        base = first % 8
        last_of_band = base + BLOCK == 8
        live = range(band, len(bands))
        column = [
            [jnp.broadcast_to(bands[i][:, first + k : first + k + 1], (8, lanes)) for i in live]
            for k in range(BLOCK)
        ]
        row = [
            jnp.broadcast_to(bands[band][base + k : base + k + 1], (8, lanes)) for k in range(BLOCK)
        ]
        entry = [
            [
                jnp.broadcast_to(column[l][0][base + k : base + k + 1], (8, lanes))
                for l in range(k + 1)
            ]
            for k in range(BLOCK)
        ]
        inverse = []
        factor = [[None] * BLOCK for _ in range(BLOCK)]
        for l in range(BLOCK):
            inverse.append(1.0 / entry[l][l])
            for k in range(l + 1, BLOCK):
                factor[k][l] = entry[k][l] * inverse[l]
                for m in range(l + 1, k + 1):
                    entry[k][m] = entry[k][m] - factor[k][l] * entry[m][l]
        start = 1 if last_of_band else 0
        for k in range(BLOCK):
            for l in range(k):
                row[k] = row[k] - factor[k][l] * row[l]
                for i in range(start, len(live)):
                    column[k][i] = column[k][i] - factor[k][l] * column[l][i]
        for k in range(BLOCK):
            scaled = row[k] * inverse_root(entry[k][k])
            if done[band] is None:
                done[band] = scaled
            else:
                done[band] = jnp.where(sublane == base + k, scaled, done[band])
            left = row[k] * inverse[k]
            for i in range(start, len(live)):
                bands[band + i] = bands[band + i] - column[k][i] * left
    return jnp.concatenate(done, axis=0)[:, order:]


def half_sum(matrix):
    return 0.5 * (matrix + matrix.T)


def orthonormal(image):
    return nt(image, inverse_factor(tn(image, image)))


def project(linv, gram, basis_ref):
    order = linv.shape[0]
    columns = basis_ref.shape[1]
    projected = half_sum(nt(nn(linv, gram), linv))
    scale = jnp.sqrt(jnp.sum(projected * projected, keepdims=True) + 1e-06)
    unit = projected / scale
    identity = eye(order)
    filtered = unit + 1.25 * identity
    square = nn(filtered, filtered)
    fourth = nn(square, square)
    eighth = nn(fourth, fourth)
    unit2 = square - 2.5 * unit - 1.5625 * identity
    unit4 = nn(unit2, unit2)
    bound = jnp.sum(unit4 * unit4)
    basis_ref[...] = orthonormal(nn(eighth, eighth[:, :columns]))

    @pl.when(jnp.logical_not(bound < RADIUS**8))
    def _():
        basis_ref[...] = identity[:, :columns]

        def sweep(_, carry):
            basis_ref[...] = orthonormal(nn(fourth, basis_ref[...]))
            return carry

        lax.fori_loop(0, NSUB, sweep, 0)

    basis = basis_ref[...]
    coeffs = tn(linv, basis)
    theta = half_sum(tn(basis, nn(projected, basis)))
    return coeffs, theta


def load_square(gathered_ref):
    width = gathered_ref.shape[2]
    members = gathered_ref.shape[0]
    share = width // 4 // members
    packed = jnp.concatenate([gathered_ref[i, :share] for i in range(members)], axis=0)
    return jnp.concatenate([packed[:, : width // 2], packed[:, width // 2 :]], axis=0)


def store_parcel(ref, value, partial):
    members, rows = ref.shape[0], value.shape[0]
    share = partial.shape[0] // members
    for i in range(members):
        ref[i, :rows] = value
        ref[i, rows : rows + share] = partial[share * i : share * (i + 1)]
        if ref.shape[1] > rows + share:
            ref[i, rows + share :] = jnp.zeros((ref.shape[1] - rows - share, ref.shape[2]), F32)


def pack(matrix):
    half = matrix.shape[0] // 2
    return jnp.concatenate([matrix[:half], matrix[half:]], axis=1)


def gram_kernel(start_ref, parcel_ref):
    start = start_ref[...]
    store_parcel(parcel_ref, start, pack(nt(start, start)))


def neighbour_rows(index_ref, own_ref, other_ref, mine_ref, rows):
    count = own_ref.shape[0]

    def at(slot):
        side = lax.div(index_ref[slot], count)
        member = lax.rem(index_ref[slot], count)
        outer = jnp.where(side == 0, mine_ref[member, :rows], other_ref[member, :rows])
        return jnp.where(side == 1, own_ref[member, :rows], outer)

    return at


def multiply_tiles(weight_ref, tiles_ref, slot_values):
    acc = None
    for slot in range(tiles_ref.shape[0]):
        product = lax.dot_general(
            slot_values(slot).astype(BF16),
            tiles_ref[slot],
            (((1,), (1,)), ((), ())),
            preferred_element_type=F32,
        )
        product = weight_ref[slot] * product
        acc = product if acc is None else acc + product
    return acc


def start_kernel(weight_ref, index_ref, own_ref, other_ref, mine_ref, gram_ref, start_ref, tiles_ref, block_ref, block_slots_ref, applied_ref, parcel_ref):
    inverse = inverse_factor(load_square(gram_ref))
    block = nn(inverse, start_ref[...])
    block_ref[...] = block

    rows_at = neighbour_rows(index_ref, own_ref, other_ref, mine_ref, block.shape[0])

    def values(slot):
        there = nn(inverse, rows_at(slot))
        block_slots_ref[slot] = there
        return there

    applied = multiply_tiles(weight_ref, tiles_ref, values)
    applied_ref[...] = applied
    store_parcel(parcel_ref, applied, pack(nt(block, applied)))


def first_kernel(root, weight_ref, index_ref, own_ref, other_ref, mine_ref, sum_ref, block_ref, applied_ref, block_slots_ref, tiles_ref, theta_ref, start_theta_ref, residual_ref, residual_slots_ref, image_ref, parcel_ref, overlap_ref, applied_slots_ref):
    product = load_square(sum_ref)
    theta = half_sum(product)
    overlap_ref[...] = product - theta
    theta_ref[...] = theta
    start_theta_ref[...] = root * theta
    block = block_ref[...]
    applied = applied_ref[...]
    residual = applied - nn(theta, block)
    residual_ref[...] = residual

    rows_at = neighbour_rows(index_ref, own_ref, other_ref, mine_ref, block.shape[0])

    def values(slot):
        applied_there = rows_at(slot)
        applied_slots_ref[slot] = applied_there
        there = applied_there - nn(theta, block_slots_ref[slot])
        residual_slots_ref[slot] = there
        return there

    image = multiply_tiles(weight_ref, tiles_ref, values)
    image_ref[...] = image
    cross = 0.5 * (nt(block, image) + nt(applied, residual))
    own = nt(residual, image)
    order = cross.shape[0]
    row = lax.broadcasted_iota(jnp.int32, (order, order), 0)
    column = lax.broadcasted_iota(jnp.int32, (order, order), 1)
    both = jnp.where(row >= column, nt(residual, residual), half_sum(own))
    diagonal = jnp.sum(jnp.where(row == column, own, F32(0.0)), axis=0, keepdims=True)
    partial = jnp.concatenate([cross, both], axis=1)
    tail = jnp.concatenate([diagonal, jnp.zeros_like(diagonal)], axis=1)
    members = parcel_ref.shape[0]
    share = order // members
    for i in range(members):
        parcel_ref[i, :order] = image
        parcel_ref[i, order : order + share] = partial[share * i : share * (i + 1)]
        parcel_ref[i, order + share :] = tail


def assemble_first(gathered_ref, theta):
    members = gathered_ref.shape[0]
    columns = theta.shape[0]
    share = columns // members
    grams = jnp.concatenate([gathered_ref[i, :share] for i in range(members)], axis=0)
    diagonal = gathered_ref[0, share:, :columns]
    cross = grams[:, :columns]
    both = grams[:, columns:]
    turned = both.T
    row = lax.broadcasted_iota(jnp.int32, (columns, columns), 0)
    column = lax.broadcasted_iota(jnp.int32, (columns, columns), 1)
    basis = jnp.where(row >= column, both, turned)
    own = jnp.where(row < column, both, jnp.where(row > column, turned, diagonal))
    gram = jnp.concatenate(
        [jnp.concatenate([theta, cross], axis=1), jnp.concatenate([cross.T, own], axis=1)], axis=0
    )
    return basis, gram


def second_kernel(weight_ref, index_ref, own_ref, other_ref, mine_ref, grams_ref, overlap_ref, theta_ref, block_ref, residual_ref, applied_ref, image_ref, block_slots_ref, residual_slots_ref, applied_slots_ref, tiles_ref, coeffs_ref, theta_out_ref, trial_ref, grams_out_ref, basis_ref):
    columns = theta_ref.shape[0]
    width = block_ref.shape[1]
    overlap = overlap_ref[...]
    own, gram = assemble_first(grams_ref, theta_ref[...])
    factor = inverse_factor(own - tn(overlap, overlap))
    linv = jnp.concatenate(
        [
            jnp.concatenate([eye(columns), jnp.zeros((columns, columns), F32)], axis=1),
            jnp.concatenate([-nt(factor, overlap), factor], axis=1),
        ],
        axis=0,
    )
    coeffs, theta = project(linv, gram, basis_ref)
    theta_out_ref[...] = theta
    lower = jnp.concatenate([jnp.zeros((columns, columns), F32), coeffs[columns:]], axis=0)
    both = jnp.concatenate([coeffs, lower], axis=1)
    coeffs_ref[...] = both
    mix = jnp.concatenate([coeffs, -nn(coeffs, theta)], axis=0).T

    image_at = neighbour_rows(index_ref, own_ref, other_ref, mine_ref, columns)

    def values(slot):
        parts = [
            applied_slots_ref[slot],
            image_at(slot),
            block_slots_ref[slot],
            residual_slots_ref[slot],
        ]
        return nn(mix, jnp.concatenate(parts, axis=0))

    image = multiply_tiles(weight_ref, tiles_ref, values)
    block, applied = block_ref[...], applied_ref[...]
    previous, previous_image = residual_ref[...], image_ref[...]
    residual = nn(mix, jnp.concatenate([applied, previous_image, block, previous], axis=0))
    old_trial = jnp.concatenate([block, previous], axis=0)
    old_applied = jnp.concatenate([applied, previous_image], axis=0)
    fresh = tn(both, jnp.concatenate([old_trial, old_applied], axis=1))
    trial = jnp.concatenate([fresh[:columns, :width], residual, fresh[columns:, :width]], axis=0)
    trial_ref[...] = trial
    applied_trial = jnp.concatenate([fresh[:columns, width:], image, fresh[columns:, width:]], axis=0)
    cross = 0.5 * (nt(image, trial) + nt(residual, applied_trial))
    grams_out_ref[...] = jnp.concatenate([nt(residual, trial), cross], axis=0)


def carry_kernel(coeffs_ref, grams_ref, overlap_ref, theta_ref, trial_ref, order_ref, carried_ref, pieces_ref):
    columns = theta_ref.shape[0]
    coeffs = coeffs_ref[...]
    overlap = overlap_ref[...]
    own, gram = assemble_first(grams_ref, theta_ref[...])
    basis = jnp.concatenate(
        [
            jnp.concatenate([eye(columns), overlap], axis=1),
            jnp.concatenate([overlap.T, own], axis=1),
        ],
        axis=0,
    )
    carried_ref[...] = jnp.concatenate(
        [tn(coeffs, nn(basis, coeffs)), tn(coeffs, nn(gram, coeffs))], axis=0
    )
    width = trial_ref.shape[1]
    place = lax.broadcasted_iota(jnp.int32, (width, width), 0)
    pick = jnp.where(place == order_ref[...], F32(1.0), F32(0.0))
    pieces_ref[...] = mm(pick, trial_ref[...], (0, 1))


def last_step_kernel(root, gathered_ref, carried_ref, theta_ref, theta_out_ref, embedding_ref, basis_ref):
    columns = theta_ref.shape[0]
    width = gathered_ref.shape[1] // 2
    grams = gathered_ref[:, :width].T
    arrived = gathered_ref[:, width:]
    carried = carried_ref[...]
    wide = 2 * columns
    overlap = jnp.concatenate([grams[:columns, :columns], carried[:columns, columns:wide]], axis=1)
    mixed = grams[wide:, :columns]
    spread = tn(overlap, overlap)
    first = grams[columns:wide, :columns] - spread[:columns, :columns]
    corner = mixed.T - spread[:columns, columns:]
    second = carried[columns:wide, columns:wide] - spread[columns:, columns:]
    factor = inverse_factor(first)
    middle = nn(factor, corner)
    other = inverse_factor(second - tn(middle, middle))
    zero = jnp.zeros((columns, columns), F32)
    lower = jnp.concatenate(
        [
            jnp.concatenate([factor, zero], axis=1),
            jnp.concatenate([-nn(other, tn(middle, factor)), other], axis=1),
        ],
        axis=0,
    )
    linv = jnp.concatenate(
        [
            jnp.concatenate([eye(columns), zero, zero], axis=1),
            jnp.concatenate([-nt(lower, overlap), lower], axis=1),
        ],
        axis=0,
    )
    cross = grams[:columns, columns:]
    own = half_sum(grams[columns:wide, columns:])
    momentum_cross = grams[wide:, columns:]
    block_momentum = carried[wide : wide + columns, columns:wide]
    momentum = half_sum(carried[wide + columns :, columns:wide])
    gram = jnp.concatenate(
        [
            jnp.concatenate([theta_ref[...], cross, block_momentum], axis=1),
            jnp.concatenate([cross.T, own, momentum_cross.T], axis=1),
            jnp.concatenate([block_momentum.T, momentum_cross, momentum], axis=1),
        ],
        axis=0,
    )
    coeffs, theta = project(linv, gram, basis_ref)
    theta_out_ref[...] = theta
    embedding_ref[...] = root * mm(coeffs, arrived, (0, 1))


def local(start_block, weight_tiles, tile_scales, neighbour_ids, live_counts, row_order):
    columns = start_block.shape[0]
    rows_dev = start_block.shape[1]
    groups = lax.axis_size("grp")
    nodes = lax.axis_size("node")
    here = lax.axis_index("node")
    ids = neighbour_ids[0]
    slots = ids.shape[0]
    group_index = ids // nodes
    node_index = ids % nodes
    chips = nodes // 2
    chip_offset = (node_index // 2 - here // 2 + 1 + chips) % chips
    fetched = jnp.where(chip_offset // 2 == here % 2, 0, 2)
    side = jnp.where(chip_offset == 1, 1, fetched)
    index = side * (2 * groups) + node_index % 2 + 2 * group_index
    index = jnp.clip(index, 0, 6 * groups - 1).astype(jnp.int32)
    slot_iota = jnp.arange(slots, dtype=jnp.int32)
    weights = jnp.where(slot_iota < live_counts[0], tile_scales[0], F32(0.0))
    tiles = weight_tiles[0]
    outward = [(source, (source + 2 - 4 * (source % 2)) % nodes) for source in range(nodes)]
    to_pair = [(source, source ^ 1) for source in range(nodes)]
    root = float(rows_dev * groups * nodes) ** 0.5
    slab = (columns, rows_dev)
    square = (columns, columns)
    slab_slots = ((slots,) + slab, F32)

    def exchange(parcel):
        received = swap(parcel, CORE_X)
        partial = sum_copies(received, 2 ** len(Y_Z), columns)
        shared = swap(partial, Y_Z)
        later, _ = lax.optimization_barrier((received, partial))
        mine = lax.ppermute(later, "node", outward)
        other = lax.ppermute(mine, "node", to_pair)
        summed = swap(sum_copies(shared, 2 ** len(CORE_X)), CORE_X)
        return (received, other, mine), summed

    def parcel_of(share):
        return ((2 * groups, columns + share, rows_dev), F32)

    small = parcel_of(columns // (4 * groups))
    large = parcel_of(columns // (2 * groups) + 1)
    start_rows, gram = exchange(run(gram_kernel, "start_gram", [small], start_block)[0])
    block, block_slots, applied, parcel = run(
        start_kernel,
        "start_step",
        [(slab, F32), slab_slots, (slab, F32), large],
        weights,
        index,
        *start_rows,
        gram,
        start_block,
        tiles,
        scalars=2,
    )
    applied_rows, theta_sum = exchange(parcel)
    theta, start_theta, residual, residual_slots, image, parcel, overlap, applied_slots = run(
        lambda *refs: first_kernel(root, *refs),
        "first_residual",
        [
            (square, F32),
            (square, F32),
            (slab, F32),
            slab_slots,
            (slab, F32),
            large,
            (square, F32),
            slab_slots,
        ],
        weights,
        index,
        *applied_rows,
        theta_sum,
        block,
        applied,
        block_slots,
        tiles,
        scalars=2,
    )
    image_rows, grams = exchange(parcel)
    coeffs, next_theta, trial, last_grams = run(
        second_kernel,
        "second_step",
        [
            ((2 * columns, 2 * columns), F32),
            (square, F32),
            ((3 * columns, rows_dev), F32),
            ((2 * columns, 3 * columns), F32),
        ],
        weights,
        index,
        *image_rows,
        grams,
        overlap,
        theta,
        block,
        residual,
        applied,
        image,
        block_slots,
        residual_slots,
        applied_slots,
        tiles,
        scalars=2,
        scratch=[pltpu.VMEM((2 * columns, columns), F32)],
    )
    carried, pieces = run(
        carry_kernel,
        "carry",
        [((4 * columns, 2 * columns), F32), ((rows_dev, 3 * columns), F32)],
        coeffs,
        grams,
        overlap,
        theta,
        trial,
        row_order,
    )

    def over(values, axis):
        return lax.all_to_all(values, axis, split_axis=0, concat_axis=0, tiled=True)

    row_parts = run(
        row_sum_kernel, "row_sum", [((groups, 3 * columns), F32)], over(last_grams, "node")
    )[0]
    gathered = over(
        run(
            gather_kernel, "gather", [((nodes, 6 * columns), F32)], over(row_parts, "grp"), pieces
        )[0],
        "node",
    )
    ritz, embedding = run(
        lambda *refs: last_step_kernel(root, *refs),
        "last_step",
        [(square, F32), (slab, F32)],
        gathered,
        carried,
        next_theta,
        scratch=[pltpu.VMEM((3 * columns, columns), F32)],
    )
    return (embedding, ritz, start_theta)


def solution(mesh):
    return jax.shard_map(
        local,
        mesh=mesh,
        in_specs=(
            P(None, BOTH),
            P(BOTH, None, None, None),
            P(BOTH, None),
            P(BOTH, None),
            P(BOTH),
            P(BOTH, None),
        ),
        out_specs=(P(None, BOTH), P(), P()),
        check_vma=False,
    )
```

```python
import jax
import jax.numpy as jnp
from jax import lax
from jax.experimental import pallas as pl
from jax.experimental.pallas import tpu as pltpu
from jax.sharding import PartitionSpec as P

REACH = 2
NSUB = 4
BLOCK = 8
RADIUS = 0.18
BOTH = ("grp", "node")
CORE_X = (1, 128, 256)
CORE = (1,)
CORE_X1 = (1, 128)
Y_Z = (2, 4, 8, 16, 32, 64)


def groups_over(bits):
    mask = sum(bits)
    groups = []
    for base in range(512):
        if base & mask:
            continue
        members = [base]
        for bit in bits:
            members = members + [member | bit for member in members]
        groups.append(members)
    return groups


def swap(values, bits):
    return lax.all_to_all(
        values, BOTH, split_axis=0, concat_axis=0, tiled=True, axis_index_groups=groups_over(bits)
    )


def run(kernel, name, results, *operands, scalars=0, scratch=()):
    smem = pl.BlockSpec(memory_space=pltpu.SMEM)
    vmem = pl.BlockSpec(memory_space=pltpu.VMEM)
    return pl.pallas_call(
        kernel,
        out_shape=[jax.ShapeDtypeStruct(shape, dtype) for shape, dtype in results],
        in_specs=[smem] * scalars + [vmem] * (len(operands) - scalars),
        out_specs=[vmem] * len(results),
        scratch_shapes=list(scratch),
        compiler_params=pltpu.CompilerParams(vmem_limit_bytes=32 << 20),
        name=name,
    )(*operands)


F32 = jnp.float32
BF16 = jnp.bfloat16


def tree_sum(parts):
    while len(parts) > 1:
        parts = [parts[i] + parts[i + 1] for i in range(0, len(parts), 2)]
    return parts[0]


def sum_kernel(first, parts_ref, out_ref):
    summed = tree_sum([parts_ref[i, first:] for i in range(parts_ref.shape[0])])
    for i in range(out_ref.shape[0]):
        out_ref[i] = summed


def sum_copies(parts, count, first=0):
    return run(
        lambda *refs: sum_kernel(first, *refs),
        "sum_copies",
        [((count, parts.shape[1] - first, parts.shape[2]), F32)],
        parts,
    )[0]


def row_sum_kernel(parts_ref, out_ref):
    summed = jnp.sum(parts_ref[...], axis=0, keepdims=True)
    out_ref[...] = jnp.broadcast_to(summed, out_ref.shape)


def gather_kernel(parts_ref, pieces_ref, out_ref):
    summed = tree_sum([parts_ref[i : i + 1] for i in range(parts_ref.shape[0])])
    rows, width = pieces_ref.shape
    out_ref[:, :width] = jnp.broadcast_to(summed, (rows, width))
    out_ref[:, width:] = pieces_ref[...]


def mm(left, right, contract):
    return lax.dot_general(
        left,
        right,
        ((contract[:1], contract[1:]), ((), ())),
        precision=lax.Precision.HIGHEST,
        preferred_element_type=jnp.float32,
    )


def nn(left, right):
    return mm(left, right, (1, 0))


def nt(left, right):
    return mm(left, right, (1, 1))


def tn(left, right):
    return mm(left, right, (0, 0))


def eye(order):
    row = lax.broadcasted_iota(jnp.int32, (order, order), 0)
    column = lax.broadcasted_iota(jnp.int32, (order, order), 1)
    return jnp.where(row == column, jnp.float32(1.0), jnp.float32(0.0))


def inverse_root(value):
    guess = lax.rsqrt(value)
    return guess * (1.5 - 0.5 * value * guess * guess)


def inverse_factor(matrix):
    order = matrix.shape[0]
    lanes = 2 * order
    both = jnp.concatenate([matrix, eye(order)], axis=1)
    bands = [both[8 * i : 8 * i + 8] for i in range(order // 8)]
    sublane = lax.broadcasted_iota(jnp.int32, (8, lanes), 0)
    done = [None] * len(bands)
    for first in range(0, order, BLOCK):
        band = first // 8
        base = first % 8
        last_of_band = base + BLOCK == 8
        live = range(band, len(bands))
        column = [
            [jnp.broadcast_to(bands[i][:, first + k : first + k + 1], (8, lanes)) for i in live]
            for k in range(BLOCK)
        ]
        row = [
            jnp.broadcast_to(bands[band][base + k : base + k + 1], (8, lanes)) for k in range(BLOCK)
        ]
        entry = [
            [
                jnp.broadcast_to(column[l][0][base + k : base + k + 1], (8, lanes))
                for l in range(k + 1)
            ]
            for k in range(BLOCK)
        ]
        inverse = []
        factor = [[None] * BLOCK for _ in range(BLOCK)]
        for l in range(BLOCK):
            inverse.append(1.0 / entry[l][l])
            for k in range(l + 1, BLOCK):
                factor[k][l] = entry[k][l] * inverse[l]
                for m in range(l + 1, k + 1):
                    entry[k][m] = entry[k][m] - factor[k][l] * entry[m][l]
        start = 1 if last_of_band else 0
        for k in range(BLOCK):
            for l in range(k):
                row[k] = row[k] - factor[k][l] * row[l]
                for i in range(start, len(live)):
                    column[k][i] = column[k][i] - factor[k][l] * column[l][i]
        for k in range(BLOCK):
            scaled = row[k] * inverse_root(entry[k][k])
            if done[band] is None:
                done[band] = scaled
            else:
                done[band] = jnp.where(sublane == base + k, scaled, done[band])
            left = row[k] * inverse[k]
            for i in range(start, len(live)):
                bands[band + i] = bands[band + i] - column[k][i] * left
    return jnp.concatenate(done, axis=0)[:, order:]


def half_sum(matrix):
    return 0.5 * (matrix + matrix.T)


def orthonormal(image):
    return nt(image, inverse_factor(tn(image, image)))


def project(linv, gram, basis_ref):
    order = linv.shape[0]
    columns = basis_ref.shape[1]
    projected = half_sum(nt(nn(linv, gram), linv))
    scale = jnp.sqrt(jnp.sum(projected * projected, keepdims=True) + 1e-06)
    unit = projected / scale
    identity = eye(order)
    filtered = unit + 1.25 * identity
    square = nn(filtered, filtered)
    fourth = nn(square, square)
    eighth = nn(fourth, fourth)
    unit2 = square - 2.5 * unit - 1.5625 * identity
    unit4 = nn(unit2, unit2)
    bound = jnp.sum(unit4 * unit4)
    basis_ref[...] = orthonormal(nn(eighth, eighth[:, :columns]))

    @pl.when(jnp.logical_not(bound < RADIUS**8))
    def _():
        basis_ref[...] = identity[:, :columns]

        def sweep(_, carry):
            basis_ref[...] = orthonormal(nn(fourth, basis_ref[...]))
            return carry

        lax.fori_loop(0, NSUB, sweep, 0)

    basis = basis_ref[...]
    coeffs = tn(linv, basis)
    theta = half_sum(tn(basis, nn(projected, basis)))
    return coeffs, theta


def load_square(gathered_ref):
    members, _, width = gathered_ref.shape
    packed = jnp.concatenate([gathered_ref[i] for i in range(members)], axis=0)
    return jnp.concatenate([packed[:, : width // 2], packed[:, width // 2 :]], axis=0)


def store_parcel(ref, value, partial):
    rows = value.shape[0]
    share = ref.shape[1] - rows
    shares = partial.shape[0] // share
    for i in range(ref.shape[0]):
        first = share * (i % shares)
        ref[i, :rows] = value
        ref[i, rows:] = partial[first : first + share]


def pack(matrix):
    half = matrix.shape[0] // 2
    return jnp.concatenate([matrix[:half], matrix[half:]], axis=1)


def gram_kernel(start_ref, parcel_ref):
    start = start_ref[...]
    store_parcel(parcel_ref, start, pack(nt(start, start)))


def neighbour_rows(index_ref, own_ref, up_ref, down_ref, rows):
    count = own_ref.shape[0]

    def at(slot):
        side = lax.div(index_ref[slot], count)
        member = lax.rem(index_ref[slot], count)
        outer = jnp.where(side == 0, down_ref[member, :rows], up_ref[member, :rows])
        return jnp.where(side == 1, own_ref[member, :rows], outer)

    return at


def multiply_tiles(weight_ref, tiles_ref, slot_values):
    acc = None
    for slot in range(tiles_ref.shape[0]):
        product = lax.dot_general(
            slot_values(slot).astype(BF16),
            tiles_ref[slot],
            (((1,), (1,)), ((), ())),
            preferred_element_type=F32,
        )
        product = weight_ref[slot] * product
        acc = product if acc is None else acc + product
    return acc


def start_kernel(weight_ref, index_ref, own_ref, up_ref, down_ref, gram_ref, start_ref, tiles_ref, block_ref, block_slots_ref, applied_ref, parcel_ref):
    inverse = inverse_factor(load_square(gram_ref))
    block = nn(inverse, start_ref[...])
    block_ref[...] = block

    rows_at = neighbour_rows(index_ref, own_ref, up_ref, down_ref, block.shape[0])

    def values(slot):
        there = nn(inverse, rows_at(slot))
        block_slots_ref[slot] = there
        return there

    applied = multiply_tiles(weight_ref, tiles_ref, values)
    applied_ref[...] = applied
    store_parcel(parcel_ref, applied, pack(nt(block, applied)))


def first_kernel(root, weight_ref, index_ref, own_ref, up_ref, down_ref, sum_ref, block_ref, applied_ref, block_slots_ref, tiles_ref, theta_ref, start_theta_ref, residual_ref, residual_slots_ref, image_ref, parcel_ref, overlap_ref, applied_slots_ref):
    product = load_square(sum_ref)
    theta = half_sum(product)
    overlap_ref[...] = product - theta
    theta_ref[...] = theta
    start_theta_ref[...] = root * theta
    block = block_ref[...]
    applied = applied_ref[...]
    residual = applied - nn(theta, block)
    residual_ref[...] = residual

    rows_at = neighbour_rows(index_ref, own_ref, up_ref, down_ref, block.shape[0])

    def values(slot):
        applied_there = rows_at(slot)
        applied_slots_ref[slot] = applied_there
        there = applied_there - nn(theta, block_slots_ref[slot])
        residual_slots_ref[slot] = there
        return there

    image = multiply_tiles(weight_ref, tiles_ref, values)
    image_ref[...] = image
    cross = 0.5 * (nt(block, image) + nt(applied, residual))
    own = nt(residual, image)
    order = cross.shape[0]
    row = lax.broadcasted_iota(jnp.int32, (order, order), 0)
    column = lax.broadcasted_iota(jnp.int32, (order, order), 1)
    both = jnp.where(row >= column, nt(residual, residual), half_sum(own))
    diagonal = jnp.sum(jnp.where(row == column, own, F32(0.0)), axis=0, keepdims=True)
    partial = jnp.concatenate([cross, both], axis=1)
    tail = jnp.concatenate([diagonal, jnp.zeros_like(diagonal)], axis=1)
    share = parcel_ref.shape[1] - order - 1
    shares = order // share
    for i in range(parcel_ref.shape[0]):
        first = share * (i % shares)
        parcel_ref[i, :order] = image
        parcel_ref[i, order : order + share] = partial[first : first + share]
        parcel_ref[i, order + share :] = tail


def assemble_first(gathered_ref, theta):
    members = gathered_ref.shape[0]
    columns = theta.shape[0]
    share = columns // members
    grams = jnp.concatenate([gathered_ref[i, :share] for i in range(members)], axis=0)
    diagonal = gathered_ref[0, share:, :columns]
    cross = grams[:, :columns]
    both = grams[:, columns:]
    turned = both.T
    row = lax.broadcasted_iota(jnp.int32, (columns, columns), 0)
    column = lax.broadcasted_iota(jnp.int32, (columns, columns), 1)
    basis = jnp.where(row >= column, both, turned)
    own = jnp.where(row < column, both, jnp.where(row > column, turned, diagonal))
    gram = jnp.concatenate(
        [jnp.concatenate([theta, cross], axis=1), jnp.concatenate([cross.T, own], axis=1)], axis=0
    )
    return basis, gram


def second_kernel(weight_ref, index_ref, own_ref, up_ref, down_ref, grams_ref, overlap_ref, theta_ref, block_ref, residual_ref, applied_ref, image_ref, block_slots_ref, residual_slots_ref, applied_slots_ref, tiles_ref, coeffs_ref, theta_out_ref, trial_ref, grams_out_ref, basis_ref):
    columns = theta_ref.shape[0]
    width = block_ref.shape[1]
    overlap = overlap_ref[...]
    own, gram = assemble_first(grams_ref, theta_ref[...])
    factor = inverse_factor(own - tn(overlap, overlap))
    linv = jnp.concatenate(
        [
            jnp.concatenate([eye(columns), jnp.zeros((columns, columns), F32)], axis=1),
            jnp.concatenate([-nt(factor, overlap), factor], axis=1),
        ],
        axis=0,
    )
    coeffs, theta = project(linv, gram, basis_ref)
    theta_out_ref[...] = theta
    lower = jnp.concatenate([jnp.zeros((columns, columns), F32), coeffs[columns:]], axis=0)
    both = jnp.concatenate([coeffs, lower], axis=1)
    coeffs_ref[...] = both
    mix = jnp.concatenate([coeffs, -nn(coeffs, theta)], axis=0).T

    image_at = neighbour_rows(index_ref, own_ref, up_ref, down_ref, columns)

    def values(slot):
        parts = [
            applied_slots_ref[slot],
            image_at(slot),
            block_slots_ref[slot],
            residual_slots_ref[slot],
        ]
        return nn(mix, jnp.concatenate(parts, axis=0))

    image = multiply_tiles(weight_ref, tiles_ref, values)
    block, applied = block_ref[...], applied_ref[...]
    previous, previous_image = residual_ref[...], image_ref[...]
    residual = nn(mix, jnp.concatenate([applied, previous_image, block, previous], axis=0))
    old_trial = jnp.concatenate([block, previous], axis=0)
    old_applied = jnp.concatenate([applied, previous_image], axis=0)
    fresh = tn(both, jnp.concatenate([old_trial, old_applied], axis=1))
    trial = jnp.concatenate([fresh[:columns, :width], residual, fresh[columns:, :width]], axis=0)
    trial_ref[...] = trial
    applied_trial = jnp.concatenate([fresh[:columns, width:], image, fresh[columns:, width:]], axis=0)
    cross = 0.5 * (nt(image, trial) + nt(residual, applied_trial))
    grams_out_ref[...] = jnp.concatenate([nt(residual, trial), cross], axis=0)


def carry_kernel(coeffs_ref, grams_ref, overlap_ref, theta_ref, trial_ref, order_ref, carried_ref, pieces_ref):
    columns = theta_ref.shape[0]
    coeffs = coeffs_ref[...]
    overlap = overlap_ref[...]
    own, gram = assemble_first(grams_ref, theta_ref[...])
    basis = jnp.concatenate(
        [
            jnp.concatenate([eye(columns), overlap], axis=1),
            jnp.concatenate([overlap.T, own], axis=1),
        ],
        axis=0,
    )
    carried_ref[...] = jnp.concatenate(
        [tn(coeffs, nn(basis, coeffs)), tn(coeffs, nn(gram, coeffs))], axis=0
    )
    width = trial_ref.shape[1]
    place = lax.broadcasted_iota(jnp.int32, (width, width), 0)
    pick = jnp.where(place == order_ref[...], F32(1.0), F32(0.0))
    pieces_ref[...] = mm(pick, trial_ref[...], (0, 1))


def last_step_kernel(root, gathered_ref, carried_ref, theta_ref, theta_out_ref, embedding_ref, basis_ref):
    columns = theta_ref.shape[0]
    width = gathered_ref.shape[1] // 2
    grams = gathered_ref[:, :width].T
    arrived = gathered_ref[:, width:]
    carried = carried_ref[...]
    wide = 2 * columns
    overlap = jnp.concatenate([grams[:columns, :columns], carried[:columns, columns:wide]], axis=1)
    mixed = grams[wide:, :columns]
    spread = tn(overlap, overlap)
    first = grams[columns:wide, :columns] - spread[:columns, :columns]
    corner = mixed.T - spread[:columns, columns:]
    second = carried[columns:wide, columns:wide] - spread[columns:, columns:]
    factor = inverse_factor(first)
    middle = nn(factor, corner)
    other = inverse_factor(second - tn(middle, middle))
    zero = jnp.zeros((columns, columns), F32)
    lower = jnp.concatenate(
        [
            jnp.concatenate([factor, zero], axis=1),
            jnp.concatenate([-nn(other, tn(middle, factor)), other], axis=1),
        ],
        axis=0,
    )
    linv = jnp.concatenate(
        [
            jnp.concatenate([eye(columns), zero, zero], axis=1),
            jnp.concatenate([-nt(lower, overlap), lower], axis=1),
        ],
        axis=0,
    )
    cross = grams[:columns, columns:]
    own = half_sum(grams[columns:wide, columns:])
    momentum_cross = grams[wide:, columns:]
    block_momentum = carried[wide : wide + columns, columns:wide]
    momentum = half_sum(carried[wide + columns :, columns:wide])
    gram = jnp.concatenate(
        [
            jnp.concatenate([theta_ref[...], cross, block_momentum], axis=1),
            jnp.concatenate([cross.T, own, momentum_cross.T], axis=1),
            jnp.concatenate([block_momentum.T, momentum_cross, momentum], axis=1),
        ],
        axis=0,
    )
    coeffs, theta = project(linv, gram, basis_ref)
    theta_out_ref[...] = theta
    embedding_ref[...] = root * mm(coeffs, arrived, (0, 1))


def local(start_block, weight_tiles, tile_scales, neighbour_ids, live_counts, row_order):
    columns = start_block.shape[0]
    rows_dev = start_block.shape[1]
    groups = lax.axis_size("grp")
    nodes = lax.axis_size("node")
    here = lax.axis_index("node")
    ids = neighbour_ids[0]
    slots = ids.shape[0]
    group_index = ids // nodes
    node_index = ids % nodes
    chips = nodes // 2
    chip_offset = (node_index // 2 - here // 2 + 1 + chips) % chips
    index = jnp.clip(chip_offset * 8 + node_index % 2 + 2 * group_index, 0, 23).astype(jnp.int32)
    slot_iota = jnp.arange(slots, dtype=jnp.int32)
    weights = jnp.where(slot_iota < live_counts[0], tile_scales[0], F32(0.0))
    tiles = weight_tiles[0]
    to_next = [(source, (source + 2) % nodes) for source in range(nodes)]
    to_last = [(source, (source - 2) % nodes) for source in range(nodes)]
    root = float(rows_dev * groups * nodes) ** 0.5
    slab = (columns, rows_dev)
    square = (columns, columns)
    slab_slots = ((slots,) + slab, F32)

    def exchange(parcel, last):
        received = swap(parcel, CORE_X)
        partial = sum_copies(received, 2 ** len(Y_Z), columns)
        shared = swap(partial, Y_Z)
        later, _ = lax.optimization_barrier((received, partial))
        down = lax.ppermute(later, "node", to_next)
        up = lax.ppermute(later, "node", to_last)
        summed = swap(sum_copies(shared, 2 ** len(last)), last)
        return (received, up, down), summed

    def parcel_of(share):
        return ((2 * groups, columns + share, rows_dev), F32)

    small = parcel_of(columns // 4)
    start_rows, gram = exchange(run(gram_kernel, "start_gram", [small], start_block)[0], CORE)
    block, block_slots, applied, parcel = run(
        start_kernel,
        "start_step",
        [(slab, F32), slab_slots, (slab, F32), small],
        weights,
        index,
        *start_rows,
        gram,
        start_block,
        tiles,
        scalars=2,
    )
    applied_rows, theta_sum = exchange(parcel, CORE)
    theta, start_theta, residual, residual_slots, image, parcel, overlap, applied_slots = run(
        lambda *refs: first_kernel(root, *refs),
        "first_residual",
        [
            (square, F32),
            (square, F32),
            (slab, F32),
            slab_slots,
            (slab, F32),
            parcel_of(columns // 4 + 1),
            (square, F32),
            slab_slots,
        ],
        weights,
        index,
        *applied_rows,
        theta_sum,
        block,
        applied,
        block_slots,
        tiles,
        scalars=2,
    )
    image_rows, grams = exchange(parcel, CORE_X1)
    coeffs, next_theta, trial, last_grams = run(
        second_kernel,
        "second_step",
        [
            ((2 * columns, 2 * columns), F32),
            (square, F32),
            ((3 * columns, rows_dev), F32),
            ((2 * columns, 3 * columns), F32),
        ],
        weights,
        index,
        *image_rows,
        grams,
        overlap,
        theta,
        block,
        residual,
        applied,
        image,
        block_slots,
        residual_slots,
        applied_slots,
        tiles,
        scalars=2,
        scratch=[pltpu.VMEM((2 * columns, columns), F32)],
    )
    carried, pieces = run(
        carry_kernel,
        "carry",
        [((4 * columns, 2 * columns), F32), ((rows_dev, 3 * columns), F32)],
        coeffs,
        grams,
        overlap,
        theta,
        trial,
        row_order,
    )

    def over(values, axis):
        return lax.all_to_all(values, axis, split_axis=0, concat_axis=0, tiled=True)

    row_parts = run(
        row_sum_kernel, "row_sum", [((groups, 3 * columns), F32)], over(last_grams, "node")
    )[0]
    gathered = over(
        run(
            gather_kernel, "gather", [((nodes, 6 * columns), F32)], over(row_parts, "grp"), pieces
        )[0],
        "node",
    )
    ritz, embedding = run(
        lambda *refs: last_step_kernel(root, *refs),
        "last_step",
        [(square, F32), (slab, F32)],
        gathered,
        carried,
        next_theta,
        scratch=[pltpu.VMEM((3 * columns, columns), F32)],
    )
    return (embedding, ritz, start_theta)


def solution(mesh):
    return jax.shard_map(
        local,
        mesh=mesh,
        in_specs=(
            P(None, BOTH),
            P(BOTH, None, None, None),
            P(BOTH, None),
            P(BOTH, None),
            P(BOTH),
            P(BOTH, None),
        ),
        out_specs=(P(None, BOTH), P(), P()),
        check_vma=False,
    )
```

```python
import jax
import jax.numpy as jnp
from jax import lax
from jax.experimental import pallas as pl
from jax.experimental.pallas import tpu as pltpu
from jax.sharding import PartitionSpec as P

REACH = 2
NSUB = 4
BLOCK = 8
RADIUS = 0.18
BOTH = ("grp", "node")
CORE_X = (1, 128, 256)
Y_Z = (2, 4, 8, 16, 32, 64)


def groups_over(bits):
    mask = sum(bits)
    groups = []
    for base in range(512):
        if base & mask:
            continue
        members = [base]
        for bit in bits:
            members = members + [member | bit for member in members]
        groups.append(members)
    return groups


def swap(values, bits):
    return lax.all_to_all(
        values, BOTH, split_axis=0, concat_axis=0, tiled=True, axis_index_groups=groups_over(bits)
    )


def run(kernel, name, results, *operands, scalars=0, scratch=()):
    smem = pl.BlockSpec(memory_space=pltpu.SMEM)
    vmem = pl.BlockSpec(memory_space=pltpu.VMEM)
    return pl.pallas_call(
        kernel,
        out_shape=[jax.ShapeDtypeStruct(shape, dtype) for shape, dtype in results],
        in_specs=[smem] * scalars + [vmem] * (len(operands) - scalars),
        out_specs=[vmem] * len(results),
        scratch_shapes=list(scratch),
        compiler_params=pltpu.CompilerParams(vmem_limit_bytes=32 << 20),
        name=name,
    )(*operands)


F32 = jnp.float32
BF16 = jnp.bfloat16


def tree_sum(parts):
    while len(parts) > 1:
        parts = [parts[i] + parts[i + 1] for i in range(0, len(parts), 2)]
    return parts[0]


def sum_kernel(first, parts_ref, out_ref):
    summed = tree_sum([parts_ref[i, first:] for i in range(parts_ref.shape[0])])
    for i in range(out_ref.shape[0]):
        out_ref[i] = summed


def sum_copies(parts, count, first=0):
    return run(
        lambda *refs: sum_kernel(first, *refs),
        "sum_copies",
        [((count, parts.shape[1] - first, parts.shape[2]), F32)],
        parts,
    )[0]


def row_sum_kernel(parts_ref, out_ref):
    summed = jnp.sum(parts_ref[...], axis=0, keepdims=True)
    out_ref[...] = jnp.broadcast_to(summed, out_ref.shape)


def gather_kernel(parts_ref, pieces_ref, out_ref):
    summed = tree_sum([parts_ref[i : i + 1] for i in range(parts_ref.shape[0])])
    rows, width = pieces_ref.shape
    out_ref[:, :width] = jnp.broadcast_to(summed, (rows, width))
    out_ref[:, width:] = pieces_ref[...]


def mm(left, right, contract):
    return lax.dot_general(
        left,
        right,
        ((contract[:1], contract[1:]), ((), ())),
        precision=lax.Precision.HIGHEST,
        preferred_element_type=jnp.float32,
    )


def nn(left, right):
    return mm(left, right, (1, 0))


def nt(left, right):
    return mm(left, right, (1, 1))


def tn(left, right):
    return mm(left, right, (0, 0))


def eye(order):
    row = lax.broadcasted_iota(jnp.int32, (order, order), 0)
    column = lax.broadcasted_iota(jnp.int32, (order, order), 1)
    return jnp.where(row == column, jnp.float32(1.0), jnp.float32(0.0))


def inverse_root(value):
    guess = lax.rsqrt(value)
    return guess * (1.5 - 0.5 * value * guess * guess)


def inverse_factor(matrix):
    order = matrix.shape[0]
    lanes = 2 * order
    both = jnp.concatenate([matrix, eye(order)], axis=1)
    bands = [both[8 * i : 8 * i + 8] for i in range(order // 8)]
    sublane = lax.broadcasted_iota(jnp.int32, (8, lanes), 0)
    done = [None] * len(bands)
    for first in range(0, order, BLOCK):
        band = first // 8
        base = first % 8
        last_of_band = base + BLOCK == 8
        live = range(band, len(bands))
        column = [
            [jnp.broadcast_to(bands[i][:, first + k : first + k + 1], (8, lanes)) for i in live]
            for k in range(BLOCK)
        ]
        row = [
            jnp.broadcast_to(bands[band][base + k : base + k + 1], (8, lanes)) for k in range(BLOCK)
        ]
        entry = [
            [
                jnp.broadcast_to(column[l][0][base + k : base + k + 1], (8, lanes))
                for l in range(k + 1)
            ]
            for k in range(BLOCK)
        ]
        inverse = []
        factor = [[None] * BLOCK for _ in range(BLOCK)]
        for l in range(BLOCK):
            inverse.append(1.0 / entry[l][l])
            for k in range(l + 1, BLOCK):
                factor[k][l] = entry[k][l] * inverse[l]
                for m in range(l + 1, k + 1):
                    entry[k][m] = entry[k][m] - factor[k][l] * entry[m][l]
        start = 1 if last_of_band else 0
        for k in range(BLOCK):
            for l in range(k):
                row[k] = row[k] - factor[k][l] * row[l]
                for i in range(start, len(live)):
                    column[k][i] = column[k][i] - factor[k][l] * column[l][i]
        for k in range(BLOCK):
            scaled = row[k] * inverse_root(entry[k][k])
            if done[band] is None:
                done[band] = scaled
            else:
                done[band] = jnp.where(sublane == base + k, scaled, done[band])
            left = row[k] * inverse[k]
            for i in range(start, len(live)):
                bands[band + i] = bands[band + i] - column[k][i] * left
    return jnp.concatenate(done, axis=0)[:, order:]


def half_sum(matrix):
    return 0.5 * (matrix + matrix.T)


def orthonormal(image):
    return nt(image, inverse_factor(tn(image, image)))


def project(linv, gram, basis_ref):
    order = linv.shape[0]
    columns = basis_ref.shape[1]
    projected = half_sum(nt(nn(linv, gram), linv))
    scale = jnp.sqrt(jnp.sum(projected * projected, keepdims=True) + 1e-06)
    unit = projected / scale
    identity = eye(order)
    filtered = unit + 1.25 * identity
    square = nn(filtered, filtered)
    fourth = nn(square, square)
    eighth = nn(fourth, fourth)
    unit2 = square - 2.5 * unit - 1.5625 * identity
    unit4 = nn(unit2, unit2)
    bound = jnp.sum(unit4 * unit4)
    basis_ref[...] = orthonormal(nn(eighth, eighth[:, :columns]))

    @pl.when(jnp.logical_not(bound < RADIUS**8))
    def _():
        basis_ref[...] = identity[:, :columns]

        def sweep(_, carry):
            basis_ref[...] = orthonormal(nn(fourth, basis_ref[...]))
            return carry

        lax.fori_loop(0, NSUB, sweep, 0)

    basis = basis_ref[...]
    coeffs = tn(linv, basis)
    theta = half_sum(tn(basis, nn(projected, basis)))
    return coeffs, theta


def load_packed(ref):
    width = ref.shape[1] // 2
    return jnp.concatenate([ref[:, :width], ref[:, width:]], axis=0)


def store_parcel(ref, value, partial):
    members, rows = ref.shape[0], value.shape[0]
    share = partial.shape[0] // members
    for i in range(members):
        ref[i, :rows] = value
        ref[i, rows:] = partial[share * i : share * (i + 1)]


def pack(matrix):
    half = matrix.shape[0] // 2
    return jnp.concatenate([matrix[:half], matrix[half:]], axis=1)


def gram_kernel(start_ref, parcel_ref):
    start = start_ref[...]
    store_parcel(parcel_ref, start, pack(nt(start, start)))


def neighbour_rows(index_ref, own_ref, up_ref, down_ref, rows):
    count = own_ref.shape[0]

    def at(slot):
        side = lax.div(index_ref[slot], count)
        member = lax.rem(index_ref[slot], count)
        outer = jnp.where(side == 0, down_ref[member, :rows], up_ref[member, :rows])
        return jnp.where(side == 1, own_ref[member, :rows], outer)

    return at


def multiply_tiles(weight_ref, tiles_ref, slot_values):
    acc = None
    for slot in range(tiles_ref.shape[0]):
        product = lax.dot_general(
            slot_values(slot).astype(BF16),
            tiles_ref[slot],
            (((1,), (1,)), ((), ())),
            preferred_element_type=F32,
        )
        product = weight_ref[slot] * product
        acc = product if acc is None else acc + product
    return acc


def start_kernel(weight_ref, index_ref, own_ref, up_ref, down_ref, gram_ref, start_ref, tiles_ref, block_ref, block_slots_ref, applied_ref, parcel_ref):
    inverse = inverse_factor(load_packed(gram_ref))
    block = nn(inverse, start_ref[...])
    block_ref[...] = block

    rows_at = neighbour_rows(index_ref, own_ref, up_ref, down_ref, block.shape[0])

    def values(slot):
        there = nn(inverse, rows_at(slot))
        block_slots_ref[slot] = there
        return there

    applied = multiply_tiles(weight_ref, tiles_ref, values)
    applied_ref[...] = applied
    store_parcel(parcel_ref, applied, pack(nt(block, applied)))


def first_kernel(root, weight_ref, index_ref, own_ref, up_ref, down_ref, sum_ref, block_ref, applied_ref, block_slots_ref, tiles_ref, theta_ref, start_theta_ref, residual_ref, residual_slots_ref, image_ref, parcel_ref, overlap_ref, applied_slots_ref):
    product = load_packed(sum_ref)
    theta = half_sum(product)
    overlap_ref[...] = product - theta
    theta_ref[...] = theta
    start_theta_ref[...] = root * theta
    block = block_ref[...]
    applied = applied_ref[...]
    residual = applied - nn(theta, block)
    residual_ref[...] = residual

    rows_at = neighbour_rows(index_ref, own_ref, up_ref, down_ref, block.shape[0])

    def values(slot):
        applied_there = rows_at(slot)
        applied_slots_ref[slot] = applied_there
        there = applied_there - nn(theta, block_slots_ref[slot])
        residual_slots_ref[slot] = there
        return there

    image = multiply_tiles(weight_ref, tiles_ref, values)
    image_ref[...] = image
    cross = 0.5 * (nt(block, image) + nt(applied, residual))
    own = nt(residual, image)
    order = cross.shape[0]
    row = lax.broadcasted_iota(jnp.int32, (order, order), 0)
    column = lax.broadcasted_iota(jnp.int32, (order, order), 1)
    both = jnp.where(row >= column, nt(residual, residual), half_sum(own))
    diagonal = jnp.sum(jnp.where(row == column, own, F32(0.0)), axis=0, keepdims=True)
    partial = jnp.concatenate([cross, both], axis=1)
    tail = jnp.concatenate([diagonal, jnp.zeros_like(diagonal)], axis=1)
    members = parcel_ref.shape[0]
    share = order // members
    for i in range(members):
        parcel_ref[i, :order] = image
        parcel_ref[i, order : order + share] = partial[share * i : share * (i + 1)]
        parcel_ref[i, order + share :] = tail


def assemble_first(gathered_ref, theta):
    members = gathered_ref.shape[0]
    columns = theta.shape[0]
    share = columns // members
    grams = jnp.concatenate([gathered_ref[i, :share] for i in range(members)], axis=0)
    diagonal = gathered_ref[0, share:, :columns]
    cross = grams[:, :columns]
    both = grams[:, columns:]
    turned = both.T
    row = lax.broadcasted_iota(jnp.int32, (columns, columns), 0)
    column = lax.broadcasted_iota(jnp.int32, (columns, columns), 1)
    basis = jnp.where(row >= column, both, turned)
    own = jnp.where(row < column, both, jnp.where(row > column, turned, diagonal))
    gram = jnp.concatenate(
        [jnp.concatenate([theta, cross], axis=1), jnp.concatenate([cross.T, own], axis=1)], axis=0
    )
    return basis, gram


def second_kernel(weight_ref, index_ref, own_ref, up_ref, down_ref, grams_ref, overlap_ref, theta_ref, block_ref, residual_ref, applied_ref, image_ref, block_slots_ref, residual_slots_ref, applied_slots_ref, tiles_ref, coeffs_ref, theta_out_ref, trial_ref, grams_out_ref, basis_ref):
    columns = theta_ref.shape[0]
    width = block_ref.shape[1]
    overlap = overlap_ref[...]
    own, gram = assemble_first(grams_ref, theta_ref[...])
    factor = inverse_factor(own - tn(overlap, overlap))
    linv = jnp.concatenate(
        [
            jnp.concatenate([eye(columns), jnp.zeros((columns, columns), F32)], axis=1),
            jnp.concatenate([-nt(factor, overlap), factor], axis=1),
        ],
        axis=0,
    )
    coeffs, theta = project(linv, gram, basis_ref)
    theta_out_ref[...] = theta
    lower = jnp.concatenate([jnp.zeros((columns, columns), F32), coeffs[columns:]], axis=0)
    both = jnp.concatenate([coeffs, lower], axis=1)
    coeffs_ref[...] = both
    mix = jnp.concatenate([coeffs, -nn(coeffs, theta)], axis=0).T

    image_at = neighbour_rows(index_ref, own_ref, up_ref, down_ref, columns)

    def values(slot):
        parts = [
            applied_slots_ref[slot],
            image_at(slot),
            block_slots_ref[slot],
            residual_slots_ref[slot],
        ]
        return nn(mix, jnp.concatenate(parts, axis=0))

    image = multiply_tiles(weight_ref, tiles_ref, values)
    block, applied = block_ref[...], applied_ref[...]
    previous, previous_image = residual_ref[...], image_ref[...]
    residual = nn(mix, jnp.concatenate([applied, previous_image, block, previous], axis=0))
    old_trial = jnp.concatenate([block, previous], axis=0)
    old_applied = jnp.concatenate([applied, previous_image], axis=0)
    fresh = tn(both, jnp.concatenate([old_trial, old_applied], axis=1))
    trial = jnp.concatenate([fresh[:, :width], residual], axis=0)
    trial_ref[...] = trial
    applied_trial = jnp.concatenate([fresh[:, width:], image], axis=0)
    cross = 0.5 * (nt(image, trial) + nt(residual, applied_trial))
    grams_out_ref[...] = jnp.concatenate([nt(residual, trial), cross], axis=0)


def carry_kernel(coeffs_ref, grams_ref, overlap_ref, theta_ref, trial_ref, order_ref, carried_ref, pieces_ref):
    columns = theta_ref.shape[0]
    coeffs = coeffs_ref[...]
    overlap = overlap_ref[...]
    own, gram = assemble_first(grams_ref, theta_ref[...])
    basis = jnp.concatenate(
        [
            jnp.concatenate([eye(columns), overlap], axis=1),
            jnp.concatenate([overlap.T, own], axis=1),
        ],
        axis=0,
    )
    products = tn(coeffs, nn(basis, coeffs))
    block_momentum = products[:columns, columns:]
    factor = inverse_factor(products[columns:, columns:] - tn(block_momentum, block_momentum))
    zero = jnp.zeros((columns, columns), F32)
    inverse = jnp.concatenate(
        [
            jnp.concatenate([eye(columns), zero], axis=1),
            jnp.concatenate([-nt(factor, block_momentum), factor], axis=1),
        ],
        axis=0,
    )
    carried_ref[...] = jnp.concatenate([inverse, tn(coeffs, nn(gram, coeffs))], axis=0)
    width = trial_ref.shape[1]
    place = lax.broadcasted_iota(jnp.int32, (width, width), 0)
    pick = jnp.where(place == order_ref[...], F32(1.0), F32(0.0))
    pieces_ref[...] = mm(pick, trial_ref[...], (0, 1))


def last_step_kernel(root, gathered_ref, carried_ref, theta_ref, theta_out_ref, embedding_ref, basis_ref):
    columns = theta_ref.shape[0]
    width = gathered_ref.shape[1] // 2
    grams = gathered_ref[:, :width].T
    arrived = gathered_ref[:, width:]
    carried = carried_ref[...]
    wide = 2 * columns
    known = carried[:wide]
    overlap = nn(known, grams[:wide, :columns])
    factor = inverse_factor(grams[wide:, :columns] - tn(overlap, overlap))
    linv = jnp.concatenate(
        [
            jnp.concatenate([known, jnp.zeros((wide, columns), F32)], axis=1),
            jnp.concatenate([-nn(factor, tn(overlap, known)), factor], axis=1),
        ],
        axis=0,
    )
    cross = grams[:wide, columns:]
    own = half_sum(grams[wide:, columns:])
    block_momentum = carried[wide : wide + columns, columns:]
    momentum = half_sum(carried[wide + columns :, columns:])
    upper = jnp.concatenate(
        [
            jnp.concatenate([theta_ref[...], block_momentum], axis=1),
            jnp.concatenate([block_momentum.T, momentum], axis=1),
        ],
        axis=0,
    )
    gram = jnp.concatenate(
        [
            jnp.concatenate([upper, cross], axis=1),
            jnp.concatenate([cross.T, own], axis=1),
        ],
        axis=0,
    )
    coeffs, theta = project(linv, gram, basis_ref)
    theta_out_ref[...] = theta
    embedding_ref[...] = root * mm(coeffs, arrived, (0, 1))


def local(start_block, weight_tiles, tile_scales, neighbour_ids, live_counts, row_order):
    columns = start_block.shape[0]
    rows_dev = start_block.shape[1]
    groups = lax.axis_size("grp")
    nodes = lax.axis_size("node")
    here = lax.axis_index("node")
    ids = neighbour_ids[0]
    slots = ids.shape[0]
    group_index = ids // nodes
    node_index = ids % nodes
    chips = nodes // 2
    chip_offset = (node_index // 2 - here // 2 + 1 + chips) % chips
    index = jnp.clip(chip_offset * 8 + node_index % 2 + 2 * group_index, 0, 23).astype(jnp.int32)
    slot_iota = jnp.arange(slots, dtype=jnp.int32)
    weights = jnp.where(slot_iota < live_counts[0], tile_scales[0], F32(0.0))
    tiles = weight_tiles[0]
    to_next = [(source, (source + 2) % nodes) for source in range(nodes)]
    to_last = [(source, (source - 2) % nodes) for source in range(nodes)]
    root = float(rows_dev * groups * nodes) ** 0.5
    slab = (columns, rows_dev)
    square = (columns, columns)
    packed = (columns // 2, 2 * columns)
    slab_slots = ((slots,) + slab, F32)

    def exchange(parcel):
        received = swap(parcel, CORE_X)
        partial = sum_copies(received, 2 ** len(Y_Z), columns)
        shared = swap(partial, Y_Z)
        later, _ = lax.optimization_barrier((received, partial))
        down = lax.ppermute(later, "node", to_next)
        up = lax.ppermute(later, "node", to_last)
        summed = swap(sum_copies(shared, 2 ** len(CORE_X)), CORE_X)
        return (received, up, down), summed

    def parcel_of(share):
        return ((2 * groups, columns + share, rows_dev), F32)

    small = parcel_of(columns // (4 * groups))
    start_rows, gram = exchange(run(gram_kernel, "start_gram", [small], start_block)[0])
    block, block_slots, applied, parcel = run(
        start_kernel,
        "start_step",
        [(slab, F32), slab_slots, (slab, F32), small],
        weights,
        index,
        *start_rows,
        gram.reshape(packed),
        start_block,
        tiles,
        scalars=2,
    )
    applied_rows, theta_sum = exchange(parcel)
    theta, start_theta, residual, residual_slots, image, parcel, overlap, applied_slots = run(
        lambda *refs: first_kernel(root, *refs),
        "first_residual",
        [
            (square, F32),
            (square, F32),
            (slab, F32),
            slab_slots,
            (slab, F32),
            parcel_of(columns // (2 * groups) + 1),
            (square, F32),
            slab_slots,
        ],
        weights,
        index,
        *applied_rows,
        theta_sum.reshape(packed),
        block,
        applied,
        block_slots,
        tiles,
        scalars=2,
    )
    image_rows, grams = exchange(parcel)
    coeffs, next_theta, trial, last_grams = run(
        second_kernel,
        "second_step",
        [
            ((2 * columns, 2 * columns), F32),
            (square, F32),
            ((3 * columns, rows_dev), F32),
            ((2 * columns, 3 * columns), F32),
        ],
        weights,
        index,
        *image_rows,
        grams,
        overlap,
        theta,
        block,
        residual,
        applied,
        image,
        block_slots,
        residual_slots,
        applied_slots,
        tiles,
        scalars=2,
        scratch=[pltpu.VMEM((2 * columns, columns), F32)],
    )
    carried, pieces = run(
        carry_kernel,
        "carry",
        [((4 * columns, 2 * columns), F32), ((rows_dev, 3 * columns), F32)],
        coeffs,
        grams,
        overlap,
        theta,
        trial,
        row_order,
    )

    def over(values, axis):
        return lax.all_to_all(values, axis, split_axis=0, concat_axis=0, tiled=True)

    row_parts = run(
        row_sum_kernel, "row_sum", [((groups, 3 * columns), F32)], over(last_grams, "node")
    )[0]
    gathered = over(
        run(
            gather_kernel, "gather", [((nodes, 6 * columns), F32)], over(row_parts, "grp"), pieces
        )[0],
        "node",
    )
    ritz, embedding = run(
        lambda *refs: last_step_kernel(root, *refs),
        "last_step",
        [(square, F32), (slab, F32)],
        gathered,
        carried,
        next_theta,
        scratch=[pltpu.VMEM((3 * columns, columns), F32)],
    )
    return (embedding, ritz, start_theta)


def solution(mesh):
    return jax.shard_map(
        local,
        mesh=mesh,
        in_specs=(
            P(None, BOTH),
            P(BOTH, None, None, None),
            P(BOTH, None),
            P(BOTH, None),
            P(BOTH),
            P(BOTH, None),
        ),
        out_specs=(P(None, BOTH), P(), P()),
        check_vma=False,
    )
```

```python
import jax
import jax.numpy as jnp
from jax import lax
from jax.experimental import pallas as pl
from jax.experimental.pallas import tpu as pltpu
from jax.sharding import PartitionSpec as P

REACH = 2
NSUB = 4
BLOCK = 8
RADIUS = 0.18
BOTH = ("grp", "node")
CORE_X = (1, 128, 256)
Y_Z = (2, 4, 8, 16, 32, 64)


def groups_over(bits):
    mask = sum(bits)
    groups = []
    for base in range(512):
        if base & mask:
            continue
        members = [base]
        for bit in bits:
            members = members + [member | bit for member in members]
        groups.append(members)
    return groups


def swap(values, bits):
    return lax.all_to_all(
        values, BOTH, split_axis=0, concat_axis=0, tiled=True, axis_index_groups=groups_over(bits)
    )


def run(kernel, name, results, *operands, scalars=0, scratch=()):
    smem = pl.BlockSpec(memory_space=pltpu.SMEM)
    vmem = pl.BlockSpec(memory_space=pltpu.VMEM)
    return pl.pallas_call(
        kernel,
        out_shape=[jax.ShapeDtypeStruct(shape, dtype) for shape, dtype in results],
        in_specs=[smem] * scalars + [vmem] * (len(operands) - scalars),
        out_specs=[vmem] * len(results),
        scratch_shapes=list(scratch),
        compiler_params=pltpu.CompilerParams(vmem_limit_bytes=32 << 20),
        name=name,
    )(*operands)


F32 = jnp.float32
BF16 = jnp.bfloat16


def tree_sum(parts):
    while len(parts) > 1:
        parts = [parts[i] + parts[i + 1] for i in range(0, len(parts), 2)]
    return parts[0]


def sum_kernel(first, parts_ref, out_ref):
    summed = tree_sum([parts_ref[i, first:] for i in range(parts_ref.shape[0])])
    for i in range(out_ref.shape[0]):
        out_ref[i] = summed


def sum_copies(parts, count, first=0):
    return run(
        lambda *refs: sum_kernel(first, *refs),
        "sum_copies",
        [((count, parts.shape[1] - first, parts.shape[2]), F32)],
        parts,
    )[0]


def row_sum_kernel(parts_ref, out_ref):
    summed = jnp.sum(parts_ref[...], axis=0)
    for i in range(out_ref.shape[0]):
        out_ref[i] = summed


def gather_kernel(parts_ref, pieces_ref, out_ref):
    summed = tree_sum([parts_ref[i] for i in range(parts_ref.shape[0])])
    rows, width = pieces_ref.shape
    out_ref[:, :width] = jnp.broadcast_to(summed, (rows, width))
    out_ref[:, width:] = pieces_ref[...]


def mm(left, right, contract):
    return lax.dot_general(
        left,
        right,
        ((contract[:1], contract[1:]), ((), ())),
        precision=lax.Precision.HIGHEST,
        preferred_element_type=jnp.float32,
    )


def nn(left, right):
    return mm(left, right, (1, 0))


def nt(left, right):
    return mm(left, right, (1, 1))


def tn(left, right):
    return mm(left, right, (0, 0))


def eye(order):
    row = lax.broadcasted_iota(jnp.int32, (order, order), 0)
    column = lax.broadcasted_iota(jnp.int32, (order, order), 1)
    return jnp.where(row == column, jnp.float32(1.0), jnp.float32(0.0))


def inverse_root(value):
    guess = lax.rsqrt(value)
    return guess * (1.5 - 0.5 * value * guess * guess)


def inverse_factor(matrix):
    order = matrix.shape[0]
    lanes = 2 * order
    both = jnp.concatenate([matrix, eye(order)], axis=1)
    bands = [both[8 * i : 8 * i + 8] for i in range(order // 8)]
    sublane = lax.broadcasted_iota(jnp.int32, (8, lanes), 0)
    done = [None] * len(bands)
    for first in range(0, order, BLOCK):
        band = first // 8
        base = first % 8
        last_of_band = base + BLOCK == 8
        live = range(band, len(bands))
        column = [
            [jnp.broadcast_to(bands[i][:, first + k : first + k + 1], (8, lanes)) for i in live]
            for k in range(BLOCK)
        ]
        row = [
            jnp.broadcast_to(bands[band][base + k : base + k + 1], (8, lanes)) for k in range(BLOCK)
        ]
        entry = [
            [
                jnp.broadcast_to(column[l][0][base + k : base + k + 1], (8, lanes))
                for l in range(k + 1)
            ]
            for k in range(BLOCK)
        ]
        inverse = []
        factor = [[None] * BLOCK for _ in range(BLOCK)]
        for l in range(BLOCK):
            inverse.append(1.0 / entry[l][l])
            for k in range(l + 1, BLOCK):
                factor[k][l] = entry[k][l] * inverse[l]
                for m in range(l + 1, k + 1):
                    entry[k][m] = entry[k][m] - factor[k][l] * entry[m][l]
        start = 1 if last_of_band else 0
        for k in range(BLOCK):
            for l in range(k):
                row[k] = row[k] - factor[k][l] * row[l]
                for i in range(start, len(live)):
                    column[k][i] = column[k][i] - factor[k][l] * column[l][i]
        for k in range(BLOCK):
            scaled = row[k] * inverse_root(entry[k][k])
            if done[band] is None:
                done[band] = scaled
            else:
                done[band] = jnp.where(sublane == base + k, scaled, done[band])
            left = row[k] * inverse[k]
            for i in range(start, len(live)):
                bands[band + i] = bands[band + i] - column[k][i] * left
    return jnp.concatenate(done, axis=0)[:, order:]


def half_sum(matrix):
    return 0.5 * (matrix + matrix.T)


def orthonormal(image):
    return nt(image, inverse_factor(tn(image, image)))


def project(linv, gram, basis_ref):
    order = linv.shape[0]
    columns = basis_ref.shape[1]
    projected = half_sum(nt(nn(linv, gram), linv))
    scale = jnp.sqrt(jnp.sum(projected * projected, keepdims=True) + 1e-06)
    unit = projected / scale
    identity = eye(order)
    filtered = unit + 1.25 * identity
    square = nn(filtered, filtered)
    fourth = nn(square, square)
    eighth = nn(fourth, fourth)
    unit2 = square - 2.5 * unit - 1.5625 * identity
    unit4 = nn(unit2, unit2)
    bound = jnp.sum(unit4 * unit4)
    basis_ref[...] = orthonormal(nn(eighth, eighth[:, :columns]))

    @pl.when(jnp.logical_not(bound < RADIUS**8))
    def _():
        basis_ref[...] = identity[:, :columns]

        def sweep(_, carry):
            basis_ref[...] = orthonormal(nn(fourth, basis_ref[...]))
            return carry

        lax.fori_loop(0, NSUB, sweep, 0)

    basis = basis_ref[...]
    coeffs = tn(linv, basis)
    theta = half_sum(tn(basis, nn(projected, basis)))
    return coeffs, theta


def load_packed(ref):
    width = ref.shape[1] // 2
    return jnp.concatenate([ref[:, :width], ref[:, width:]], axis=0)


def store_parcel(ref, value, partial):
    members, rows = ref.shape[0], value.shape[0]
    share = partial.shape[0] // members
    for i in range(members):
        ref[i, :rows] = value
        ref[i, rows:] = partial[share * i : share * (i + 1)]


def pack(matrix):
    half = matrix.shape[0] // 2
    return jnp.concatenate([matrix[:half], matrix[half:]], axis=1)


def gram_kernel(start_ref, parcel_ref):
    start = start_ref[...]
    store_parcel(parcel_ref, start, pack(nt(start, start)))


def neighbour_rows(index_ref, own_ref, up_ref, down_ref, rows):
    count = own_ref.shape[0]

    def at(slot):
        side = lax.div(index_ref[slot], count)
        member = lax.rem(index_ref[slot], count)
        outer = jnp.where(side == 0, down_ref[member, :rows], up_ref[member, :rows])
        return jnp.where(side == 1, own_ref[member, :rows], outer)

    return at


def multiply_tiles(weight_ref, tiles_ref, slot_values):
    acc = None
    for slot in range(tiles_ref.shape[0]):
        product = lax.dot_general(
            slot_values(slot).astype(BF16),
            tiles_ref[slot],
            (((1,), (1,)), ((), ())),
            preferred_element_type=F32,
        )
        product = weight_ref[slot] * product
        acc = product if acc is None else acc + product
    return acc


def start_kernel(weight_ref, index_ref, own_ref, up_ref, down_ref, gram_ref, start_ref, tiles_ref, block_ref, block_slots_ref, applied_ref, parcel_ref):
    inverse = inverse_factor(load_packed(gram_ref))
    block = nn(inverse, start_ref[...])
    block_ref[...] = block

    rows_at = neighbour_rows(index_ref, own_ref, up_ref, down_ref, block.shape[0])

    def values(slot):
        there = nn(inverse, rows_at(slot))
        block_slots_ref[slot] = there
        return there

    applied = multiply_tiles(weight_ref, tiles_ref, values)
    applied_ref[...] = applied
    store_parcel(parcel_ref, applied, pack(nt(block, applied)))


def first_kernel(root, weight_ref, index_ref, own_ref, up_ref, down_ref, sum_ref, block_ref, applied_ref, block_slots_ref, tiles_ref, theta_ref, start_theta_ref, residual_ref, residual_slots_ref, image_ref, parcel_ref, overlap_ref, applied_slots_ref):
    product = load_packed(sum_ref)
    theta = half_sum(product)
    overlap_ref[...] = product - theta
    theta_ref[...] = theta
    start_theta_ref[...] = root * theta
    block = block_ref[...]
    applied = applied_ref[...]
    residual = applied - nn(theta, block)
    residual_ref[...] = residual

    rows_at = neighbour_rows(index_ref, own_ref, up_ref, down_ref, block.shape[0])

    def values(slot):
        applied_there = rows_at(slot)
        applied_slots_ref[slot] = applied_there
        there = applied_there - nn(theta, block_slots_ref[slot])
        residual_slots_ref[slot] = there
        return there

    image = multiply_tiles(weight_ref, tiles_ref, values)
    image_ref[...] = image
    cross = 0.5 * (nt(block, image) + nt(applied, residual))
    own = nt(residual, image)
    order = cross.shape[0]
    row = lax.broadcasted_iota(jnp.int32, (order, order), 0)
    column = lax.broadcasted_iota(jnp.int32, (order, order), 1)
    both = jnp.where(row >= column, nt(residual, residual), half_sum(own))
    diagonal = jnp.sum(jnp.where(row == column, own, F32(0.0)), axis=0, keepdims=True)
    partial = jnp.concatenate([cross, both], axis=1)
    tail = jnp.concatenate([diagonal, jnp.zeros_like(diagonal)], axis=1)
    members = parcel_ref.shape[0]
    share = order // members
    for i in range(members):
        parcel_ref[i, :order] = image
        parcel_ref[i, order : order + share] = partial[share * i : share * (i + 1)]
        parcel_ref[i, order + share :] = tail


def assemble_first(gathered_ref, theta):
    members = gathered_ref.shape[0]
    columns = theta.shape[0]
    share = columns // members
    grams = jnp.concatenate([gathered_ref[i, :share] for i in range(members)], axis=0)
    diagonal = gathered_ref[0, share:, :columns]
    cross = grams[:, :columns]
    both = grams[:, columns:]
    turned = both.T
    row = lax.broadcasted_iota(jnp.int32, (columns, columns), 0)
    column = lax.broadcasted_iota(jnp.int32, (columns, columns), 1)
    basis = jnp.where(row >= column, both, turned)
    own = jnp.where(row < column, both, jnp.where(row > column, turned, diagonal))
    gram = jnp.concatenate(
        [jnp.concatenate([theta, cross], axis=1), jnp.concatenate([cross.T, own], axis=1)], axis=0
    )
    return basis, gram


def second_kernel(weight_ref, index_ref, own_ref, up_ref, down_ref, grams_ref, overlap_ref, theta_ref, block_ref, residual_ref, applied_ref, image_ref, block_slots_ref, residual_slots_ref, applied_slots_ref, tiles_ref, coeffs_ref, theta_out_ref, trial_ref, grams_out_ref, basis_ref):
    columns = theta_ref.shape[0]
    width = block_ref.shape[1]
    overlap = overlap_ref[...]
    own, gram = assemble_first(grams_ref, theta_ref[...])
    factor = inverse_factor(own - tn(overlap, overlap))
    linv = jnp.concatenate(
        [
            jnp.concatenate([eye(columns), jnp.zeros((columns, columns), F32)], axis=1),
            jnp.concatenate([-nt(factor, overlap), factor], axis=1),
        ],
        axis=0,
    )
    coeffs, theta = project(linv, gram, basis_ref)
    theta_out_ref[...] = theta
    lower = jnp.concatenate([jnp.zeros((columns, columns), F32), coeffs[columns:]], axis=0)
    both = jnp.concatenate([coeffs, lower], axis=1)
    coeffs_ref[...] = both
    mix = jnp.concatenate([coeffs, -nn(coeffs, theta)], axis=0).T

    image_at = neighbour_rows(index_ref, own_ref, up_ref, down_ref, columns)

    def values(slot):
        parts = [
            applied_slots_ref[slot],
            image_at(slot),
            block_slots_ref[slot],
            residual_slots_ref[slot],
        ]
        return nn(mix, jnp.concatenate(parts, axis=0))

    image = multiply_tiles(weight_ref, tiles_ref, values)
    block, applied = block_ref[...], applied_ref[...]
    previous, previous_image = residual_ref[...], image_ref[...]
    residual = nn(mix, jnp.concatenate([applied, previous_image, block, previous], axis=0))
    old_trial = jnp.concatenate([block, previous], axis=0)
    old_applied = jnp.concatenate([applied, previous_image], axis=0)
    fresh = tn(both, jnp.concatenate([old_trial, old_applied], axis=1))
    trial = jnp.concatenate([fresh[:, :width], residual], axis=0)
    trial_ref[...] = trial
    applied_trial = jnp.concatenate([fresh[:, width:], image], axis=0)
    cross = 0.5 * (nt(image, trial) + nt(residual, applied_trial))
    grams_out_ref[...] = jnp.concatenate([nt(residual, trial), cross], axis=0)


def carry_kernel(coeffs_ref, grams_ref, overlap_ref, theta_ref, trial_ref, order_ref, carried_ref, pieces_ref):
    columns = theta_ref.shape[0]
    coeffs = coeffs_ref[...]
    overlap = overlap_ref[...]
    own, gram = assemble_first(grams_ref, theta_ref[...])
    basis = jnp.concatenate(
        [
            jnp.concatenate([eye(columns), overlap], axis=1),
            jnp.concatenate([overlap.T, own], axis=1),
        ],
        axis=0,
    )
    products = tn(coeffs, nn(basis, coeffs))
    block_momentum = products[:columns, columns:]
    factor = inverse_factor(products[columns:, columns:] - tn(block_momentum, block_momentum))
    zero = jnp.zeros((columns, columns), F32)
    inverse = jnp.concatenate(
        [
            jnp.concatenate([eye(columns), zero], axis=1),
            jnp.concatenate([-nt(factor, block_momentum), factor], axis=1),
        ],
        axis=0,
    )
    carried_ref[...] = jnp.concatenate([inverse, tn(coeffs, nn(gram, coeffs))], axis=0)
    width = trial_ref.shape[1]
    place = lax.broadcasted_iota(jnp.int32, (width, width), 0)
    pick = jnp.where(place == order_ref[...], F32(1.0), F32(0.0))
    pieces_ref[...] = mm(pick, trial_ref[...], (0, 1))


def last_step_kernel(root, gathered_ref, carried_ref, theta_ref, theta_out_ref, embedding_ref, basis_ref):
    columns = theta_ref.shape[0]
    width = gathered_ref.shape[1] // 2
    grams = gathered_ref[:, :width].T
    arrived = gathered_ref[:, width:]
    carried = carried_ref[...]
    wide = 2 * columns
    known = carried[:wide]
    overlap = nn(known, grams[:wide, :columns])
    factor = inverse_factor(grams[wide:, :columns] - tn(overlap, overlap))
    linv = jnp.concatenate(
        [
            jnp.concatenate([known, jnp.zeros((wide, columns), F32)], axis=1),
            jnp.concatenate([-nn(factor, tn(overlap, known)), factor], axis=1),
        ],
        axis=0,
    )
    cross = grams[:wide, columns:]
    own = half_sum(grams[wide:, columns:])
    block_momentum = carried[wide : wide + columns, columns:]
    momentum = half_sum(carried[wide + columns :, columns:])
    upper = jnp.concatenate(
        [
            jnp.concatenate([theta_ref[...], block_momentum], axis=1),
            jnp.concatenate([block_momentum.T, momentum], axis=1),
        ],
        axis=0,
    )
    gram = jnp.concatenate(
        [
            jnp.concatenate([upper, cross], axis=1),
            jnp.concatenate([cross.T, own], axis=1),
        ],
        axis=0,
    )
    coeffs, theta = project(linv, gram, basis_ref)
    theta_out_ref[...] = theta
    embedding_ref[...] = root * mm(coeffs, arrived, (0, 1))


def local(start_block, weight_tiles, tile_scales, neighbour_ids, live_counts, row_order):
    columns = start_block.shape[0]
    rows_dev = start_block.shape[1]
    groups = lax.axis_size("grp")
    nodes = lax.axis_size("node")
    here = lax.axis_index("node")
    ids = neighbour_ids[0]
    slots = ids.shape[0]
    group_index = ids // nodes
    node_index = ids % nodes
    chips = nodes // 2
    chip_offset = (node_index // 2 - here // 2 + 1 + chips) % chips
    index = jnp.clip(chip_offset * 8 + node_index % 2 + 2 * group_index, 0, 23).astype(jnp.int32)
    slot_iota = jnp.arange(slots, dtype=jnp.int32)
    weights = jnp.where(slot_iota < live_counts[0], tile_scales[0], F32(0.0))
    tiles = weight_tiles[0]
    to_next = [(source, (source + 2) % nodes) for source in range(nodes)]
    to_last = [(source, (source - 2) % nodes) for source in range(nodes)]
    root = float(rows_dev * groups * nodes) ** 0.5
    slab = (columns, rows_dev)
    square = (columns, columns)
    packed = (columns // 2, 2 * columns)
    slab_slots = ((slots,) + slab, F32)

    def exchange(parcel):
        received = swap(parcel, CORE_X)
        partial = sum_copies(received, 2 ** len(Y_Z), columns)
        shared = swap(partial, Y_Z)
        later, _ = lax.optimization_barrier((received, partial))
        down = lax.ppermute(later, "node", to_next)
        up = lax.ppermute(later, "node", to_last)
        summed = swap(sum_copies(shared, 2 ** len(CORE_X)), CORE_X)
        return (received, up, down), summed

    def parcel_of(share):
        return ((2 * groups, columns + share, rows_dev), F32)

    small = parcel_of(columns // (4 * groups))
    start_rows, gram = exchange(run(gram_kernel, "start_gram", [small], start_block)[0])
    block, block_slots, applied, parcel = run(
        start_kernel,
        "start_step",
        [(slab, F32), slab_slots, (slab, F32), small],
        weights,
        index,
        *start_rows,
        gram.reshape(packed),
        start_block,
        tiles,
        scalars=2,
    )
    applied_rows, theta_sum = exchange(parcel)
    theta, start_theta, residual, residual_slots, image, parcel, overlap, applied_slots = run(
        lambda *refs: first_kernel(root, *refs),
        "first_residual",
        [
            (square, F32),
            (square, F32),
            (slab, F32),
            slab_slots,
            (slab, F32),
            parcel_of(columns // (2 * groups) + 1),
            (square, F32),
            slab_slots,
        ],
        weights,
        index,
        *applied_rows,
        theta_sum.reshape(packed),
        block,
        applied,
        block_slots,
        tiles,
        scalars=2,
    )
    image_rows, grams = exchange(parcel)
    coeffs, next_theta, trial, last_grams = run(
        second_kernel,
        "second_step",
        [
            ((2 * columns, 2 * columns), F32),
            (square, F32),
            ((3 * columns, rows_dev), F32),
            ((2 * columns, 3 * columns), F32),
        ],
        weights,
        index,
        *image_rows,
        grams,
        overlap,
        theta,
        block,
        residual,
        applied,
        image,
        block_slots,
        residual_slots,
        applied_slots,
        tiles,
        scalars=2,
        scratch=[pltpu.VMEM((2 * columns, columns), F32)],
    )
    carried, pieces = run(
        carry_kernel,
        "carry",
        [((4 * columns, 2 * columns), F32), ((rows_dev, 3 * columns), F32)],
        coeffs,
        grams,
        overlap,
        theta,
        trial,
        row_order,
    )

    def over(values, axis):
        return lax.all_to_all(values, axis, split_axis=0, concat_axis=0, tiled=True)

    row_parts = run(
        row_sum_kernel, "row_sum", [((groups, 1, 3 * columns), F32)], over(last_grams[:, None], "node")
    )[0]
    gathered = over(
        run(
            gather_kernel, "gather", [((nodes, 6 * columns), F32)], over(row_parts, "grp"), pieces
        )[0],
        "node",
    )
    ritz, embedding = run(
        lambda *refs: last_step_kernel(root, *refs),
        "last_step",
        [(square, F32), (slab, F32)],
        gathered,
        carried,
        next_theta,
        scratch=[pltpu.VMEM((3 * columns, columns), F32)],
    )
    return (embedding, ritz, start_theta)


def solution(mesh):
    return jax.shard_map(
        local,
        mesh=mesh,
        in_specs=(
            P(None, BOTH),
            P(BOTH, None, None, None),
            P(BOTH, None),
            P(BOTH, None),
            P(BOTH),
            P(BOTH, None),
        ),
        out_specs=(P(None, BOTH), P(), P()),
        check_vma=False,
    )
```
